256 devices in a mesh: img: 64 (over z, x, core), ref: 4 (over y).
Axes of the slice: x: 4, y: 4, z: 8, core: 2. Of those that a mesh axis runs over, the one named last changes fastest.
Arguments:
- particles: bfloat16 [16384, 4096], P('img'), may hold values from -40 to 40
- projections: bfloat16 [512, 8, 4096], P(('img', 'ref')), may hold values from -6 to 6
- significance: int32 [64, 512], replicated, may hold values from 0 to 1, as said below
- insertion: int32 [512, 8, 2048], P(('img', 'ref')), may hold values from 0 to 4095
Outputs:
- volume: float32 [2, 1048576], P(None, ('img', 'ref'))
- log_evidence: float32 [16384], P('img')
The draws below stay inside these ranges and needn't reach their ends.
Inputs may be any that keep to these rules, and one draw needn't show every extreme that they name: `significance`: runs are blocks o * 2 to o * 2 + 1, o counted over img and ref with img slowest. For each particle block and each run at most one block is significant; particle block q has one in run q * 4; in every draw some particle block has one in every run.
All inputs are finite; a program needn't handle non-finite values.
Results may differ from the reference program's by a relative error of at most 0.00064.
Values may be sent and summed in bfloat16 or wider, within the bound.
No kernel may reach another device: no remote copies, remote signals or barrier semaphores. Data moves between devices by JAX's collectives and lax.ppermute only.
A program may use at most 128 MiB of HBM per device.

```python
import math
import jax
import jax.numpy as jnp
from jax import lax

SIDE = 64
PIX = 2048
SHIFTS = 5
PART_DEV = 256
BLK = 8
BPD = 2
VOX = 4096
PARTICLES = 16384
NBLK = 512
VOX_ALL = 1048576
N_IMG = 64
N_REF = 4


def projection_values(key):
    return jax.random.truncated_normal(jax.random.fold_in(key, 101), -6.0, 6.0, (NBLK, BLK, 2 * PIX), jnp.float32)


def significance_pattern(key):
    owners = N_IMG * N_REF
    base_key = jax.random.fold_in(key, 202)
    key_level, key_roll, key_which, key_full = jax.random.split(base_key, 4)
    level = jax.random.randint(key_level, (N_IMG, 1), 1, 4)
    rolled = jax.random.randint(key_roll, (N_IMG, owners), 0, 4)
    row_ids = jnp.arange(N_IMG)[:, None]
    column_ids = jnp.arange(owners)[None, :]
    full_row = jax.random.randint(key_full, (), 0, N_IMG)
    live_runs = (rolled < level) | (column_ids == row_ids * N_REF) | (row_ids == full_row)
    which_block = jax.random.randint(key_which, (N_IMG, owners), 0, BPD)
    picked = live_runs[:, :, None] & (which_block[:, :, None] == jnp.arange(BPD)[None, None, :])
    return (picked.astype(jnp.int32).reshape(N_IMG, owners * BPD), which_block)


def draw_projections(key, part):
    return projection_values(key).astype(jnp.bfloat16)


def draw_significance(key, part):
    return significance_pattern(key)[0]


def draw_particles(key, part):
    features = 2 * PIX
    noise_key, pick_key, strength_key = jax.random.split(jax.random.fold_in(key, 303), 3)
    noise = jax.random.truncated_normal(noise_key, -6.0, 6.0, (N_IMG, PART_DEV, features), jnp.float32)
    values = projection_values(key)
    pattern, which_block = significance_pattern(key)
    block_rows = jnp.arange(N_IMG)
    forced = which_block[block_rows, block_rows * N_REF]
    blocks = block_rows * N_REF * BPD + forced
    target = values[blocks, 0] + values[blocks, 1]
    picked = jax.random.randint(pick_key, (N_IMG, PART_DEV, 1), 0, 16) == 0
    strength = jax.random.randint(strength_key, (N_IMG, PART_DEV, 1), 2, 6).astype(jnp.float32)
    amplitude = 25.0 * strength / math.sqrt(features)
    aligned = jnp.clip(amplitude * target[:, None, :] + 0.1 * noise, -40.0, 40.0)
    images = jnp.where(picked, aligned, noise)
    return images.reshape(PARTICLES, features).astype(jnp.bfloat16)


def set_ends(entries, key, smallest, largest):
    extent = entries.shape
    place = [jax.random.randint(jax.random.fold_in(key, axis), (), 0, extent[axis]) for axis in range(len(extent))]
    entries = entries.at[tuple(place)].set(smallest)
    longest = extent.index(max(extent))
    place[longest] = (place[longest] + 1) % extent[longest]
    return entries.at[tuple(place)].set(largest)


def setup_inputs(seed: int = 0) -> dict:
    splits = jax.random.split(jax.random.key(seed), 5)
    return {
        "particles": draw_particles(jax.random.fold_in(splits[4], 71), 0),
        "projections": draw_projections(jax.random.fold_in(splits[4], 71), 0),
        "significance": draw_significance(jax.random.fold_in(splits[4], 71), 0),
        "insertion": set_ends(jax.random.randint(splits[3], (NBLK, BLK, PIX), 0, VOX), jax.random.fold_in(splits[3], 1), 0, VOX - 1).astype(jnp.int32),
    }


SHIFT_X = (0.0, 1.0, -1.0, 0.0, 0.0)
SHIFT_Y = (0.0, 0.0, 0.0, 1.0, -1.0)
NEGATIVE = -1e+30

def shifted_images(images, side_cells):
    pixels = images.shape[1] // 2
    positions = jnp.arange(pixels, dtype=jnp.int32)
    freq_x = (positions % side_cells - side_cells // 2).astype(jnp.float32)
    freq_y = (positions // side_cells).astype(jnp.float32)
    shift_x = jnp.array(SHIFT_X, jnp.float32)[:, None]
    shift_y = jnp.array(SHIFT_Y, jnp.float32)[:, None]
    angles = 2.0 * math.pi / side_cells * (shift_x * freq_x[None, :] + shift_y * freq_y[None, :])
    cosine = jnp.cos(angles)
    sine_table = jnp.sin(angles)
    real_part = images[:, None, :pixels].astype(jnp.float32)
    imag_part = images[:, None, pixels:].astype(jnp.float32)
    new_real = real_part * cosine - imag_part * sine_table
    new_imag = real_part * sine_table + imag_part * cosine
    stacked = jnp.concatenate([new_real, new_imag], axis=2).astype(jnp.bfloat16)
    return stacked.reshape(images.shape[0] * len(SHIFT_X), 2 * pixels)

def reference(particles, projections, significance, insertion):
    owners = N_IMG * N_REF
    features = 2 * PIX
    pattern = significance.reshape(N_IMG, owners, BPD)
    live_blocks = lax.optimization_barrier(jnp.sum(pattern, axis=2))
    chosen = lax.optimization_barrier(jnp.sum(pattern * jnp.arange(BPD, dtype=jnp.int32)[None, None, :], axis=2)).astype(jnp.int32)
    scale_factor = 2.0 / math.sqrt(features)
    images = particles.reshape(N_IMG, PART_DEV, features)

    def one_block(totals, inputs):
        block_images, block_live, block_chosen = inputs
        shifted = shifted_images(block_images, SIDE)
        rows_used = (jnp.arange(owners, dtype=jnp.int32) * BPD + block_chosen).astype(jnp.int32)
        selected = projections[rows_used].reshape(owners * BLK, features)
        scores = jnp.dot(shifted, selected.T, preferred_element_type=jnp.float32) * scale_factor
        scores = scores.reshape(PART_DEV, SHIFTS, owners, BLK)
        valid_mask = jnp.broadcast_to((block_live > 0)[None, None, :, None], scores.shape)
        row_top = lax.optimization_barrier(jnp.max(jnp.where(valid_mask, scores, NEGATIVE), axis=(1, 2, 3)))
        row_total = lax.optimization_barrier(jnp.sum(jnp.where(valid_mask, jnp.exp(scores - row_top[:, None, None, None]), 0.0), axis=(1, 2, 3)))
        evidence = row_top + jnp.log(row_total)
        weights = jnp.where(valid_mask, jnp.exp(scores - evidence[:, None, None, None]), 0.0).astype(jnp.bfloat16)
        weights = weights.reshape(PART_DEV * SHIFTS, owners * BLK)
        partial_value = jnp.dot(weights.T, shifted, preferred_element_type=jnp.float32)
        totals = totals.at[rows_used].add(partial_value.reshape(owners, BLK, features))
        return (totals, evidence)
    initial = jnp.zeros((NBLK, BLK, features), jnp.float32)
    weighted, evidence = lax.scan(one_block, initial, (images, live_blocks, chosen))
    owner_of = (jnp.arange(NBLK, dtype=jnp.int32) // BPD).astype(jnp.int32)
    voxel_ids = (insertion + owner_of[:, None, None] * VOX).reshape(-1)
    real_sum = jax.ops.segment_sum(weighted[:, :, :PIX].reshape(-1), voxel_ids, num_segments=VOX_ALL)
    imag_sum = jax.ops.segment_sum(weighted[:, :, PIX:].reshape(-1), voxel_ids, num_segments=VOX_ALL)
    volume = jnp.stack([real_sum, imag_sum])
    return (volume, evidence.reshape(PARTICLES))
```

```python
import math

import jax
import jax.numpy as jnp
import numpy as np
from jax import lax
from jax.experimental import pallas as pl
from jax.experimental.pallas import tpu as pltpu
from jax.sharding import PartitionSpec as P

SIDE = 64
PIX = 2048
FEATURES = 2 * PIX
VOX = 4096
Z, X, CORES, REFS = 8, 4, 2, 4
RUNS = Z * X
COLS = RUNS * 8
N = 256
SHIFTS = 5
ROWS = SHIFTS * N
NEGATIVE = -1e30
SCALE = 2.0 / math.sqrt(FEATURES)
HEADROOM = 2.5
TILE = 512
EXTRA = 128


def shift_tables():
    p = np.arange(PIX)
    unit = np.float32(2.0 * math.pi / SIDE)
    ax = (unit * (p % SIDE - SIDE // 2).astype(np.float32)).astype(np.float64)
    ay = (unit * (p // SIDE).astype(np.float32)).astype(np.float64)
    rows = [np.cos(ax), np.sin(ax), np.cos(ay), np.sin(ay)]
    return np.stack(rows + rows).astype(np.float32)


def shift_kernel(table_ref, re_ref, im_ref, out_re, out_im):
    re = re_ref[...].astype(jnp.float32)
    im = im_ref[...].astype(jnp.float32)
    out_re[0] = re_ref[...]
    out_im[0] = im_ref[...]
    for k in range(2):
        c = table_ref[2 * k : 2 * k + 1, :]
        s = table_ref[2 * k + 1 : 2 * k + 2, :]
        rc, rs, ic, is_ = re * c, re * s, im * c, im * s
        out_re[1 + 2 * k] = (rc - is_).astype(jnp.bfloat16)
        out_im[1 + 2 * k] = (rs + ic).astype(jnp.bfloat16)
        out_re[2 + 2 * k] = (rc + is_).astype(jnp.bfloat16)
        out_im[2 + 2 * k] = (ic - rs).astype(jnp.bfloat16)


def shifted_images(table, images):
    tiles = PIX // TILE
    shape = jax.ShapeDtypeStruct((SHIFTS, N, PIX), jnp.bfloat16)
    out_spec = pl.BlockSpec((SHIFTS, N, TILE), lambda i: (0, 0, i))
    return pl.pallas_call(
        shift_kernel,
        grid=(tiles,),
        in_specs=[
            pl.BlockSpec((8, TILE), lambda i: (0, i)),
            pl.BlockSpec((N, TILE), lambda i: (0, i)),
            pl.BlockSpec((N, TILE), lambda i: (0, i + tiles)),
        ],
        out_specs=[out_spec, out_spec],
        out_shape=[shape, shape],
        cost_estimate=pl.CostEstimate(
            flops=24 * N * PIX, bytes_accessed=12 * 1024 * 1024, transcendentals=0
        ),
        name="shift",
    )(table, images, images)


def run_entry(sig_ref, pos_ref, q, dz, dx):
    zz = lax.rem(pos_ref[0] + dz, Z)
    xx = lax.rem(pos_ref[1] + dx, X)
    at = (((zz * X + xx) * CORES + pos_ref[2]) * REFS + pos_ref[3]) * 2
    row = pos_ref[2] if q == 0 else 1 - pos_ref[2]
    return sig_ref[row, at], sig_ref[row, at + 1], zz


def score_kernel(sig_ref, pos_ref, *refs):
    by_z = refs[:Z]
    by_x = refs[Z : Z + X]
    sh = refs[Z + X : Z + X + 4]
    st_ref, stat_ref = refs[Z + X + 4 : Z + X + 6]
    sel, acc, mask, tops, sem, sem_top = refs[Z + X + 6 :]
    step = pl.program_id(0)

    @pl.when(step == 0)
    def _():
        for q in range(2):
            for dz in range(Z):
                for dx in range(X):
                    o = dz * X + dx
                    first, second, zz = run_entry(sig_ref, pos_ref, q, dz, dx)
                    pltpu.make_async_copy(
                        by_z[dz].at[dx, second], sel.at[q, o, :, pl.ds(0, PIX)], sem
                    ).start()
                    pltpu.make_async_copy(
                        by_x[dx].at[zz, second, :, pl.ds(0, PIX)],
                        sel.at[q, o, :, pl.ds(PIX, PIX)],
                        sem,
                    ).start()
                    live = (first + second).astype(jnp.float32)
                    mask[q, o * 8 : o * 8 + 8, :] = jnp.full((8, 128), live, jnp.float32)
        for dx in range(X):
            pltpu.make_async_copy(
                by_x[dx].at[:, 0, :, pl.ds(PIX, EXTRA)], tops.at[dx], sem_top
            ).start()
        pltpu.make_async_copy(sel, sel, sem).wait()
        pltpu.make_async_copy(tops, tops, sem_top).wait()

    for q in range(2):
        lhs_re = sh[2 * q][...].reshape(ROWS, TILE)
        lhs_im = sh[2 * q + 1][...].reshape(ROWS, TILE)
        at = pl.multiple_of(step * TILE, TILE)
        rhs_re = sel[q, :, :, pl.ds(at, TILE)].reshape(COLS, TILE)
        rhs_im = sel[q, :, :, pl.ds(PIX + at, TILE)].reshape(COLS, TILE)
        dims = (((1,), (1,)), ((), ()))
        part = lax.dot_general(
            lhs_re, rhs_re, dims, preferred_element_type=jnp.float32
        ) + lax.dot_general(lhs_im, rhs_im, dims, preferred_element_type=jnp.float32)

        @pl.when(step == 0)
        def _():
            acc[q] = part

        @pl.when(step > 0)
        def _():
            acc[q] += part

    @pl.when(step == pl.num_programs(0) - 1)
    def _():
        stat_ref[...] = jnp.zeros_like(stat_ref)
        for q in range(2):
            live = mask[q, :, 0:1] > 0.5
            top = jnp.full((1, N), NEGATIVE, jnp.float32)
            for t in range(SHIFTS):
                s = acc[q, t * N : (t + 1) * N, :].T * SCALE
                s = jnp.where(live, s, NEGATIVE)
                st_ref[q, :, t * N : (t + 1) * N] = s
                top = jnp.maximum(top, jnp.max(s, axis=0, keepdims=True))
            total = jnp.zeros((1, N), jnp.float32)
            for t in range(SHIFTS):
                s = st_ref[q, :, t * N : (t + 1) * N]
                e = jnp.where(live, jnp.exp(s - top), 0.0)
                total = total + jnp.sum(e, axis=0, keepdims=True)
            stat_ref[q : q + 1, :] = top
            stat_ref[2 + q : 3 + q, :] = total
        largest = jnp.max(tops[...].astype(jnp.float32).reshape(X * Z * 8, EXTRA), axis=0, keepdims=True)
        stat_ref[4:5, 0:EXTRA] = largest


def score_all(sig, pos, by_z, by_x, shifted):
    tiles = PIX // TILE
    sh_spec = pl.BlockSpec((SHIFTS, N, TILE), lambda i: (0, 0, i))
    smem = pl.BlockSpec(memory_space=pltpu.SMEM)
    anywhere = pl.BlockSpec(memory_space=pl.ANY)
    return pl.pallas_call(
        score_kernel,
        grid=(tiles,),
        in_specs=[smem, smem] + [anywhere] * (Z + X) + [sh_spec] * 4,
        out_specs=[
            pl.BlockSpec((2, COLS, ROWS), lambda i: (0, 0, 0)),
            pl.BlockSpec((8, N), lambda i: (0, 0)),
        ],
        out_shape=[
            jax.ShapeDtypeStruct((2, COLS, ROWS), jnp.float32),
            jax.ShapeDtypeStruct((8, N), jnp.float32),
        ],
        scratch_shapes=[
            pltpu.VMEM((2, RUNS, 8, FEATURES), jnp.bfloat16),
            pltpu.VMEM((2, ROWS, COLS), jnp.float32),
            pltpu.VMEM((2, COLS, 128), jnp.float32),
            pltpu.VMEM((X, Z, 8, EXTRA), jnp.bfloat16),
            pltpu.SemaphoreType.DMA,
            pltpu.SemaphoreType.DMA,
        ],
        compiler_params=pltpu.CompilerParams(vmem_limit_bytes=48 * 1024 * 1024),
        cost_estimate=pl.CostEstimate(
            flops=4 * ROWS * COLS * FEATURES, bytes_accessed=28 * 1024 * 1024, transcendentals=2 * ROWS * COLS
        ),
        name="scores",
    )(sig, pos, *by_z, *by_x, *shifted)


def partial_kernel(z_first, first_call, sig_ref, pos_ref, scale_ref, *refs):
    if first_call:
        st_ref, ev_ref, own_ref, mate_ref, out_ref, w_ref = refs

        @pl.when(pl.program_id(0) == 0)
        def _():
            for q in range(2):
                for t in range(SHIFTS):
                    s = st_ref[q, :, t * N : (t + 1) * N]
                    e = jnp.exp(s - ev_ref[q : q + 1, :])
                    w_ref[q, :, t * N : (t + 1) * N] = e.astype(jnp.bfloat16)
    else:
        w_ref, own_ref, mate_ref, out_ref = refs
    scale = scale_ref[0]
    for q, images in ((0, own_ref), (1, mate_ref)):
        value = (
            jnp.dot(w_ref[q], images[...].reshape(ROWS, TILE), preferred_element_type=jnp.float32)
            * scale
        )
        for dz in range(Z):
            for dx in range(X):
                o = dz * X + dx
                _, second, zz = run_entry(sig_ref, pos_ref, q, dz, dx)
                base = (o if z_first else dx * Z + zz) * 16
                rows = pl.ds(pl.multiple_of(base + second * 8, 8), 8)
                block = value[o * 8 : o * 8 + 8, :]
                if q == 0:
                    other = pl.ds(pl.multiple_of(base + (1 - second) * 8, 8), 8)
                    out_ref[rows, :] = block
                    out_ref[other, :] = jnp.zeros_like(block)
                else:
                    out_ref[rows, :] += block


def partial_sums(z_first, sig, pos, scale, weights, own, mate):
    first_call = len(weights) == 2
    tiles = PIX // TILE
    smem = pl.BlockSpec(memory_space=pltpu.SMEM)
    sh_spec = pl.BlockSpec((SHIFTS, N, TILE), lambda i: (0, 0, i))
    w_spec = pl.BlockSpec((2, COLS, ROWS), lambda i: (0, 0, 0))
    out_specs = [pl.BlockSpec((2 * COLS, TILE), lambda i: (0, i))]
    out_shape = [jax.ShapeDtypeStruct((2 * COLS, PIX), jnp.float32)]
    in_w = [w_spec]
    if first_call:
        in_w.append(pl.BlockSpec((8, N), lambda i: (0, 0)))
        out_specs.append(w_spec)
        out_shape.append(jax.ShapeDtypeStruct((2, COLS, ROWS), jnp.bfloat16))
    return pl.pallas_call(
        lambda *refs: partial_kernel(z_first, first_call, *refs),
        grid=(tiles,),
        in_specs=[smem, smem, smem] + in_w + [sh_spec, sh_spec],
        out_specs=out_specs,
        out_shape=out_shape,
        compiler_params=pltpu.CompilerParams(vmem_limit_bytes=48 * 1024 * 1024),
        cost_estimate=pl.CostEstimate(
            flops=2 * ROWS * COLS * FEATURES, bytes_accessed=16 * 1024 * 1024, transcendentals=0
        ),
        name="partial_re" if first_call else "partial_im",
    )(sig, pos, scale, *weights, own, mate)


HIGH, LOW = 32, 128


def insert_kernel(scale_ref, w_ref, ins_ref, out_ref):
    scale = scale_ref[0]
    acc = jnp.zeros((2 * HIGH, LOW), jnp.float32)
    high_ids = lax.broadcasted_iota(jnp.int32, (HIGH, PIX), 0)
    low_ids = lax.broadcasted_iota(jnp.int32, (LOW, PIX), 0)
    for r in range(16):
        ids = ins_ref[r : r + 1, :]
        high = ids // LOW
        low = ids % LOW
        value = w_ref[r : r + 1, :] * scale
        head = value.astype(jnp.bfloat16).astype(jnp.float32)
        tail = value - head
        here = high == high_ids
        rows = jnp.concatenate(
            [jnp.where(here, head, 0.0), jnp.where(here, tail, 0.0)], axis=0
        ).astype(jnp.bfloat16)
        table = jnp.where(low == low_ids, 1.0, 0.0).astype(jnp.bfloat16)
        acc += lax.dot_general(
            rows, table, (((1,), (1,)), ((), ())), preferred_element_type=jnp.float32
        )
    out_ref[...] = acc[:HIGH] + acc[HIGH:]


def insert(scale, weighted, insertion):
    vmem = pl.BlockSpec(memory_space=pltpu.VMEM)
    return pl.pallas_call(
        insert_kernel,
        in_specs=[pl.BlockSpec(memory_space=pltpu.SMEM), vmem, vmem],
        out_specs=vmem,
        out_shape=jax.ShapeDtypeStruct((HIGH, LOW), jnp.float32),
        cost_estimate=pl.CostEstimate(
            flops=4 * HIGH * LOW * 16 * PIX, bytes_accessed=512 * 1024, transcendentals=0
        ),
        name="insert",
    )(scale, weighted.reshape(16, PIX), insertion)


def img_index(z, x, c):
    return (z * X + x) * CORES + c


def pairs(dz, dx, dc=0):
    return [
        (img_index(z, x, c), img_index((z + dz) % Z, (x + dx) % X, (c + dc) % CORES))
        for z in range(Z)
        for x in range(X)
        for c in range(CORES)
    ]


Z_GROUPS = [[img_index(z, x, c) for z in range(Z)] for x in range(X) for c in range(CORES)]


def send(value, dz=0, dx=0, dc=0):
    return lax.ppermute(value, "img", pairs(dz, dx, dc))


def all_to_all_z(value):
    return lax.all_to_all(
        value, "img", split_axis=0, concat_axis=0, tiled=True, axis_index_groups=Z_GROUPS
    )


def gather_x_first(unit):
    row = jnp.stack([unit, send(unit, dx=-1), send(unit, dx=-2), send(unit, dx=1)])
    out = {0: row}
    ahead = behind = row
    for k in range(1, Z // 2 + 1):
        behind = send(behind, dz=1)
        out[Z - k] = behind
        if k < Z // 2:
            ahead = send(ahead, dz=-1)
            out[k] = ahead
    return [out[k] for k in range(Z)]


def gather_z_first(unit):
    column = all_to_all_z(jnp.broadcast_to(unit[None], (Z,) + unit.shape))
    return [column, send(column, dx=-1), send(column, dx=-2), send(column, dx=1)]


def wide(value):
    return value.astype(jnp.float32)


def narrow(value):
    return value.astype(jnp.float16)


def scatter_z_first(parts):
    half = Z // 2
    behind = narrow(parts[half])
    for k in range(half, 0, -1):
        if k < half:
            behind = narrow(parts[k] + wide(behind))
        behind = send(behind, dz=1)
    ahead = narrow(parts[half + 1])
    for k in range(half - 1, 0, -1):
        if k < half - 1:
            ahead = narrow(parts[Z - k] + wide(ahead))
        ahead = send(ahead, dz=-1)
    row = parts[0] + wide(behind) + wide(ahead)
    arrived = [send(narrow(row[k]), dx=k) for k in range(1, X)]
    return row[0] + wide(arrived[0]) + wide(arrived[1]) + wide(arrived[2])


def scatter_x_first(parts):
    arrived = [send(narrow(parts[k]), dx=k) for k in range(1, X)]
    column = parts[0] + wide(arrived[0]) + wide(arrived[1]) + wide(arrived[2])
    return jnp.sum(wide(all_to_all_z(narrow(column))), axis=0)


def per_device(particles, projections, significance, insertion):
    img = lax.axis_index("img")
    ref = lax.axis_index("ref")
    z, x, core = img // (X * CORES), (img // CORES) % X, img % CORES
    pos = jnp.stack([z, x, core, ref]).astype(jnp.int32)
    sig = lax.dynamic_slice_in_dim(significance, img - core, 2, axis=0)
    table = jnp.asarray(shift_tables())

    mate = send(particles, dc=1)
    by_z = gather_x_first(projections[:, :, :PIX])
    largest = jnp.max(jnp.abs(particles))
    unit = jnp.concatenate(
        [projections[:, :, PIX:], jnp.broadcast_to(largest, (2, 8, EXTRA))], axis=2
    )
    by_x = gather_z_first(unit)
    own_re, own_im = shifted_images(table, particles)
    mate_re, mate_im = shifted_images(table, mate)

    scores, stats = score_all(sig, pos, by_z, by_x, (own_re, own_im, mate_re, mate_im))
    other = send(stats, dc=1)
    top_a, top_b = stats[0:2], other[1::-1]
    sum_a, sum_b = stats[2:4], other[3:1:-1]
    top = jnp.maximum(top_a, top_b)
    total = sum_a * jnp.exp(top_a - top) + sum_b * jnp.exp(top_b - top)
    both = jnp.concatenate([top, total])
    every = lax.all_to_all(
        jnp.broadcast_to(both[None], (REFS,) + both.shape), "ref", split_axis=0, concat_axis=0, tiled=True
    )
    tops, totals = every[:, 0:2], every[:, 2:4]
    top = jnp.max(tops, axis=0)
    evidence = top + jnp.log(jnp.sum(totals * jnp.exp(tops - top), axis=0))
    evidence8 = jnp.concatenate([evidence] * 4)
    bound = jnp.maximum(jnp.maximum(jnp.max(stats[4]), jnp.max(other[4])), 1e-30)
    scale = (HEADROOM / bound).reshape(1)
    unscale = (bound / HEADROOM).reshape(1)

    sums_re, weights = partial_sums(True, sig, pos, scale, (scores, evidence8), own_re, mate_re)
    (sums_im,) = partial_sums(False, sig, pos, scale, (weights,), own_im, mate_im)
    total_re = scatter_z_first(sums_re.reshape(Z, X, 2, 8, PIX))
    total_im = scatter_x_first(sums_im.reshape(X, Z, 2, 8, PIX))
    ids = insertion.reshape(16, PIX)
    volume_re = insert(unscale, total_re, ids)
    volume_im = insert(unscale, total_im, ids)
    volume = jnp.stack([volume_re, volume_im]).reshape(2, VOX)
    return volume, evidence[0]


def solution(mesh):
    in_specs = (P("img", None), P(("img", "ref"), None, None), P(), P(("img", "ref"), None, None))
    out_specs = (P(None, ("img", "ref")), P("img"))
    return jax.shard_map(
        per_device, mesh=mesh, in_specs=in_specs, out_specs=out_specs, check_vma=False
    )
```

```python
import math

import jax
import jax.numpy as jnp
import numpy as np
from jax import lax
from jax.experimental import pallas as pl
from jax.experimental.pallas import tpu as pltpu
from jax.sharding import PartitionSpec as P

SIDE = 64
PIX = 2048
FEATURES = 2 * PIX
VOX = 4096
Z, X, CORES, REFS = 8, 4, 2, 4
RUNS = Z * X
COLS = RUNS * 8
N = 256
SHIFTS = 5
ROWS = SHIFTS * N
NEGATIVE = -1e30
SCALE = 2.0 / math.sqrt(FEATURES)
HEADROOM = 2.5
EXTRA = 128


def shift_tables():
    p = np.arange(PIX)
    unit = np.float32(2.0 * math.pi / SIDE)
    ax = (unit * (p % SIDE - SIDE // 2).astype(np.float32)).astype(np.float64)
    ay = (unit * (p // SIDE).astype(np.float32)).astype(np.float64)
    rows = [np.cos(ax), np.sin(ax), np.cos(ay), np.sin(ay)]
    return np.stack(rows + rows).astype(np.float32)


VMEM = pl.BlockSpec(memory_space=pltpu.VMEM)
SMEM = pl.BlockSpec(memory_space=pltpu.SMEM)
LANES = 512
PTILE = 512


def in_vmem(value):
    return pltpu.with_memory_space_constraint(value, pltpu.VMEM)


def limit(mib):
    return pltpu.CompilerParams(vmem_limit_bytes=mib * 1024 * 1024)


def shift_kernel(table_ref, image_ref, out_re, out_im):
    for j in range(PIX // LANES):
        at = slice(j * LANES, (j + 1) * LANES)
        at_im = slice(PIX + j * LANES, PIX + (j + 1) * LANES)
        tables = [table_ref[k : k + 1, at] for k in range(4)]

        @pl.loop(0, N // 16)
        def _(i):
            rows = pl.ds(pl.multiple_of(i * 16, 16), 16)
            re_in, im_in = image_ref[rows, at], image_ref[rows, at_im]
            out_re[0, rows, at] = re_in
            out_im[0, rows, at] = im_in
            re, im = re_in.astype(jnp.float32), im_in.astype(jnp.float32)
            for k in range(2):
                c, s = tables[2 * k], tables[2 * k + 1]
                rc, rs, ic, is_ = re * c, re * s, im * c, im * s
                out_re[1 + 2 * k, rows, at] = (rc - is_).astype(jnp.bfloat16)
                out_im[1 + 2 * k, rows, at] = (rs + ic).astype(jnp.bfloat16)
                out_re[2 + 2 * k, rows, at] = (rc + is_).astype(jnp.bfloat16)
                out_im[2 + 2 * k, rows, at] = (ic - rs).astype(jnp.bfloat16)


def shifted_images(table, images):
    shape = pltpu.VMEM((SHIFTS, N, PIX), jnp.bfloat16)
    return pl.pallas_call(
        shift_kernel,
        in_specs=[VMEM, VMEM],
        out_specs=[VMEM, VMEM],
        out_shape=[shape, shape],
        compiler_params=limit(4),
        cost_estimate=pl.CostEstimate(
            flops=24 * N * PIX, bytes_accessed=12 * 1024 * 1024, transcendentals=0
        ),
        name="shift",
    )(in_vmem(table), in_vmem(images))


def run_entry(sig_ref, pos_ref, q, dz, dx):
    zz = lax.rem(pos_ref[0] + dz, Z)
    xx = lax.rem(pos_ref[1] + dx, X)
    at = (((zz * X + xx) * CORES + pos_ref[2]) * REFS + pos_ref[3]) * 2
    row = pos_ref[2] if q == 0 else 1 - pos_ref[2]
    return sig_ref[row, at], sig_ref[row, at + 1], zz


def score_kernel(sig_ref, pos_ref, *refs):
    by_z = refs[:Z]
    by_x = refs[Z : Z + X]
    sh = refs[Z + X : Z + X + 4]
    st_ref, stat_ref = refs[Z + X + 4 : Z + X + 6]
    sel, acc, mask = refs[Z + X + 6 :]
    stat_ref[...] = jnp.zeros_like(stat_ref)
    for q in range(2):
        for dz in range(Z):
            for dx in range(X):
                o = dz * X + dx
                first, second, zz = run_entry(sig_ref, pos_ref, q, dz, dx)
                sel[q, o, :, 0:PIX] = by_z[dz][dx, second]
                sel[q, o, :, PIX:] = by_x[dx][zz, second, :, 0:PIX]
                live = (first + second).astype(jnp.float32)
                mask[q, o * 8 : o * 8 + 8, :] = jnp.full((8, 128), live, jnp.float32)
    dims = (((1,), (1,)), ((), ()))
    for q in range(2):
        for half in range(2):
            part = lax.dot_general(
                sh[2 * q + half][...].reshape(ROWS, PIX),
                sel[q, :, :, half * PIX : (half + 1) * PIX].reshape(COLS, PIX),
                dims,
                preferred_element_type=jnp.float32,
            )
            if half == 0:
                acc[...] = part
            else:
                acc[...] += part
        live = mask[q, :, 0:1] > 0.5
        top = jnp.full((1, N), NEGATIVE, jnp.float32)
        for t in range(SHIFTS):
            s = acc[t * N : (t + 1) * N, :].T * SCALE
            s = jnp.where(live, s, NEGATIVE)
            st_ref[q, :, t * N : (t + 1) * N] = s
            top = jnp.maximum(top, jnp.max(s, axis=0, keepdims=True))
        total = jnp.zeros((1, N), jnp.float32)
        for t in range(SHIFTS):
            s = st_ref[q, :, t * N : (t + 1) * N]
            e = jnp.where(live, jnp.exp(s - top), 0.0)
            total = total + jnp.sum(e, axis=0, keepdims=True)
        stat_ref[q : q + 1, :] = top
        stat_ref[2 + q : 3 + q, :] = total
    largest = jnp.zeros((8, EXTRA), jnp.float32)
    for dx in range(X):
        for zz in range(Z):
            largest = jnp.maximum(largest, by_x[dx][zz, 0, :, PIX:].astype(jnp.float32))
    stat_ref[4:5, 0:EXTRA] = jnp.max(largest, axis=0, keepdims=True)


def score_all(sig, pos, by_z, by_x, shifted):
    return pl.pallas_call(
        score_kernel,
        in_specs=[SMEM, SMEM] + [VMEM] * (Z + X + 4),
        out_specs=[VMEM, VMEM],
        out_shape=[
            pltpu.VMEM((2, COLS, ROWS), jnp.float32),
            pltpu.VMEM((8, N), jnp.float32),
        ],
        scratch_shapes=[
            pltpu.VMEM((2, RUNS, 8, FEATURES), jnp.bfloat16),
            pltpu.VMEM((ROWS, COLS), jnp.float32),
            pltpu.VMEM((2, COLS, 128), jnp.float32),
        ],
        compiler_params=limit(24),
        cost_estimate=pl.CostEstimate(
            flops=4 * ROWS * COLS * FEATURES, bytes_accessed=28 * 1024 * 1024, transcendentals=2 * ROWS * COLS
        ),
        name="scores",
    )(sig, pos, *[in_vmem(v) for v in by_z], *[in_vmem(v) for v in by_x], *[in_vmem(v) for v in shifted])


def merge_kernel(stat_ref, other_ref, out_ref):
    out_ref[...] = jnp.zeros_like(out_ref)
    for q in range(2):
        a, b = stat_ref[q : q + 1, :], other_ref[1 - q : 2 - q, :]
        top = jnp.maximum(a, b)
        out_ref[q : q + 1, :] = top
        out_ref[2 + q : 3 + q, :] = stat_ref[2 + q : 3 + q, :] * jnp.exp(a - top) + other_ref[
            3 - q : 4 - q, :
        ] * jnp.exp(b - top)
    bound = jnp.max(jnp.maximum(stat_ref[4:5, :], other_ref[4:5, :]), axis=1, keepdims=True)
    out_ref[4:5, :] = jnp.broadcast_to(jnp.maximum(bound, 1e-30), (1, N))


def merge(stats, other):
    return pl.pallas_call(
        merge_kernel,
        in_specs=[VMEM, VMEM],
        out_specs=VMEM,
        out_shape=pltpu.VMEM((8, N), jnp.float32),
        compiler_params=limit(2),
        name="merge",
    )(in_vmem(stats), in_vmem(other))


def partial_kernel(z_first, first_call, sig_ref, pos_ref, *refs):
    if first_call:
        st_ref, *every, own_ref, mate_ref, out_ref, w_ref, ev_ref = refs
        for q in range(2):
            tops = [r[q : q + 1, :] for r in every]
            top = jnp.maximum(jnp.maximum(tops[0], tops[1]), jnp.maximum(tops[2], tops[3]))
            total = sum(r[2 + q : 3 + q, :] * jnp.exp(t - top) for r, t in zip(every, tops))
            evidence = top + jnp.log(total)
            if q == 0:
                ev_ref[...] = evidence

            @pl.loop(0, SHIFTS)
            def _(t):
                at = pl.ds(pl.multiple_of(t * N, N), N)
                w_ref[q, :, at] = jnp.exp(st_ref[q, :, at] - evidence).astype(jnp.bfloat16)

        bound_ref = every[0]
    else:
        w_ref, bound_ref, own_ref, mate_ref, out_ref = refs
    scale = HEADROOM / bound_ref[4:5, 0:1]
    entries = [
        [run_entry(sig_ref, pos_ref, q, dz, dx) for dz in range(Z) for dx in range(X)]
        for q in range(2)
    ]

    @pl.loop(0, PIX // PTILE)
    def _(i):
        at = pl.ds(pl.multiple_of(i * PTILE, PTILE), PTILE)
        for q, images in ((0, own_ref), (1, mate_ref)):
            value = (
                jnp.dot(
                    w_ref[q],
                    images[:, :, at].reshape(ROWS, PTILE),
                    preferred_element_type=jnp.float32,
                )
                * scale
            )
            for o in range(RUNS):
                _, second, zz = entries[q][o]
                base = (o if z_first else (o % X) * Z + zz) * 16
                rows = pl.ds(pl.multiple_of(base + second * 8, 8), 8)
                block = value[o * 8 : o * 8 + 8, :]
                if q == 0:
                    other = pl.ds(pl.multiple_of(base + (1 - second) * 8, 8), 8)
                    out_ref[rows, at] = block
                    out_ref[other, at] = jnp.zeros_like(block)
                else:
                    out_ref[rows, at] += block


def partial_sums(z_first, sig, pos, weights, own, mate):
    first_call = z_first
    out_shape = [pltpu.VMEM((2 * COLS, PIX), jnp.float32)]
    if first_call:
        out_shape.append(pltpu.VMEM((2, COLS, ROWS), jnp.bfloat16))
        out_shape.append(jax.ShapeDtypeStruct((1, N), jnp.float32))
    return pl.pallas_call(
        lambda *refs: partial_kernel(z_first, first_call, *refs),
        in_specs=[SMEM, SMEM] + [VMEM] * (len(weights) + 2),
        out_specs=[VMEM] * len(out_shape),
        out_shape=out_shape,
        compiler_params=limit(12),
        cost_estimate=pl.CostEstimate(
            flops=2 * ROWS * COLS * FEATURES, bytes_accessed=16 * 1024 * 1024, transcendentals=0
        ),
        name="partial_re" if first_call else "partial_im",
    )(sig, pos, *[in_vmem(v) for v in weights], in_vmem(own), in_vmem(mate))


HIGH, LOW = 32, 128
PART = 2048


def insert_kernel(bound_ref, w_ref, ins_ref, *refs):
    scale = bound_ref[4:5, 0:1] * (1.0 / HEADROOM)
    high_ids = lax.broadcasted_iota(jnp.int32, (HIGH, PART), 0)
    low_ids = lax.broadcasted_iota(jnp.int32, (LOW, PART), 0)

    def body(i, acc):
        row = pl.ds(i, 1)
        for j in range(PIX // PART):
            at = slice(j * PART, (j + 1) * PART)
            ids = ins_ref[row, at]
            high = lax.shift_right_logical(ids, 7)
            low = lax.bitwise_and(ids, LOW - 1)
            value = w_ref[row, at] * scale
            head = value.astype(jnp.bfloat16).astype(jnp.float32)
            tail = value - head
            here = high == high_ids
            rows = jnp.concatenate(
                [jnp.where(here, head, 0.0), jnp.where(here, tail, 0.0)], axis=0
            ).astype(jnp.bfloat16)
            table = jnp.where(low == low_ids, 1.0, 0.0).astype(jnp.bfloat16)
            acc = acc + lax.dot_general(
                rows, table, (((1,), (1,)), ((), ())), preferred_element_type=jnp.float32
            )
        return acc

    acc = lax.fori_loop(0, 16, body, jnp.zeros((2 * HIGH, LOW), jnp.float32), unroll=2)
    slab = acc[:HIGH] + acc[HIGH:]
    if len(refs) == 1:
        refs[0][...] = slab
    else:
        first_ref, out_ref = refs
        for h in range(HIGH):
            at = slice(h * LOW, (h + 1) * LOW)
            out_ref[0:1, at] = first_ref[h : h + 1, :]
            out_ref[1:2, at] = slab[h : h + 1, :]


def insert(bound, weighted, insertion, *first):
    shape = (2, VOX) if first else (HIGH, LOW)
    return pl.pallas_call(
        insert_kernel,
        in_specs=[VMEM] * (3 + len(first)),
        out_specs=VMEM,
        out_shape=jax.ShapeDtypeStruct(shape, jnp.float32),
        compiler_params=limit(8),
        cost_estimate=pl.CostEstimate(
            flops=4 * HIGH * LOW * 16 * PIX, bytes_accessed=512 * 1024, transcendentals=0
        ),
        name="insert_im" if first else "insert_re",
    )(bound, weighted.reshape(16, PIX), insertion, *first)


def img_index(z, x, c):
    return (z * X + x) * CORES + c


def pairs(dz, dx, dc=0):
    return [
        (img_index(z, x, c), img_index((z + dz) % Z, (x + dx) % X, (c + dc) % CORES))
        for z in range(Z)
        for x in range(X)
        for c in range(CORES)
    ]


Z_GROUPS = [[img_index(z, x, c) for z in range(Z)] for x in range(X) for c in range(CORES)]


def send(value, dz=0, dx=0, dc=0):
    return lax.ppermute(value, "img", pairs(dz, dx, dc))


def all_to_all_z(value):
    return lax.all_to_all(
        value, "img", split_axis=0, concat_axis=0, tiled=True, axis_index_groups=Z_GROUPS
    )


def gather_x_first(unit):
    row = jnp.stack([unit, send(unit, dx=-1), send(unit, dx=-2), send(unit, dx=1)])
    out = {0: row}
    ahead = behind = row
    for k in range(1, Z // 2 + 1):
        behind = send(behind, dz=1)
        out[Z - k] = behind
        if k < Z // 2:
            ahead = send(ahead, dz=-1)
            out[k] = ahead
    return [out[k] for k in range(Z)]


def gather_z_first(unit):
    copies = jnp.broadcast_to(unit[None], (Z,) + unit.shape)
    column = all_to_all_z(copies)
    return [column, send(column, dx=-1), send(column, dx=-2), send(column, dx=1)]


def wide(value):
    return value.astype(jnp.float32)


def narrow(value):
    return value.astype(jnp.float16)


def scatter_z_first(parts):
    half = Z // 2
    behind = narrow(parts[half])
    for k in range(half, 0, -1):
        if k < half:
            behind = narrow(parts[k] + wide(behind))
        behind = send(behind, dz=1)
    ahead = narrow(parts[half + 1])
    for k in range(half - 1, 0, -1):
        if k < half - 1:
            ahead = narrow(parts[Z - k] + wide(ahead))
        ahead = send(ahead, dz=-1)
    row = parts[0] + wide(behind) + wide(ahead)
    arrived = [send(narrow(row[k]), dx=k) for k in range(1, X)]
    return row[0] + wide(arrived[0]) + wide(arrived[1]) + wide(arrived[2])


def scatter_x_first(parts):
    arrived = [send(narrow(parts[k]), dx=k) for k in range(1, X)]
    column = parts[0] + wide(arrived[0]) + wide(arrived[1]) + wide(arrived[2])
    return jnp.sum(wide(all_to_all_z(narrow(column))), axis=0)


def exchange_refs(value):
    out = [value]
    for k in range(1, REFS):
        out.append(lax.ppermute(value, "ref", [(r, (r + k) % REFS) for r in range(REFS)]))
    return out


def one_device(particles, projections, significance, insertion):
    img = lax.axis_index("img")
    ref = lax.axis_index("ref")
    z, x, core = img >> 3, (img >> 1) & 3, img & 1
    pos = jnp.stack([z, x, core, ref]).astype(jnp.int32)
    sig = lax.dynamic_slice_in_dim(significance, img - core, 2, axis=0)
    table = jnp.asarray(shift_tables())

    mate = send(particles, dc=1)
    by_z = gather_x_first(projections[:, :, :PIX])
    largest = jnp.max(jnp.abs(particles))
    unit = jnp.concatenate(
        [projections[:, :, PIX:], jnp.broadcast_to(largest, (2, 8, EXTRA))], axis=2
    )
    unit, pos, sig = lax.optimization_barrier((unit, pos, sig))
    by_x = gather_z_first(unit)
    own_re, own_im = shifted_images(table, particles)
    mate_re, mate_im = shifted_images(table, mate)

    scores, stats = score_all(sig, pos, by_z, by_x, (own_re, own_im, mate_re, mate_im))
    merged = merge(stats, send(stats, dc=1))
    every = exchange_refs(merged)
    sums_re, weights, evidence = partial_sums(
        True, sig, pos, (scores, *every), own_re, mate_re
    )
    (sums_im,) = partial_sums(False, sig, pos, (weights, merged), own_im, mate_im)
    total_re = scatter_z_first(sums_re.reshape(Z, X, 2, 8, PIX))
    total_im = scatter_x_first(sums_im.reshape(X, Z, 2, 8, PIX))
    ids = insertion.reshape(16, PIX)
    volume_re = insert(merged, total_re, ids)
    volume = insert(merged, total_im, ids, volume_re)
    return volume, evidence.reshape(N)


def solution(mesh):
    in_specs = (P("img", None), P(("img", "ref"), None, None), P(), P(("img", "ref"), None, None))
    out_specs = (P(None, ("img", "ref")), P("img"))
    return jax.shard_map(
        one_device, mesh=mesh, in_specs=in_specs, out_specs=out_specs, check_vma=False
    )
```

```python
import math

import jax
import jax.numpy as jnp
import numpy as np
from jax import lax
from jax.experimental import pallas as pl
from jax.experimental.pallas import tpu as pltpu
from jax.sharding import PartitionSpec as P

SIDE = 64
PIX = 2048
FEATURES = 2 * PIX
VOX = 4096
Z, X, CORES, REFS = 8, 4, 2, 4
RUNS = Z * X
COLS = RUNS * 8
N = 256
SHIFTS = 5
ROWS = SHIFTS * N
NEGATIVE = -1e30
SCALE = 2.0 / math.sqrt(FEATURES)
HEADROOM = 2.5
EXTRA = 128
SPLIT = 2560
REST = FEATURES - SPLIT
BORDER = SPLIT - PIX


def shift_tables():
    p = np.arange(PIX)
    unit = np.float32(2.0 * math.pi / SIDE)
    ax = (unit * (p % SIDE - SIDE // 2).astype(np.float32)).astype(np.float64)
    ay = (unit * (p // SIDE).astype(np.float32)).astype(np.float64)
    rows = [np.cos(ax), np.sin(ax), np.cos(ay), np.sin(ay)]
    return np.stack(rows + rows).astype(np.float32)


VMEM = pl.BlockSpec(memory_space=pltpu.VMEM)
SMEM = pl.BlockSpec(memory_space=pltpu.SMEM)
LANES = 512
PTILE = 512


def in_vmem(value):
    return pltpu.with_memory_space_constraint(value, pltpu.VMEM)


def limit(mib):
    return pltpu.CompilerParams(vmem_limit_bytes=mib * 1024 * 1024)


def prepare_kernel(image_ref, proj_ref, out_ref):
    top = jnp.zeros((16, FEATURES), jnp.bfloat16)
    for i in range(N // 16):
        top = jnp.maximum(top, jnp.abs(image_ref[i * 16 : i * 16 + 16, :]))
    largest = jnp.max(top.astype(jnp.float32), axis=0, keepdims=True)
    largest = jnp.max(largest, axis=1, keepdims=True)
    spread = jnp.broadcast_to(largest, (8, EXTRA)).astype(jnp.bfloat16)
    for b in range(2):
        row = proj_ref[b, :, SPLIT:]
        for k in range(Z):
            out_ref[k, b, :, 0:REST] = row
            out_ref[k, b, :, REST:] = spread


def prepare(images, projections):
    return pl.pallas_call(
        prepare_kernel,
        in_specs=[VMEM, VMEM],
        out_specs=VMEM,
        out_shape=jax.ShapeDtypeStruct((Z, 2, 8, REST + EXTRA), jnp.bfloat16),
        compiler_params=limit(4),
        name="prepare",
    )(in_vmem(images), in_vmem(projections))


def shift_kernel(table_ref, image_ref, out_re, out_im):
    for j in range(PIX // LANES):
        at = slice(j * LANES, (j + 1) * LANES)
        at_im = slice(PIX + j * LANES, PIX + (j + 1) * LANES)
        tables = [table_ref[k : k + 1, at] for k in range(4)]

        @pl.loop(0, N // 16)
        def _(i):
            rows = pl.ds(pl.multiple_of(i * 16, 16), 16)
            re_in, im_in = image_ref[rows, at], image_ref[rows, at_im]
            out_re[0, rows, at] = re_in
            out_im[0, rows, at] = im_in
            re, im = re_in.astype(jnp.float32), im_in.astype(jnp.float32)
            for k in range(2):
                c, s = tables[2 * k], tables[2 * k + 1]
                rc, rs, ic, is_ = re * c, re * s, im * c, im * s
                out_re[1 + 2 * k, rows, at] = (rc - is_).astype(jnp.bfloat16)
                out_im[1 + 2 * k, rows, at] = (rs + ic).astype(jnp.bfloat16)
                out_re[2 + 2 * k, rows, at] = (rc + is_).astype(jnp.bfloat16)
                out_im[2 + 2 * k, rows, at] = (ic - rs).astype(jnp.bfloat16)


def shifted_images(table, images):
    shape = pltpu.VMEM((SHIFTS, N, PIX), jnp.bfloat16)
    return pl.pallas_call(
        shift_kernel,
        in_specs=[VMEM, VMEM],
        out_specs=[VMEM, VMEM],
        out_shape=[shape, shape],
        compiler_params=limit(4),
        cost_estimate=pl.CostEstimate(
            flops=24 * N * PIX, bytes_accessed=12 * 1024 * 1024, transcendentals=0
        ),
        name="shift",
    )(in_vmem(table), in_vmem(images))


def run_entry(sig_ref, pos_ref, q, dz, dx):
    zz = lax.rem(pos_ref[0] + dz, Z)
    xx = lax.rem(pos_ref[1] + dx, X)
    at = (((zz * X + xx) * CORES + pos_ref[2]) * REFS + pos_ref[3]) * 2
    row = pos_ref[2] if q == 0 else 1 - pos_ref[2]
    return sig_ref[row, at], sig_ref[row, at + 1], zz


def score_kernel(sig_ref, pos_ref, *refs):
    by_z = refs[:Z]
    by_x = refs[Z : Z + X]
    sh = refs[Z + X : Z + X + 4]
    st_ref, stat_ref = refs[Z + X + 4 : Z + X + 6]
    sel, acc, mask = refs[Z + X + 6 :]
    stat_ref[...] = jnp.zeros_like(stat_ref)
    for q in range(2):
        for dz in range(Z):
            for dx in range(X):
                o = dz * X + dx
                first, second, zz = run_entry(sig_ref, pos_ref, q, dz, dx)
                sel[q, o, :, 0:SPLIT] = by_z[dz][dx, second]
                sel[q, o, :, SPLIT:] = by_x[dx][zz, second, :, 0:REST]
                live = (first + second).astype(jnp.float32)
                mask[q, o * 8 : o * 8 + 8, :] = jnp.full((8, 128), live, jnp.float32)
    dims = (((1,), (1,)), ((), ()))
    for q in range(2):
        for half in range(2):
            part = lax.dot_general(
                sh[2 * q + half][...].reshape(ROWS, PIX),
                sel[q, :, :, half * PIX : (half + 1) * PIX].reshape(COLS, PIX),
                dims,
                preferred_element_type=jnp.float32,
            )
            if half == 0:
                acc[...] = part
            else:
                acc[...] += part
        live = mask[q, :, 0:1] > 0.5
        top = jnp.full((1, N), NEGATIVE, jnp.float32)
        for t in range(SHIFTS):
            s = acc[t * N : (t + 1) * N, :].T * SCALE
            s = jnp.where(live, s, NEGATIVE)
            st_ref[q, :, t * N : (t + 1) * N] = s
            top = jnp.maximum(top, jnp.max(s, axis=0, keepdims=True))
        total = jnp.zeros((1, N), jnp.float32)
        for t in range(SHIFTS):
            s = st_ref[q, :, t * N : (t + 1) * N]
            e = jnp.where(live, jnp.exp(s - top), 0.0)
            total = total + jnp.sum(e, axis=0, keepdims=True)
        stat_ref[q : q + 1, :] = top
        stat_ref[2 + q : 3 + q, :] = total
    largest = jnp.zeros((8, EXTRA), jnp.float32)
    for dx in range(X):
        for zz in range(Z):
            largest = jnp.maximum(largest, by_x[dx][zz, 0, :, REST:].astype(jnp.float32))
    stat_ref[4:5, 0:EXTRA] = jnp.max(largest, axis=0, keepdims=True)


def score_all(sig, pos, by_z, by_x, shifted):
    return pl.pallas_call(
        score_kernel,
        in_specs=[SMEM, SMEM] + [VMEM] * (Z + X + 4),
        out_specs=[VMEM, VMEM],
        out_shape=[
            pltpu.VMEM((2, COLS, ROWS), jnp.float32),
            pltpu.VMEM((8, N), jnp.float32),
        ],
        scratch_shapes=[
            pltpu.VMEM((2, RUNS, 8, FEATURES), jnp.bfloat16),
            pltpu.VMEM((ROWS, COLS), jnp.float32),
            pltpu.VMEM((2, COLS, 128), jnp.float32),
        ],
        compiler_params=limit(8),
        cost_estimate=pl.CostEstimate(
            flops=4 * ROWS * COLS * FEATURES, bytes_accessed=28 * 1024 * 1024, transcendentals=2 * ROWS * COLS
        ),
        name="scores",
    )(sig, pos, *[in_vmem(v) for v in by_z], *[in_vmem(v) for v in by_x], *[in_vmem(v) for v in shifted])


def merge_kernel(stat_ref, other_ref, out_ref):
    out_ref[...] = jnp.zeros_like(out_ref)
    for q in range(2):
        a, b = stat_ref[q : q + 1, :], other_ref[1 - q : 2 - q, :]
        top = jnp.maximum(a, b)
        out_ref[q : q + 1, :] = top
        out_ref[2 + q : 3 + q, :] = stat_ref[2 + q : 3 + q, :] * jnp.exp(a - top) + other_ref[
            3 - q : 4 - q, :
        ] * jnp.exp(b - top)
    bound = jnp.max(jnp.maximum(stat_ref[4:5, :], other_ref[4:5, :]), axis=1, keepdims=True)
    out_ref[4:5, :] = jnp.broadcast_to(jnp.maximum(bound, 1e-30), (1, N))


def merge(stats, other):
    return pl.pallas_call(
        merge_kernel,
        in_specs=[VMEM, VMEM],
        out_specs=VMEM,
        out_shape=pltpu.VMEM((8, N), jnp.float32),
        compiler_params=limit(2),
        name="merge",
    )(in_vmem(stats), in_vmem(other))


def partial_kernel(z_first, sig_ref, pos_ref, *refs):
    if z_first:
        st_ref, *every = refs[:5]
        images, (out_ref, w_ref, ev_ref) = refs[5:9], refs[9:]
        for q in range(2):
            tops = [r[q : q + 1, :] for r in every]
            top = jnp.maximum(jnp.maximum(tops[0], tops[1]), jnp.maximum(tops[2], tops[3]))
            total = sum(r[2 + q : 3 + q, :] * jnp.exp(t - top) for r, t in zip(every, tops))
            evidence = top + jnp.log(total)
            if q == 0:
                ev_ref[...] = evidence
            for t in range(SHIFTS):
                s = st_ref[q, :, t * N : (t + 1) * N]
                w_ref[q, :, t * N : (t + 1) * N] = jnp.exp(s - evidence).astype(jnp.bfloat16)
        bound_ref = every[0]
        tiles = ((0, 0, PIX // PTILE), (PIX, 1, BORDER // PTILE))
    else:
        w_ref, bound_ref = refs[:2]
        images, (out_ref,) = refs[2:6], refs[6:]
        tiles = ((-BORDER, 1, PIX // PTILE),)
    scale = HEADROOM / bound_ref[4:5, 0:1]
    entries = [
        [run_entry(sig_ref, pos_ref, q, dz, dx) for dz in range(Z) for dx in range(X)]
        for q in range(2)
    ]

    def one_tile(offset, half, i):
        at_in = pl.ds(pl.multiple_of(i * PTILE, PTILE), PTILE)
        at = pl.ds(pl.multiple_of(offset + i * PTILE, PTILE), PTILE)
        for q in range(2):
            value = (
                jnp.dot(
                    w_ref[q],
                    images[2 * q + half][:, :, at_in].reshape(ROWS, PTILE),
                    preferred_element_type=jnp.float32,
                )
                * scale
            )
            for o in range(RUNS):
                _, second, zz = entries[q][o]
                base = (o if z_first else (o % X) * Z + zz) * 16
                rows = pl.ds(pl.multiple_of(base + second * 8, 8), 8)
                block = value[o * 8 : o * 8 + 8, :]
                if q == 0:
                    other = pl.ds(pl.multiple_of(base + (1 - second) * 8, 8), 8)
                    out_ref[rows, at] = block
                    out_ref[other, at] = jnp.zeros_like(block)
                else:
                    out_ref[rows, at] += block

    for offset, half, count in tiles:
        start = max(0, -offset) // PTILE
        pl.loop(start, count)(lambda i, offset=offset, half=half: one_tile(offset, half, i))


def partial_sums(z_first, sig, pos, weights, shifted):
    out_shape = [pltpu.VMEM((2 * COLS, SPLIT if z_first else REST), jnp.float32)]
    if z_first:
        out_shape.append(pltpu.VMEM((2, COLS, ROWS), jnp.bfloat16))
        out_shape.append(jax.ShapeDtypeStruct((1, N), jnp.float32))
    return pl.pallas_call(
        lambda *refs: partial_kernel(z_first, *refs),
        in_specs=[SMEM, SMEM] + [VMEM] * (len(weights) + 4),
        out_specs=[VMEM] * len(out_shape),
        out_shape=out_shape,
        compiler_params=limit(4),
        cost_estimate=pl.CostEstimate(
            flops=2 * ROWS * COLS * FEATURES, bytes_accessed=16 * 1024 * 1024, transcendentals=0
        ),
        name="partial_first" if z_first else "partial_rest",
    )(sig, pos, *[in_vmem(v) for v in weights], *[in_vmem(v) for v in shifted])


HIGH, LOW = 32, 128


def insert_kernel(bound_ref, w_ref, ins_ref, *refs):
    scale = bound_ref[4:5, 0:1] * (1.0 / HEADROOM)
    rest = len(refs) == 3

    def add(acc, i, at, at_ids, width):
        row = pl.ds(i, 1)
        ids = ins_ref[row, at_ids]
        high = lax.shift_right_logical(ids, 7)
        low = lax.bitwise_and(ids, LOW - 1)
        value = w_ref[row, at] * scale
        head = value.astype(jnp.bfloat16).astype(jnp.float32)
        tail = value - head
        here = high == lax.broadcasted_iota(jnp.int32, (HIGH, width), 0)
        rows = jnp.concatenate(
            [jnp.where(here, head, 0.0), jnp.where(here, tail, 0.0)], axis=0
        ).astype(jnp.bfloat16)
        there = low == lax.broadcasted_iota(jnp.int32, (LOW, width), 0)
        table = jnp.where(there, 1.0, 0.0).astype(jnp.bfloat16)
        return acc + lax.dot_general(
            rows, table, (((1,), (1,)), ((), ())), preferred_element_type=jnp.float32
        )

    empty = jnp.zeros((2 * HIGH, LOW), jnp.float32)
    if rest:
        re_ref, im_ref, out_ref = refs
        step = lambda i, acc: add(acc, i, slice(0, REST), slice(BORDER, PIX), REST)
        acc = lax.fori_loop(0, 16, step, empty, unroll=2)
        slab = im_ref[...] + acc[:HIGH] + acc[HIGH:]
        for h in range(HIGH):
            at = slice(h * LOW, (h + 1) * LOW)
            out_ref[0:1, at] = re_ref[h : h + 1, :]
            out_ref[1:2, at] = slab[h : h + 1, :]
    else:
        re_ref, im_ref = refs

        def step(i, both):
            re, im = both
            re = add(re, i, slice(0, PIX), slice(0, PIX), PIX)
            im = add(im, i, slice(PIX, SPLIT), slice(0, BORDER), BORDER)
            return re, im

        re, im = lax.fori_loop(0, 16, step, (empty, empty))
        re_ref[...] = re[:HIGH] + re[HIGH:]
        im_ref[...] = im[:HIGH] + im[HIGH:]


def insert(bound, weighted, insertion, *slabs):
    slab = jax.ShapeDtypeStruct((HIGH, LOW), jnp.float32)
    return pl.pallas_call(
        insert_kernel,
        in_specs=[VMEM] * (3 + len(slabs)),
        out_specs=VMEM if slabs else [VMEM, VMEM],
        out_shape=jax.ShapeDtypeStruct((2, VOX), jnp.float32) if slabs else [slab, slab],
        compiler_params=limit(8),
        cost_estimate=pl.CostEstimate(
            flops=4 * HIGH * LOW * 16 * PIX, bytes_accessed=512 * 1024, transcendentals=0
        ),
        name="insert_rest" if slabs else "insert_first",
    )(bound, weighted.reshape(16, weighted.shape[-1]), insertion, *slabs)


def img_index(z, x, c):
    return (z * X + x) * CORES + c


def pairs(dz, dx, dc=0):
    return [
        (img_index(z, x, c), img_index((z + dz) % Z, (x + dx) % X, (c + dc) % CORES))
        for z in range(Z)
        for x in range(X)
        for c in range(CORES)
    ]


Z_GROUPS = [[img_index(z, x, c) for z in range(Z)] for x in range(X) for c in range(CORES)]


def send(value, dz=0, dx=0, dc=0):
    return lax.ppermute(value, "img", pairs(dz, dx, dc))


def all_to_all_z(value):
    return lax.all_to_all(
        value, "img", split_axis=0, concat_axis=0, tiled=True, axis_index_groups=Z_GROUPS
    )


def gather_x_first(unit):
    row = jnp.stack([unit, send(unit, dx=-1), send(unit, dx=-2), send(unit, dx=1)])
    out = {0: row}
    ahead = behind = row
    for k in range(1, Z // 2 + 1):
        behind = send(behind, dz=1)
        out[Z - k] = behind
        if k < Z // 2:
            ahead = send(ahead, dz=-1)
            out[k] = ahead
    return [out[k] for k in range(Z)]


def gather_z_first(copies):
    column = all_to_all_z(copies)
    return [column, send(column, dx=-1), send(column, dx=-2), send(column, dx=1)]


def wide(value):
    return value.astype(jnp.float32)


def narrow(value):
    return value.astype(jnp.float16)


def scatter_z_first(parts):
    half = Z // 2
    behind = narrow(parts[half])
    for k in range(half, 0, -1):
        if k < half:
            behind = narrow(parts[k] + wide(behind))
        behind = send(behind, dz=1)
    ahead = narrow(parts[half + 1])
    for k in range(half - 1, 0, -1):
        if k < half - 1:
            ahead = narrow(parts[Z - k] + wide(ahead))
        ahead = send(ahead, dz=-1)
    row = parts[0] + wide(behind) + wide(ahead)
    arrived = [send(narrow(row[k]), dx=k) for k in range(1, X)]
    return row[0] + wide(arrived[0]) + wide(arrived[1]) + wide(arrived[2])


def scatter_x_first(parts):
    arrived = [send(narrow(parts[k]), dx=k) for k in range(1, X)]
    column = parts[0] + wide(arrived[0]) + wide(arrived[1]) + wide(arrived[2])
    return jnp.sum(wide(all_to_all_z(narrow(column))), axis=0)


def exchange_refs(value):
    out = [value]
    for k in range(1, REFS):
        out.append(lax.ppermute(value, "ref", [(r, (r + k) % REFS) for r in range(REFS)]))
    return out


def one_device(particles, projections, significance, insertion):
    img = lax.axis_index("img")
    ref = lax.axis_index("ref")
    z, x, core = img >> 3, (img >> 1) & 3, img & 1
    pos = jnp.stack([z, x, core, ref]).astype(jnp.int32)
    sig = lax.dynamic_slice_in_dim(significance, img - core, 2, axis=0)
    table = jnp.asarray(shift_tables())

    mate = send(particles, dc=1)
    by_z = gather_x_first(projections[:, :, :SPLIT])
    copies = prepare(particles, projections)
    copies, pos, sig = lax.optimization_barrier((copies, pos, sig))
    by_x = gather_z_first(copies)
    own_re, own_im = shifted_images(table, particles)
    mate_re, mate_im = shifted_images(table, mate)

    shifted = (own_re, own_im, mate_re, mate_im)
    scores, stats = score_all(sig, pos, by_z, by_x, shifted)
    merged = merge(stats, send(stats, dc=1))
    every = exchange_refs(merged)
    sums, weights, evidence = partial_sums(True, sig, pos, (scores, *every), shifted)
    (sums_rest,) = partial_sums(False, sig, pos, (weights, merged), shifted)
    total = scatter_z_first(sums.reshape(Z, X, 2, 8, SPLIT))
    total_rest = scatter_x_first(sums_rest.reshape(X, Z, 2, 8, REST))
    ids = insertion.reshape(16, PIX)
    slabs = insert(merged, total, ids)
    volume = insert(merged, total_rest, ids, *slabs)
    return volume, evidence.reshape(N)


def solution(mesh):
    in_specs = (P("img", None), P(("img", "ref"), None, None), P(), P(("img", "ref"), None, None))
    out_specs = (P(None, ("img", "ref")), P("img"))
    return jax.shard_map(
        one_device, mesh=mesh, in_specs=in_specs, out_specs=out_specs, check_vma=False
    )
```

```python
import math

import jax
import jax.numpy as jnp
import numpy as np
from jax import lax
from jax.experimental import pallas as pl
from jax.experimental.pallas import tpu as pltpu
from jax.sharding import PartitionSpec as P

SIDE = 64
PIX = 2048
FEATURES = 2 * PIX
VOX = 4096
Z, X, CORES, REFS = 8, 4, 2, 4
RUNS = Z * X
COLS = RUNS * 8
N = 256
SHIFTS = 5
ROWS = SHIFTS * N
NEGATIVE = -1e30
SCALE = 2.0 / math.sqrt(FEATURES)
HEADROOM = 2.5
EXTRA = 128
SPLIT = 2560
REST = FEATURES - SPLIT
BORDER = SPLIT - PIX
UNIT = REST + EXTRA
MESSAGE = X * SPLIT + UNIT
EARLY = (0, 1, 2, 6, 7)
LATE = (3, 4, 5)


def shift_tables():
    p = np.arange(PIX)
    unit = np.float32(2.0 * math.pi / SIDE)
    ax = (unit * (p % SIDE - SIDE // 2).astype(np.float32)).astype(np.float64)
    ay = (unit * (p // SIDE).astype(np.float32)).astype(np.float64)
    rows = [np.cos(ax), np.sin(ax), np.cos(ay), np.sin(ay)]
    return np.stack(rows + rows).astype(np.float32)


VMEM = pl.BlockSpec(memory_space=pltpu.VMEM)
SMEM = pl.BlockSpec(memory_space=pltpu.SMEM)
LANES = 512
PTILE = 512


def in_vmem(value):
    return pltpu.with_memory_space_constraint(value, pltpu.VMEM)


def limit(mib):
    return pltpu.CompilerParams(vmem_limit_bytes=mib * 1024 * 1024)


def prepare_kernel(image_ref, proj_ref, out_ref):
    top = jnp.zeros((16, FEATURES), jnp.bfloat16)
    for i in range(N // 16):
        top = jnp.maximum(top, jnp.abs(image_ref[i * 16 : i * 16 + 16, :]))
    largest = jnp.max(top.astype(jnp.float32), axis=0, keepdims=True)
    largest = jnp.max(largest, axis=1, keepdims=True)
    out_ref[:, :, 0:REST] = proj_ref[:, :, SPLIT:]
    for b in range(2):
        out_ref[b, :, REST:] = jnp.broadcast_to(largest, (8, EXTRA)).astype(jnp.bfloat16)


def prepare(images, projections):
    return pl.pallas_call(
        prepare_kernel,
        in_specs=[VMEM, VMEM],
        out_specs=VMEM,
        out_shape=pltpu.VMEM((2, 8, UNIT), jnp.bfloat16),
        compiler_params=limit(2),
        name="prepare",
    )(in_vmem(images), in_vmem(projections))


def assemble_kernel(*refs):
    *parts, out_ref = refs
    for k, part in enumerate(parts):
        out_ref[:, :, k * SPLIT : k * SPLIT + part.shape[2]] = part[...]


def assemble(row, unit):
    return pl.pallas_call(
        assemble_kernel,
        in_specs=[VMEM] * (X + 1),
        out_specs=VMEM,
        out_shape=pltpu.VMEM((2, 8, MESSAGE), jnp.bfloat16),
        compiler_params=limit(2),
        name="assemble",
    )(*[in_vmem(v) for v in (*row, unit)])


def pick_kernel(*refs):
    *messages, out_ref = refs
    for k, message in enumerate(messages):
        out_ref[k] = message[:, :, X * SPLIT :]


def pick(messages):
    return pl.pallas_call(
        pick_kernel,
        in_specs=[VMEM] * len(messages),
        out_specs=VMEM,
        out_shape=pltpu.VMEM((len(messages), 2, 8, UNIT), jnp.bfloat16),
        compiler_params=limit(2),
        name="pick",
    )(*[in_vmem(v) for v in messages])


def shift_kernel(table_ref, image_ref, out_re, out_im):
    for j in range(PIX // LANES):
        at = slice(j * LANES, (j + 1) * LANES)
        at_im = slice(PIX + j * LANES, PIX + (j + 1) * LANES)
        tables = [table_ref[k : k + 1, at] for k in range(4)]

        @pl.loop(0, N // 16)
        def _(i):
            rows = pl.ds(pl.multiple_of(i * 16, 16), 16)
            re_in, im_in = image_ref[rows, at], image_ref[rows, at_im]
            out_re[0, rows, at] = re_in
            out_im[0, rows, at] = im_in
            re, im = re_in.astype(jnp.float32), im_in.astype(jnp.float32)
            for k in range(2):
                c, s = tables[2 * k], tables[2 * k + 1]
                rc, rs, ic, is_ = re * c, re * s, im * c, im * s
                out_re[1 + 2 * k, rows, at] = (rc - is_).astype(jnp.bfloat16)
                out_im[1 + 2 * k, rows, at] = (rs + ic).astype(jnp.bfloat16)
                out_re[2 + 2 * k, rows, at] = (rc + is_).astype(jnp.bfloat16)
                out_im[2 + 2 * k, rows, at] = (ic - rs).astype(jnp.bfloat16)


def shifted_images(table, images):
    shape = pltpu.VMEM((SHIFTS, N, PIX), jnp.bfloat16)
    return pl.pallas_call(
        shift_kernel,
        in_specs=[VMEM, VMEM],
        out_specs=[VMEM, VMEM],
        out_shape=[shape, shape],
        compiler_params=limit(4),
        cost_estimate=pl.CostEstimate(
            flops=24 * N * PIX, bytes_accessed=12 * 1024 * 1024, transcendentals=0
        ),
        name="shift",
    )(in_vmem(table), in_vmem(images))


def run_entry(sig_ref, pos_ref, q, dz, dx):
    zz = lax.rem(pos_ref[0] + dz, Z)
    xx = lax.rem(pos_ref[1] + dx, X)
    at = (((zz * X + xx) * CORES + pos_ref[2]) * REFS + pos_ref[3]) * 2
    row = pos_ref[2] if q == 0 else 1 - pos_ref[2]
    return sig_ref[row, at], sig_ref[row, at + 1], zz


DIMS = (((1,), (1,)), ((), ()))


def score_first_kernel(sig_ref, pos_ref, *refs):
    messages, sh, (acc_ref, sel) = refs[:Z], refs[Z : Z + 4], refs[Z + 4 :]
    for q in range(2):
        for o in range(RUNS):
            dz, dx = o // X, o % X
            _, second, _ = run_entry(sig_ref, pos_ref, q, dz, dx)
            sel[o] = messages[dz][second, :, dx * SPLIT : (dx + 1) * SPLIT]
        acc_ref[q] = lax.dot_general(
            sh[2 * q][...].reshape(ROWS, PIX),
            sel[:, :, 0:PIX].reshape(COLS, PIX),
            DIMS,
            preferred_element_type=jnp.float32,
        )
        acc_ref[q] += lax.dot_general(
            sh[2 * q + 1][:, :, 0:BORDER].reshape(ROWS, BORDER),
            sel[:, :, PIX:].reshape(COLS, BORDER),
            DIMS,
            preferred_element_type=jnp.float32,
        )


def score_first(sig, pos, messages, shifted):
    return pl.pallas_call(
        score_first_kernel,
        in_specs=[SMEM, SMEM] + [VMEM] * (Z + 4),
        out_specs=VMEM,
        out_shape=pltpu.VMEM((2, ROWS, COLS), jnp.float32),
        scratch_shapes=[pltpu.VMEM((RUNS, 8, SPLIT), jnp.bfloat16)],
        compiler_params=limit(8),
        cost_estimate=pl.CostEstimate(
            flops=4 * ROWS * COLS * SPLIT, bytes_accessed=16 * 1024 * 1024, transcendentals=0
        ),
        name="score_first",
    )(sig, pos, *[in_vmem(v) for v in messages], *[in_vmem(v) for v in shifted])


def score_rest_kernel(sig_ref, pos_ref, *refs):
    messages, batches = refs[:Z], refs[Z : Z + 6]
    sh, acc = refs[Z + 6 : Z + 8], refs[Z + 8]
    st_ref, stat_ref, sel, work, mask = refs[Z + 9 :]

    def unit(dz, dx, second, at):
        if dx == 0:
            return messages[dz][second, :, X * SPLIT + at.start : X * SPLIT + at.stop]
        early = dz in EARLY
        place = (EARLY if early else LATE).index(dz)
        return batches[dx - 1 if early else dx + 2][place, second, :, at]

    stat_ref[...] = jnp.zeros_like(stat_ref)
    largest = jnp.zeros((8, EXTRA), jnp.float32)
    for o in range(RUNS):
        top = unit(o // X, o % X, 0, slice(REST, UNIT))
        largest = jnp.maximum(largest, top.astype(jnp.float32))
    stat_ref[4:5, 0:EXTRA] = jnp.max(largest, axis=0, keepdims=True)
    for q in range(2):
        for o in range(RUNS):
            first, second, _ = run_entry(sig_ref, pos_ref, q, o // X, o % X)
            sel[o] = unit(o // X, o % X, second, slice(0, REST))
            live = (first + second).astype(jnp.float32)
            mask[o * 8 : o * 8 + 8, :] = jnp.full((8, 128), live, jnp.float32)
        work[...] = acc[q] + lax.dot_general(
            sh[q][:, :, BORDER:].reshape(ROWS, REST),
            sel[...].reshape(COLS, REST),
            DIMS,
            preferred_element_type=jnp.float32,
        )
        live = mask[:, 0:1] > 0.5
        top = jnp.full((1, N), NEGATIVE, jnp.float32)
        for t in range(SHIFTS):
            s = work[t * N : (t + 1) * N, :].T * SCALE
            s = jnp.where(live, s, NEGATIVE)
            st_ref[q, :, t * N : (t + 1) * N] = s
            top = jnp.maximum(top, jnp.max(s, axis=0, keepdims=True))
        total = jnp.zeros((1, N), jnp.float32)
        for t in range(SHIFTS):
            s = st_ref[q, :, t * N : (t + 1) * N]
            e = jnp.where(live, jnp.exp(s - top), 0.0)
            total = total + jnp.sum(e, axis=0, keepdims=True)
        stat_ref[q : q + 1, :] = top
        stat_ref[2 + q : 3 + q, :] = total


def score_rest(sig, pos, messages, batches, shifted, acc):
    return pl.pallas_call(
        score_rest_kernel,
        in_specs=[SMEM, SMEM] + [VMEM] * (Z + 9),
        out_specs=[VMEM, VMEM],
        out_shape=[
            pltpu.VMEM((2, COLS, ROWS), jnp.float32),
            pltpu.VMEM((8, N), jnp.float32),
        ],
        scratch_shapes=[
            pltpu.VMEM((RUNS, 8, REST), jnp.bfloat16),
            pltpu.VMEM((ROWS, COLS), jnp.float32),
            pltpu.VMEM((COLS, 128), jnp.float32),
        ],
        compiler_params=limit(8),
        cost_estimate=pl.CostEstimate(
            flops=4 * ROWS * COLS * REST, bytes_accessed=16 * 1024 * 1024, transcendentals=2 * ROWS * COLS
        ),
        name="score_rest",
    )(
        sig,
        pos,
        *[in_vmem(v) for v in (*messages, *batches, shifted[1], shifted[3], acc)],
    )


def merge_kernel(stat_ref, other_ref, out_ref):
    out_ref[...] = jnp.zeros_like(out_ref)
    for q in range(2):
        a, b = stat_ref[q : q + 1, :], other_ref[1 - q : 2 - q, :]
        top = jnp.maximum(a, b)
        out_ref[q : q + 1, :] = top
        out_ref[2 + q : 3 + q, :] = stat_ref[2 + q : 3 + q, :] * jnp.exp(a - top) + other_ref[
            3 - q : 4 - q, :
        ] * jnp.exp(b - top)
    bound = jnp.max(jnp.maximum(stat_ref[4:5, :], other_ref[4:5, :]), axis=1, keepdims=True)
    out_ref[4:5, :] = jnp.broadcast_to(jnp.maximum(bound, 1e-30), (1, N))


def merge(stats, other):
    return pl.pallas_call(
        merge_kernel,
        in_specs=[VMEM, VMEM],
        out_specs=VMEM,
        out_shape=pltpu.VMEM((8, N), jnp.float32),
        compiler_params=limit(2),
        name="merge",
    )(in_vmem(stats), in_vmem(other))


def partial_kernel(z_first, sig_ref, pos_ref, *refs):
    if z_first:
        st_ref, every = refs[:2]
        images, (out_ref, w_ref, ev_ref) = refs[2:6], refs[6:]
        for q in range(2):
            tops = [every[k, q : q + 1, :] for k in range(REFS)]
            top = jnp.maximum(jnp.maximum(tops[0], tops[1]), jnp.maximum(tops[2], tops[3]))
            total = sum(
                every[k, 2 + q : 3 + q, :] * jnp.exp(tops[k] - top) for k in range(REFS)
            )
            evidence = top + jnp.log(total)
            if q == 0:
                ev_ref[...] = evidence
            for t in range(SHIFTS):
                s = st_ref[q, :, t * N : (t + 1) * N]
                w_ref[q, :, t * N : (t + 1) * N] = jnp.exp(s - evidence).astype(jnp.bfloat16)
        bound = every[0, 4:5, 0:1]
        tiles = ((0, 0, PIX // PTILE), (PIX, 1, BORDER // PTILE))
    else:
        w_ref, bound_ref = refs[:2]
        bound = bound_ref[4:5, 0:1]
        images, (out_ref,) = refs[2:6], refs[6:]
        tiles = ((-BORDER, 1, PIX // PTILE),)
    scale = HEADROOM / bound
    entries = [
        [run_entry(sig_ref, pos_ref, q, dz, dx) for dz in range(Z) for dx in range(X)]
        for q in range(2)
    ]

    def one_tile(offset, half, i):
        at_in = pl.ds(pl.multiple_of(i * PTILE, PTILE), PTILE)
        at = pl.ds(pl.multiple_of(offset + i * PTILE, PTILE), PTILE)
        for q in range(2):
            value = (
                jnp.dot(
                    w_ref[q],
                    images[2 * q + half][:, :, at_in].reshape(ROWS, PTILE),
                    preferred_element_type=jnp.float32,
                )
                * scale
            )
            for o in range(RUNS):
                _, second, zz = entries[q][o]
                base = (o if z_first else (o % X) * Z + zz) * 16
                rows = pl.ds(pl.multiple_of(base + second * 8, 8), 8)
                block = value[o * 8 : o * 8 + 8, :]
                if q == 0:
                    other = pl.ds(pl.multiple_of(base + (1 - second) * 8, 8), 8)
                    out_ref[rows, at] = block
                    out_ref[other, at] = jnp.zeros_like(block)
                else:
                    out_ref[rows, at] += block

    for offset, half, count in tiles:
        start = max(0, -offset) // PTILE
        pl.loop(start, count)(lambda i, offset=offset, half=half: one_tile(offset, half, i))


def partial_sums(z_first, sig, pos, weights, shifted):
    out_shape = [pltpu.VMEM((2 * COLS, SPLIT if z_first else REST), jnp.float32)]
    if z_first:
        out_shape.append(pltpu.VMEM((2, COLS, ROWS), jnp.bfloat16))
        out_shape.append(jax.ShapeDtypeStruct((1, N), jnp.float32))
    return pl.pallas_call(
        lambda *refs: partial_kernel(z_first, *refs),
        in_specs=[SMEM, SMEM] + [VMEM] * (len(weights) + 4),
        out_specs=[VMEM] * len(out_shape),
        out_shape=out_shape,
        compiler_params=limit(4),
        cost_estimate=pl.CostEstimate(
            flops=2 * ROWS * COLS * FEATURES, bytes_accessed=16 * 1024 * 1024, transcendentals=0
        ),
        name="partial_first" if z_first else "partial_rest",
    )(sig, pos, *[in_vmem(v) for v in weights], *[in_vmem(v) for v in shifted])


HIGH, LOW = 32, 128


def insert_kernel(bound_ref, w_ref, ins_ref, *refs):
    scale = bound_ref[4:5, 0:1] * (1.0 / HEADROOM)
    rest = len(refs) == 1

    def add(acc, i, at, at_ids, width):
        row = pl.ds(i, 1)
        ids = ins_ref[row, at_ids]
        high = lax.shift_right_logical(ids, 7)
        low = lax.bitwise_and(ids, LOW - 1)
        value = w_ref[row, at] * scale
        head = value.astype(jnp.bfloat16).astype(jnp.float32)
        tail = value - head
        here = high == lax.broadcasted_iota(jnp.int32, (HIGH, width), 0)
        rows = jnp.concatenate(
            [jnp.where(here, head, 0.0), jnp.where(here, tail, 0.0)], axis=0
        ).astype(jnp.bfloat16)
        there = low == lax.broadcasted_iota(jnp.int32, (LOW, width), 0)
        table = jnp.where(there, 1.0, 0.0).astype(jnp.bfloat16)
        return acc + lax.dot_general(
            rows, table, (((1,), (1,)), ((), ())), preferred_element_type=jnp.float32
        )

    empty = jnp.zeros((2 * HIGH, LOW), jnp.float32)
    if rest:
        step = lambda i, acc: add(acc, i, slice(0, REST), slice(BORDER, PIX), REST)
        acc = lax.fori_loop(0, 16, step, empty)
        refs[0][...] = acc[:HIGH] + acc[HIGH:]
    else:
        slab_ref, out_ref = refs

        def step(i, both):
            re, im = both
            re = add(re, i, slice(0, PIX), slice(0, PIX), PIX)
            im = add(im, i, slice(PIX, SPLIT), slice(0, BORDER), BORDER)
            return re, im

        re, im = lax.fori_loop(0, 16, step, (empty, empty))
        re = re[:HIGH] + re[HIGH:]
        im = slab_ref[...] + im[:HIGH] + im[HIGH:]
        for h in range(HIGH):
            at = slice(h * LOW, (h + 1) * LOW)
            out_ref[0:1, at] = re[h : h + 1, :]
            out_ref[1:2, at] = im[h : h + 1, :]


def insert_call(shape, *args):
    return pl.pallas_call(
        insert_kernel,
        in_specs=[VMEM] * len(args),
        out_specs=VMEM,
        out_shape=jax.ShapeDtypeStruct(shape, jnp.float32),
        compiler_params=limit(8),
        cost_estimate=pl.CostEstimate(
            flops=4 * HIGH * LOW * 16 * PIX, bytes_accessed=512 * 1024, transcendentals=0
        ),
    )(*args)


def insert_rest(bound, weighted, insertion):
    return insert_call((HIGH, LOW), bound, weighted.reshape(16, REST), insertion)


def insert_first(bound, weighted, insertion, slab):
    return insert_call((2, VOX), bound, weighted.reshape(16, SPLIT), insertion, slab)


def img_index(z, x, c):
    return (z * X + x) * CORES + c


def pairs(dz, dx, dc=0):
    return [
        (img_index(z, x, c), img_index((z + dz) % Z, (x + dx) % X, (c + dc) % CORES))
        for z in range(Z)
        for x in range(X)
        for c in range(CORES)
    ]


Z_GROUPS = [[img_index(z, x, c) for z in range(Z)] for x in range(X) for c in range(CORES)]


def send(value, dz=0, dx=0, dc=0):
    return lax.ppermute(value, "img", pairs(dz, dx, dc))


def all_to_all_z(value):
    return lax.all_to_all(
        value, "img", split_axis=0, concat_axis=0, tiled=True, axis_index_groups=Z_GROUPS
    )


def gather(projections, unit):
    mine = projections[:, :, :SPLIT]
    row = [mine, send(mine, dx=-1), send(mine, dx=-2), send(mine, dx=1)]
    ahead = behind = assemble(row, unit)
    messages = {0: ahead}
    for k in range(1, Z // 2 + 1):
        behind = send(behind, dz=1)
        messages[Z - k] = behind
        if k < Z // 2:
            ahead = send(ahead, dz=-1)
            messages[k] = ahead
    batches = []
    for places in (EARLY, LATE):
        column = pick([messages[k] for k in places])
        for dx in (-1, -2, 1):
            batches.append(send(column, dx=dx))
    return [messages[k] for k in range(Z)], batches


def wide(value):
    return value.astype(jnp.float32)


def narrow(value):
    return value.astype(jnp.float16)


def scatter_z_first(parts):
    half = Z // 2
    behind = narrow(parts[half])
    for k in range(half, 0, -1):
        if k < half:
            behind = narrow(parts[k] + wide(behind))
        behind = send(behind, dz=1)
    ahead = narrow(parts[half + 1])
    for k in range(half - 1, 0, -1):
        if k < half - 1:
            ahead = narrow(parts[Z - k] + wide(ahead))
        ahead = send(ahead, dz=-1)
    row = parts[0] + wide(behind) + wide(ahead)
    arrived = [send(narrow(row[k]), dx=k) for k in range(1, X)]
    return row[0] + wide(arrived[0]) + wide(arrived[1]) + wide(arrived[2])


def scatter_x_first(parts):
    arrived = [send(narrow(parts[k]), dx=k) for k in range(1, X)]
    column = parts[0] + wide(arrived[0]) + wide(arrived[1]) + wide(arrived[2])
    return jnp.sum(wide(all_to_all_z(narrow(column))), axis=0)


def exchange_refs(value):
    return lax.all_gather(value, "ref")


def one_device(particles, projections, significance, insertion):
    img = lax.axis_index("img")
    ref = lax.axis_index("ref")
    z, x, core = img >> 3, (img >> 1) & 3, img & 1
    pos = jnp.stack([z, x, core, ref]).astype(jnp.int32)
    sig = lax.dynamic_slice_in_dim(significance, img - core, 2, axis=0)
    table = jnp.asarray(shift_tables())

    mate = send(particles, dc=1)
    unit = prepare(particles, projections)
    unit, pos, sig = lax.optimization_barrier((unit, pos, sig))
    messages, batches = gather(projections, unit)
    own_re, own_im = shifted_images(table, particles)
    mate_re, mate_im = shifted_images(table, mate)

    shifted = (own_re, own_im, mate_re, mate_im)
    acc = score_first(sig, pos, messages, shifted)
    scores, stats = score_rest(sig, pos, messages, batches, shifted, acc)
    merged = merge(stats, send(stats, dc=1))
    every = exchange_refs(merged)
    sums, weights, evidence = partial_sums(True, sig, pos, (scores, every), shifted)
    (sums_rest,) = partial_sums(False, sig, pos, (weights, merged), shifted)
    total = scatter_z_first(sums.reshape(Z, X, 2, 8, SPLIT))
    total_rest = scatter_x_first(sums_rest.reshape(X, Z, 2, 8, REST))
    ids = insertion.reshape(16, PIX)
    slab = insert_rest(merged, total_rest, ids)
    volume = insert_first(merged, total, ids, slab)
    return volume, evidence.reshape(N)


def solution(mesh):
    in_specs = (P("img", None), P(("img", "ref"), None, None), P(), P(("img", "ref"), None, None))
    out_specs = (P(None, ("img", "ref")), P("img"))
    return jax.shard_map(
        one_device, mesh=mesh, in_specs=in_specs, out_specs=out_specs, check_vma=False
    )
```

```python
import math

import jax
import jax.numpy as jnp
import numpy as np
from jax import lax
from jax.experimental import pallas as pl
from jax.experimental.pallas import tpu as pltpu
from jax.sharding import PartitionSpec as P

SIDE = 64
PIX = 2048
FEATURES = 2 * PIX
VOX = 4096
Z, X, CORES, REFS = 8, 4, 2, 4
RUNS = Z * X
COLS = RUNS * 8
N = 256
SHIFTS = 5
ROWS = SHIFTS * N
NEGATIVE = -1e30
SCALE = 2.0 / math.sqrt(FEATURES)
HEADROOM = 2.5
EXTRA = 128
SPLIT = 2560
REST = FEATURES - SPLIT
BORDER = SPLIT - PIX
UNIT = REST + EXTRA
MESSAGE = X * SPLIT + UNIT
EARLY = (0, 1, 2, 6, 7)
LATE = (3, 4, 5)


def shift_tables():
    p = np.arange(PIX)
    unit = np.float32(2.0 * math.pi / SIDE)
    ax = (unit * (p % SIDE - SIDE // 2).astype(np.float32)).astype(np.float64)
    ay = (unit * (p // SIDE).astype(np.float32)).astype(np.float64)
    rows = [np.cos(ax), np.sin(ax), np.cos(ay), np.sin(ay)]
    return np.stack(rows + rows).astype(np.float32)


VMEM = pl.BlockSpec(memory_space=pltpu.VMEM)
SMEM = pl.BlockSpec(memory_space=pltpu.SMEM)
LANES = 512
PTILE = 512


def in_vmem(value):
    return pltpu.with_memory_space_constraint(value, pltpu.VMEM)


def limit(mib):
    return pltpu.CompilerParams(vmem_limit_bytes=mib * 1024 * 1024)


def prepare_kernel(image_ref, proj_ref, out_ref):
    top = jnp.zeros((16, FEATURES), jnp.bfloat16)
    for i in range(N // 16):
        top = jnp.maximum(top, jnp.abs(image_ref[i * 16 : i * 16 + 16, :]))
    largest = jnp.max(top.astype(jnp.float32), axis=0, keepdims=True)
    largest = jnp.max(largest, axis=1, keepdims=True)
    out_ref[:, :, 0:REST] = proj_ref[:, :, SPLIT:]
    for b in range(2):
        out_ref[b, :, REST:] = jnp.broadcast_to(largest, (8, EXTRA)).astype(jnp.bfloat16)


def prepare(images, projections):
    return pl.pallas_call(
        prepare_kernel,
        in_specs=[VMEM, VMEM],
        out_specs=VMEM,
        out_shape=pltpu.VMEM((2, 8, UNIT), jnp.bfloat16),
        compiler_params=limit(2),
        name="prepare",
    )(in_vmem(images), in_vmem(projections))


def assemble_kernel(*refs):
    *parts, out_ref = refs
    for k, part in enumerate(parts):
        out_ref[:, :, k * SPLIT : k * SPLIT + part.shape[2]] = part[...]


def assemble(row, unit):
    return pl.pallas_call(
        assemble_kernel,
        in_specs=[VMEM] * (X + 1),
        out_specs=VMEM,
        out_shape=pltpu.VMEM((2, 8, MESSAGE), jnp.bfloat16),
        compiler_params=limit(2),
        name="assemble",
    )(*[in_vmem(v) for v in (*row, unit)])


def pick_kernel(*refs):
    *messages, out_ref = refs
    for k, message in enumerate(messages):
        out_ref[k] = message[:, :, X * SPLIT :]


def pick(messages):
    return pl.pallas_call(
        pick_kernel,
        in_specs=[VMEM] * len(messages),
        out_specs=VMEM,
        out_shape=pltpu.VMEM((len(messages), 2, 8, UNIT), jnp.bfloat16),
        compiler_params=limit(2),
        name="pick",
    )(*[in_vmem(v) for v in messages])


def shift_kernel(table_ref, own_ref, mate_ref, out_re, out_im):
    for q, image_ref in enumerate((own_ref, mate_ref)):
        for j in range(PIX // LANES):
            at = slice(j * LANES, (j + 1) * LANES)
            at_im = slice(PIX + j * LANES, PIX + (j + 1) * LANES)
            tables = [table_ref[k : k + 1, at] for k in range(4)]

            @pl.loop(0, N // 16)
            def _(i):
                rows = pl.ds(pl.multiple_of(i * 16, 16), 16)
                re_in, im_in = image_ref[rows, at], image_ref[rows, at_im]
                out_re[q, 0, rows, at] = re_in
                out_im[q, 0, rows, at] = im_in
                re, im = re_in.astype(jnp.float32), im_in.astype(jnp.float32)
                for k in range(2):
                    c, s = tables[2 * k], tables[2 * k + 1]
                    rc, rs, ic, is_ = re * c, re * s, im * c, im * s
                    out_re[q, 1 + 2 * k, rows, at] = (rc - is_).astype(jnp.bfloat16)
                    out_im[q, 1 + 2 * k, rows, at] = (rs + ic).astype(jnp.bfloat16)
                    out_re[q, 2 + 2 * k, rows, at] = (rc + is_).astype(jnp.bfloat16)
                    out_im[q, 2 + 2 * k, rows, at] = (ic - rs).astype(jnp.bfloat16)


def shifted_images(table, own, mate):
    shape = pltpu.VMEM((2, SHIFTS, N, PIX), jnp.bfloat16)
    return pl.pallas_call(
        shift_kernel,
        in_specs=[VMEM] * 3,
        out_specs=[VMEM, VMEM],
        out_shape=[shape, shape],
        compiler_params=limit(4),
        cost_estimate=pl.CostEstimate(
            flops=48 * N * PIX, bytes_accessed=24 * 1024 * 1024, transcendentals=0
        ),
        name="shift",
    )(in_vmem(table), in_vmem(own), in_vmem(mate))


def run_entry(sig_ref, pos_ref, q, dz, dx):
    zz = lax.rem(pos_ref[0] + dz, Z)
    xx = lax.rem(pos_ref[1] + dx, X)
    at = (((zz * X + xx) * CORES + pos_ref[2]) * REFS + pos_ref[3]) * 2
    row = lax.rem(pos_ref[2] + q, 2)
    return sig_ref[row, at], sig_ref[row, at + 1], zz


DIMS = (((1,), (1,)), ((), ()))


def score_first_kernel(sig_ref, pos_ref, *refs):
    messages, (re_ref, im_ref, acc_ref, sel) = refs[:Z], refs[Z:]

    @pl.loop(0, 2)
    def _(q):
        for o in range(RUNS):
            dz, dx = o // X, o % X
            _, second, _ = run_entry(sig_ref, pos_ref, q, dz, dx)
            sel[o] = messages[dz][second, :, dx * SPLIT : (dx + 1) * SPLIT]
        acc_ref[q] = lax.dot_general(
            re_ref[q].reshape(ROWS, PIX),
            sel[:, :, 0:PIX].reshape(COLS, PIX),
            DIMS,
            preferred_element_type=jnp.float32,
        )
        acc_ref[q] += lax.dot_general(
            im_ref[q, :, :, 0:BORDER].reshape(ROWS, BORDER),
            sel[:, :, PIX:].reshape(COLS, BORDER),
            DIMS,
            preferred_element_type=jnp.float32,
        )


def score_first(sig, pos, messages, shifted):
    return pl.pallas_call(
        score_first_kernel,
        in_specs=[SMEM, SMEM] + [VMEM] * (Z + 2),
        out_specs=VMEM,
        out_shape=pltpu.VMEM((2, ROWS, COLS), jnp.float32),
        scratch_shapes=[pltpu.VMEM((RUNS, 8, SPLIT), jnp.bfloat16)],
        compiler_params=limit(8),
        cost_estimate=pl.CostEstimate(
            flops=4 * ROWS * COLS * SPLIT, bytes_accessed=16 * 1024 * 1024, transcendentals=0
        ),
        name="score_first",
    )(sig, pos, *[in_vmem(v) for v in messages], *[in_vmem(v) for v in shifted])


def score_rest_kernel(sig_ref, pos_ref, *refs):
    messages, batches = refs[:Z], refs[Z : Z + 6]
    im_ref, acc = refs[Z + 6 : Z + 8]
    st_ref, stat_ref, sel, work, mask = refs[Z + 8 :]

    def unit(dz, dx, second, at):
        if dx == 0:
            return messages[dz][second, :, X * SPLIT + at.start : X * SPLIT + at.stop]
        early = dz in EARLY
        place = (EARLY if early else LATE).index(dz)
        return batches[dx - 1 if early else dx + 2][place, second, :, at]

    stat_ref[...] = jnp.zeros_like(stat_ref)
    largest = jnp.zeros((8, EXTRA), jnp.float32)
    for o in range(RUNS):
        top = unit(o // X, o % X, 0, slice(REST, UNIT))
        largest = jnp.maximum(largest, top.astype(jnp.float32))
    stat_ref[4:5, 0:EXTRA] = jnp.max(largest, axis=0, keepdims=True)

    @pl.loop(0, 2)
    def _(q):
        for o in range(RUNS):
            first, second, _ = run_entry(sig_ref, pos_ref, q, o // X, o % X)
            sel[o] = unit(o // X, o % X, second, slice(0, REST))
            live = (first + second).astype(jnp.float32)
            mask[o * 8 : o * 8 + 8, :] = jnp.full((8, 128), live, jnp.float32)
        work[...] = acc[q] + lax.dot_general(
            im_ref[q, :, :, BORDER:].reshape(ROWS, REST),
            sel[...].reshape(COLS, REST),
            DIMS,
            preferred_element_type=jnp.float32,
        )
        live = mask[:, 0:1] > 0.5
        top = jnp.full((1, N), NEGATIVE, jnp.float32)
        for t in range(SHIFTS):
            s = work[t * N : (t + 1) * N, :].T * SCALE
            s = jnp.where(live, s, NEGATIVE)
            st_ref[q, :, t * N : (t + 1) * N] = s
            top = jnp.maximum(top, jnp.max(s, axis=0, keepdims=True))
        total = jnp.zeros((1, N), jnp.float32)
        for t in range(SHIFTS):
            s = st_ref[q, :, t * N : (t + 1) * N]
            e = jnp.where(live, jnp.exp(s - top), 0.0)
            total = total + jnp.sum(e, axis=0, keepdims=True)
        stat_ref[pl.ds(q, 1), :] = top
        stat_ref[pl.ds(2 + q, 1), :] = total


def score_rest(sig, pos, messages, batches, shifted, acc):
    return pl.pallas_call(
        score_rest_kernel,
        in_specs=[SMEM, SMEM] + [VMEM] * (Z + 8),
        out_specs=[VMEM, VMEM],
        out_shape=[
            pltpu.VMEM((2, COLS, ROWS), jnp.float32),
            pltpu.VMEM((8, N), jnp.float32),
        ],
        scratch_shapes=[
            pltpu.VMEM((RUNS, 8, REST), jnp.bfloat16),
            pltpu.VMEM((ROWS, COLS), jnp.float32),
            pltpu.VMEM((COLS, 128), jnp.float32),
        ],
        compiler_params=limit(8),
        cost_estimate=pl.CostEstimate(
            flops=4 * ROWS * COLS * REST, bytes_accessed=16 * 1024 * 1024, transcendentals=2 * ROWS * COLS
        ),
        name="score_rest",
    )(
        sig,
        pos,
        *[in_vmem(v) for v in (*messages, *batches, shifted[1], acc)],
    )


def merge_kernel(stat_ref, other_ref, out_ref):
    out_ref[...] = jnp.zeros_like(out_ref)
    for q in range(2):
        a, b = stat_ref[q : q + 1, :], other_ref[1 - q : 2 - q, :]
        top = jnp.maximum(a, b)
        out_ref[q : q + 1, :] = top
        out_ref[2 + q : 3 + q, :] = stat_ref[2 + q : 3 + q, :] * jnp.exp(a - top) + other_ref[
            3 - q : 4 - q, :
        ] * jnp.exp(b - top)
    bound = jnp.max(jnp.maximum(stat_ref[4:5, :], other_ref[4:5, :]), axis=1, keepdims=True)
    out_ref[4:5, :] = jnp.broadcast_to(jnp.maximum(bound, 1e-30), (1, N))


def merge(stats, other):
    return pl.pallas_call(
        merge_kernel,
        in_specs=[VMEM, VMEM],
        out_specs=VMEM,
        out_shape=pltpu.VMEM((8, N), jnp.float32),
        compiler_params=limit(2),
        name="merge",
    )(in_vmem(stats), in_vmem(other))


def partial_kernel(z_first, sig_ref, pos_ref, *refs):
    if z_first:
        w_ref, bound_ref, image_ref, out_ref = refs
        bound = bound_ref[4:5, 0:1]
    else:
        st_ref, *every = refs[:5]
        image_ref, out_ref, w_ref, ev_ref = refs[5:]
        for q in range(2):
            tops = [r[q : q + 1, :] for r in every]
            top = jnp.maximum(jnp.maximum(tops[0], tops[1]), jnp.maximum(tops[2], tops[3]))
            total = sum(r[2 + q : 3 + q, :] * jnp.exp(t - top) for r, t in zip(every, tops))
            evidence = top + jnp.log(total)
            if q == 0:
                ev_ref[...] = evidence
            for t in range(SHIFTS):
                s = st_ref[q, :, t * N : (t + 1) * N]
                w_ref[q, :, t * N : (t + 1) * N] = jnp.exp(s - evidence).astype(jnp.bfloat16)
        bound = every[0][4:5, 0:1]
    scale = HEADROOM / bound
    entries = [
        [run_entry(sig_ref, pos_ref, q, dz, dx) for dz in range(Z) for dx in range(X)]
        for q in range(2)
    ]

    @pl.loop(0, PIX // PTILE)
    def _(i):
        at = pl.ds(pl.multiple_of(i * PTILE, PTILE), PTILE)
        for q in range(2):
            value = (
                jnp.dot(
                    w_ref[q],
                    image_ref[q, :, :, at].reshape(ROWS, PTILE),
                    preferred_element_type=jnp.float32,
                )
                * scale
            )
            for o in range(RUNS):
                _, second, zz = entries[q][o]
                base = (o if z_first else (o % X) * Z + zz) * 16
                rows = pl.ds(pl.multiple_of(base + second * 8, 8), 8)
                block = value[o * 8 : o * 8 + 8, :]
                if q == 0:
                    other = pl.ds(pl.multiple_of(base + (1 - second) * 8, 8), 8)
                    out_ref[rows, at] = block
                    out_ref[other, at] = jnp.zeros_like(block)
                else:
                    out_ref[rows, at] += block


def partial_sums(z_first, sig, pos, weights, images):
    out_shape = [pltpu.VMEM((2 * COLS, PIX), jnp.float32)]
    if not z_first:
        out_shape.append(pltpu.VMEM((2, COLS, ROWS), jnp.bfloat16))
        out_shape.append(jax.ShapeDtypeStruct((1, N), jnp.float32))
    return pl.pallas_call(
        lambda *refs: partial_kernel(z_first, *refs),
        in_specs=[SMEM, SMEM] + [VMEM] * (len(weights) + 1),
        out_specs=[VMEM] * len(out_shape),
        out_shape=out_shape,
        compiler_params=limit(4),
        cost_estimate=pl.CostEstimate(
            flops=2 * ROWS * COLS * FEATURES, bytes_accessed=16 * 1024 * 1024, transcendentals=0
        ),
        name="partial_re" if z_first else "partial_im",
    )(sig, pos, *[in_vmem(v) for v in weights], in_vmem(images))


HIGH, LOW = 32, 128


def insert_kernel(bound_ref, w_ref, ins_ref, *refs):
    scale = bound_ref[4:5, 0:1] * (1.0 / HEADROOM)
    high_ids = lax.broadcasted_iota(jnp.int32, (HIGH, PIX), 0)
    low_ids = lax.broadcasted_iota(jnp.int32, (LOW, PIX), 0)

    def step(i, acc):
        row = pl.ds(i, 1)
        ids = ins_ref[row, :]
        high = lax.shift_right_logical(ids, 7)
        low = lax.bitwise_and(ids, LOW - 1)
        value = w_ref[row, :] * scale
        head = value.astype(jnp.bfloat16).astype(jnp.float32)
        tail = value - head
        here = high == high_ids
        rows = jnp.concatenate(
            [jnp.where(here, head, 0.0), jnp.where(here, tail, 0.0)], axis=0
        ).astype(jnp.bfloat16)
        table = jnp.where(low == low_ids, 1.0, 0.0).astype(jnp.bfloat16)
        return acc + lax.dot_general(rows, table, DIMS, preferred_element_type=jnp.float32)

    empty = jnp.zeros((2 * HIGH, LOW), jnp.float32)
    acc = lax.fori_loop(0, 16, step, empty, unroll=1 if len(refs) == 1 else 4)
    slab = acc[:HIGH] + acc[HIGH:]
    if len(refs) == 1:
        refs[0][...] = slab
    else:
        im_ref, out_ref = refs
        for h in range(HIGH):
            at = slice(h * LOW, (h + 1) * LOW)
            out_ref[0:1, at] = slab[h : h + 1, :]
            out_ref[1:2, at] = im_ref[h : h + 1, :]


def insert(bound, weighted, insertion, *im):
    shape = (2, VOX) if im else (HIGH, LOW)
    return pl.pallas_call(
        insert_kernel,
        in_specs=[VMEM] * (3 + len(im)),
        out_specs=VMEM,
        out_shape=jax.ShapeDtypeStruct(shape, jnp.float32),
        compiler_params=limit(8),
        cost_estimate=pl.CostEstimate(
            flops=4 * HIGH * LOW * 16 * PIX, bytes_accessed=512 * 1024, transcendentals=0
        ),
        name="insert_re" if im else "insert_im",
    )(bound, weighted.reshape(16, PIX), insertion, *im)


def img_index(z, x, c):
    return (z * X + x) * CORES + c


def pairs(dz, dx, dc=0):
    return [
        (img_index(z, x, c), img_index((z + dz) % Z, (x + dx) % X, (c + dc) % CORES))
        for z in range(Z)
        for x in range(X)
        for c in range(CORES)
    ]


Z_GROUPS = [[img_index(z, x, c) for z in range(Z)] for x in range(X) for c in range(CORES)]


def send(value, dz=0, dx=0, dc=0):
    return lax.ppermute(value, "img", pairs(dz, dx, dc))


def all_to_all_z(value):
    return lax.all_to_all(
        value, "img", split_axis=0, concat_axis=0, tiled=True, axis_index_groups=Z_GROUPS
    )


def gather(projections, unit):
    mine = projections[:, :, :SPLIT]
    row = [mine, send(mine, dx=-1), send(mine, dx=-2), send(mine, dx=1)]
    ahead = behind = assemble(row, unit)
    messages = {0: ahead}
    for k in range(1, Z // 2 + 1):
        behind = send(behind, dz=1)
        messages[Z - k] = behind
        if k < Z // 2:
            ahead = send(ahead, dz=-1)
            messages[k] = ahead
    batches = []
    for places in (EARLY, LATE):
        column = pick([messages[k] for k in places])
        for dx in (-1, -2, 1):
            batches.append(send(column, dx=dx))
    return [messages[k] for k in range(Z)], batches


def wide(value):
    return value.astype(jnp.float32)


def narrow(value):
    return value.astype(jnp.float16)


def scatter_z_first(parts):
    half = Z // 2
    behind = narrow(parts[half])
    for k in range(half, 0, -1):
        if k < half:
            behind = narrow(parts[k] + wide(behind))
        behind = send(behind, dz=1)
    ahead = narrow(parts[half + 1])
    for k in range(half - 1, 0, -1):
        if k < half - 1:
            ahead = narrow(parts[Z - k] + wide(ahead))
        ahead = send(ahead, dz=-1)
    row = parts[0] + wide(behind) + wide(ahead)
    arrived = [send(narrow(row[k]), dx=k) for k in range(1, X)]
    return row[0] + wide(arrived[0]) + wide(arrived[1]) + wide(arrived[2])


def scatter_x_first(parts):
    arrived = [send(narrow(parts[k]), dx=k) for k in range(1, X)]
    column = parts[0] + wide(arrived[0]) + wide(arrived[1]) + wide(arrived[2])
    return jnp.sum(wide(all_to_all_z(narrow(column))), axis=0)


def exchange_refs(value):
    out = [value]
    for k in range(1, REFS):
        out.append(lax.ppermute(value, "ref", [(r, (r + k) % REFS) for r in range(REFS)]))
    return out


def one_device(particles, projections, significance, insertion):
    img = lax.axis_index("img")
    ref = lax.axis_index("ref")
    z, x, core = img >> 3, (img >> 1) & 3, img & 1
    pos = jnp.stack([z, x, core, ref]).astype(jnp.int32)
    sig = lax.dynamic_slice_in_dim(significance, img - core, 2, axis=0)
    table = jnp.asarray(shift_tables())

    mate = send(particles, dc=1)
    unit = prepare(particles, projections)
    unit, pos, sig = lax.optimization_barrier((unit, pos, sig))
    messages, batches = gather(projections, unit)
    shifted = shifted_images(table, particles, mate)

    acc = score_first(sig, pos, messages, shifted)
    scores, stats = score_rest(sig, pos, messages, batches, shifted, acc)
    merged = merge(stats, send(stats, dc=1))
    every = exchange_refs(merged)
    sums_im, weights, evidence = partial_sums(False, sig, pos, (scores, *every), shifted[1])
    (sums_re,) = partial_sums(True, sig, pos, (weights, merged), shifted[0])
    total_im = scatter_x_first(sums_im.reshape(X, Z, 2, 8, PIX))
    total_re = scatter_z_first(sums_re.reshape(Z, X, 2, 8, PIX))
    ids = insertion.reshape(16, PIX)
    slab = insert(merged, total_im, ids)
    volume = insert(merged, total_re, ids, slab)
    return volume, evidence.reshape(N)


def solution(mesh):
    in_specs = (P("img", None), P(("img", "ref"), None, None), P(), P(("img", "ref"), None, None))
    out_specs = (P(None, ("img", "ref")), P("img"))
    return jax.shard_map(
        one_device, mesh=mesh, in_specs=in_specs, out_specs=out_specs, check_vma=False
    )
```

```python
import math

import jax
import jax.numpy as jnp
import numpy as np
from jax import lax
from jax.experimental import pallas as pl
from jax.experimental.pallas import tpu as pltpu
from jax.sharding import PartitionSpec as P

SIDE = 64
PIX = 2048
FEATURES = 2 * PIX
VOX = 4096
Z, X, CORES, REFS = 8, 4, 2, 4
RUNS = Z * X
COLS = RUNS * 8
N = 256
SHIFTS = 5
ROWS = SHIFTS * N
NEGATIVE = -1e30
SCALE = 2.0 / math.sqrt(FEATURES)
HEADROOM = 2.5
EXTRA = 128
SPLIT = 2304
REST = FEATURES - SPLIT
BORDER = SPLIT - PIX
UNIT = REST + EXTRA
MESSAGE = X * SPLIT + UNIT
EARLY = (0, 1, 2, 6, 7)
LATE = (3, 4, 5)


def shift_tables():
    p = np.arange(PIX)
    unit = np.float32(2.0 * math.pi / SIDE)
    ax = (unit * (p % SIDE - SIDE // 2).astype(np.float32)).astype(np.float64)
    ay = (unit * (p // SIDE).astype(np.float32)).astype(np.float64)
    rows = [np.cos(ax), np.sin(ax), np.cos(ay), np.sin(ay)]
    return np.stack(rows + rows).astype(np.float32)


VMEM = pl.BlockSpec(memory_space=pltpu.VMEM)
SMEM = pl.BlockSpec(memory_space=pltpu.SMEM)
LANES = 512
PTILE = 512


def in_vmem(value):
    return pltpu.with_memory_space_constraint(value, pltpu.VMEM)


def limit(mib):
    return pltpu.CompilerParams(vmem_limit_bytes=mib * 1024 * 1024)


def prepare_kernel(image_ref, proj_ref, out_ref):
    top = jnp.zeros((16, FEATURES), jnp.bfloat16)
    for i in range(N // 16):
        top = jnp.maximum(top, jnp.abs(image_ref[i * 16 : i * 16 + 16, :]))
    largest = jnp.max(top.astype(jnp.float32), axis=0, keepdims=True)
    largest = jnp.max(largest, axis=1, keepdims=True)
    out_ref[:, :, 0:REST] = proj_ref[:, :, SPLIT:]
    for b in range(2):
        out_ref[b, :, REST:] = jnp.broadcast_to(largest, (8, EXTRA)).astype(jnp.bfloat16)


def prepare(images, projections):
    return pl.pallas_call(
        prepare_kernel,
        in_specs=[VMEM, VMEM],
        out_specs=VMEM,
        out_shape=pltpu.VMEM((2, 8, UNIT), jnp.bfloat16),
        compiler_params=limit(2),
        name="prepare",
    )(in_vmem(images), in_vmem(projections))


def assemble_kernel(*refs):
    *parts, out_ref = refs
    for k, part in enumerate(parts):
        out_ref[:, :, k * SPLIT : k * SPLIT + part.shape[2]] = part[...]


def assemble(row, unit):
    return pl.pallas_call(
        assemble_kernel,
        in_specs=[VMEM] * (X + 1),
        out_specs=VMEM,
        out_shape=pltpu.VMEM((2, 8, MESSAGE), jnp.bfloat16),
        compiler_params=limit(2),
        name="assemble",
    )(*[in_vmem(v) for v in (*row, unit)])


def pick_kernel(*refs):
    *messages, out_ref = refs
    for k, message in enumerate(messages):
        out_ref[k] = message[:, :, X * SPLIT :]


def pick(messages):
    return pl.pallas_call(
        pick_kernel,
        in_specs=[VMEM] * len(messages),
        out_specs=VMEM,
        out_shape=pltpu.VMEM((len(messages), 2, 8, UNIT), jnp.bfloat16),
        compiler_params=limit(2),
        name="pick",
    )(*[in_vmem(v) for v in messages])


def shift_kernel(table_ref, own_ref, mate_ref, out_re, out_im):
    for q, image_ref in enumerate((own_ref, mate_ref)):
        for j in range(PIX // LANES):
            at = slice(j * LANES, (j + 1) * LANES)
            at_im = slice(PIX + j * LANES, PIX + (j + 1) * LANES)
            tables = [table_ref[k : k + 1, at] for k in range(4)]

            @pl.loop(0, N // 16)
            def _(i):
                rows = pl.ds(pl.multiple_of(i * 16, 16), 16)
                re_in, im_in = image_ref[rows, at], image_ref[rows, at_im]
                out_re[q, 0, rows, at] = re_in
                out_im[q, 0, rows, at] = im_in
                re, im = re_in.astype(jnp.float32), im_in.astype(jnp.float32)
                for k in range(2):
                    c, s = tables[2 * k], tables[2 * k + 1]
                    rc, rs, ic, is_ = re * c, re * s, im * c, im * s
                    out_re[q, 1 + 2 * k, rows, at] = (rc - is_).astype(jnp.bfloat16)
                    out_im[q, 1 + 2 * k, rows, at] = (rs + ic).astype(jnp.bfloat16)
                    out_re[q, 2 + 2 * k, rows, at] = (rc + is_).astype(jnp.bfloat16)
                    out_im[q, 2 + 2 * k, rows, at] = (ic - rs).astype(jnp.bfloat16)


def shifted_images(table, own, mate):
    shape = pltpu.VMEM((2, SHIFTS, N, PIX), jnp.bfloat16)
    return pl.pallas_call(
        shift_kernel,
        in_specs=[VMEM] * 3,
        out_specs=[VMEM, VMEM],
        out_shape=[shape, shape],
        compiler_params=limit(4),
        cost_estimate=pl.CostEstimate(
            flops=48 * N * PIX, bytes_accessed=24 * 1024 * 1024, transcendentals=0
        ),
        name="shift",
    )(in_vmem(table), in_vmem(own), in_vmem(mate))


def run_entry(sig_ref, pos_ref, q, dz, dx):
    zz = lax.rem(pos_ref[0] + dz, Z)
    xx = lax.rem(pos_ref[1] + dx, X)
    at = (((zz * X + xx) * CORES + pos_ref[2]) * REFS + pos_ref[3]) * 2
    row = lax.rem(pos_ref[2] + q, 2)
    return sig_ref[row, at], sig_ref[row, at + 1], zz


DIMS = (((1,), (1,)), ((), ()))


def score_first_kernel(sig_ref, pos_ref, *refs):
    messages, (re_ref, im_ref, acc_ref, sel) = refs[:Z], refs[Z:]

    @pl.loop(0, 2)
    def _(q):
        for o in range(RUNS):
            dz, dx = o // X, o % X
            _, second, _ = run_entry(sig_ref, pos_ref, q, dz, dx)
            sel[o] = messages[dz][second, :, dx * SPLIT : (dx + 1) * SPLIT]
        acc_ref[q] = lax.dot_general(
            re_ref[q].reshape(ROWS, PIX),
            sel[:, :, 0:PIX].reshape(COLS, PIX),
            DIMS,
            preferred_element_type=jnp.float32,
        )
        acc_ref[q] += lax.dot_general(
            im_ref[q, :, :, 0:BORDER].reshape(ROWS, BORDER),
            sel[:, :, PIX:].reshape(COLS, BORDER),
            DIMS,
            preferred_element_type=jnp.float32,
        )


def score_first(sig, pos, messages, shifted):
    return pl.pallas_call(
        score_first_kernel,
        in_specs=[SMEM, SMEM] + [VMEM] * (Z + 2),
        out_specs=VMEM,
        out_shape=pltpu.VMEM((2, ROWS, COLS), jnp.float32),
        scratch_shapes=[pltpu.VMEM((RUNS, 8, SPLIT), jnp.bfloat16)],
        compiler_params=limit(8),
        cost_estimate=pl.CostEstimate(
            flops=4 * ROWS * COLS * SPLIT, bytes_accessed=16 * 1024 * 1024, transcendentals=0
        ),
        name="score_first",
    )(sig, pos, *[in_vmem(v) for v in messages], *[in_vmem(v) for v in shifted])


def score_rest_kernel(sig_ref, pos_ref, *refs):
    messages, batches = refs[:Z], refs[Z : Z + 6]
    im_ref, acc = refs[Z + 6 : Z + 8]
    st_ref, stat_ref, sel, work, mask = refs[Z + 8 :]

    def unit(dz, dx, second, at):
        if dx == 0:
            return messages[dz][second, :, X * SPLIT + at.start : X * SPLIT + at.stop]
        early = dz in EARLY
        place = (EARLY if early else LATE).index(dz)
        return batches[dx - 1 if early else dx + 2][place, second, :, at]

    stat_ref[...] = jnp.zeros_like(stat_ref)
    largest = jnp.zeros((8, EXTRA), jnp.float32)
    for o in range(RUNS):
        top = unit(o // X, o % X, 0, slice(REST, UNIT))
        largest = jnp.maximum(largest, top.astype(jnp.float32))
    stat_ref[4:5, 0:EXTRA] = jnp.max(largest, axis=0, keepdims=True)

    @pl.loop(0, 2)
    def _(q):
        for o in range(RUNS):
            first, second, _ = run_entry(sig_ref, pos_ref, q, o // X, o % X)
            sel[o] = unit(o // X, o % X, second, slice(0, REST))
            live = (first + second).astype(jnp.float32)
            mask[o * 8 : o * 8 + 8, :] = jnp.full((8, 128), live, jnp.float32)
        work[...] = acc[q] + lax.dot_general(
            im_ref[q, :, :, BORDER:].reshape(ROWS, REST),
            sel[...].reshape(COLS, REST),
            DIMS,
            preferred_element_type=jnp.float32,
        )
        live = mask[:, 0:1] > 0.5
        top = jnp.full((1, N), NEGATIVE, jnp.float32)
        for t in range(SHIFTS):
            s = work[t * N : (t + 1) * N, :].T * SCALE
            s = jnp.where(live, s, NEGATIVE)
            st_ref[q, :, t * N : (t + 1) * N] = s
            top = jnp.maximum(top, jnp.max(s, axis=0, keepdims=True))
        total = jnp.zeros((1, N), jnp.float32)
        for t in range(SHIFTS):
            s = st_ref[q, :, t * N : (t + 1) * N]
            e = jnp.where(live, jnp.exp(s - top), 0.0)
            total = total + jnp.sum(e, axis=0, keepdims=True)
        stat_ref[pl.ds(q, 1), :] = top
        stat_ref[pl.ds(2 + q, 1), :] = total


def score_rest(sig, pos, messages, batches, shifted, acc):
    return pl.pallas_call(
        score_rest_kernel,
        in_specs=[SMEM, SMEM] + [VMEM] * (Z + 8),
        out_specs=[VMEM, VMEM],
        out_shape=[
            pltpu.VMEM((2, COLS, ROWS), jnp.float32),
            pltpu.VMEM((8, N), jnp.float32),
        ],
        scratch_shapes=[
            pltpu.VMEM((RUNS, 8, REST), jnp.bfloat16),
            pltpu.VMEM((ROWS, COLS), jnp.float32),
            pltpu.VMEM((COLS, 128), jnp.float32),
        ],
        compiler_params=limit(8),
        cost_estimate=pl.CostEstimate(
            flops=4 * ROWS * COLS * REST, bytes_accessed=16 * 1024 * 1024, transcendentals=2 * ROWS * COLS
        ),
        name="score_rest",
    )(
        sig,
        pos,
        *[in_vmem(v) for v in (*messages, *batches, shifted[1], acc)],
    )


def merge_kernel(stat_ref, other_ref, out_ref):
    out_ref[...] = jnp.zeros_like(out_ref)
    for q in range(2):
        a, b = stat_ref[q : q + 1, :], other_ref[1 - q : 2 - q, :]
        top = jnp.maximum(a, b)
        out_ref[q : q + 1, :] = top
        out_ref[2 + q : 3 + q, :] = stat_ref[2 + q : 3 + q, :] * jnp.exp(a - top) + other_ref[
            3 - q : 4 - q, :
        ] * jnp.exp(b - top)
    bound = jnp.max(jnp.maximum(stat_ref[4:5, :], other_ref[4:5, :]), axis=1, keepdims=True)
    out_ref[4:5, :] = jnp.broadcast_to(jnp.maximum(bound, 1e-30), (1, N))


def merge(stats, other):
    return pl.pallas_call(
        merge_kernel,
        in_specs=[VMEM, VMEM],
        out_specs=VMEM,
        out_shape=pltpu.VMEM((8, N), jnp.float32),
        compiler_params=limit(2),
        name="merge",
    )(in_vmem(stats), in_vmem(other))


def partial_kernel(z_first, sig_ref, pos_ref, *refs):
    if z_first:
        w_ref, bound_ref, image_ref, out_ref = refs
        bound = bound_ref[4:5, 0:1]
    else:
        st_ref, *every = refs[:5]
        image_ref, out_ref, w_ref, ev_ref = refs[5:]
        for q in range(2):
            tops = [r[q : q + 1, :] for r in every]
            top = jnp.maximum(jnp.maximum(tops[0], tops[1]), jnp.maximum(tops[2], tops[3]))
            total = sum(r[2 + q : 3 + q, :] * jnp.exp(t - top) for r, t in zip(every, tops))
            evidence = top + jnp.log(total)
            if q == 0:
                ev_ref[...] = evidence
            for t in range(SHIFTS):
                s = st_ref[q, :, t * N : (t + 1) * N]
                w_ref[q, :, t * N : (t + 1) * N] = jnp.exp(s - evidence).astype(jnp.bfloat16)
        bound = every[0][4:5, 0:1]
    scale = HEADROOM / bound
    entries = [
        [run_entry(sig_ref, pos_ref, q, dz, dx) for dz in range(Z) for dx in range(X)]
        for q in range(2)
    ]

    @pl.loop(0, PIX // PTILE)
    def _(i):
        at = pl.ds(pl.multiple_of(i * PTILE, PTILE), PTILE)
        for q in range(2):
            value = (
                jnp.dot(
                    w_ref[q],
                    image_ref[q, :, :, at].reshape(ROWS, PTILE),
                    preferred_element_type=jnp.float32,
                )
                * scale
            )
            for o in range(RUNS):
                _, second, zz = entries[q][o]
                base = (o if z_first else (o % X) * Z + zz) * 16
                rows = pl.ds(pl.multiple_of(base + second * 8, 8), 8)
                block = value[o * 8 : o * 8 + 8, :]
                if q == 0:
                    other = pl.ds(pl.multiple_of(base + (1 - second) * 8, 8), 8)
                    out_ref[rows, at] = block
                    out_ref[other, at] = jnp.zeros_like(block)
                else:
                    out_ref[rows, at] += block


def partial_sums(z_first, sig, pos, weights, images):
    out_shape = [pltpu.VMEM((2 * COLS, PIX), jnp.float32)]
    if not z_first:
        out_shape.append(pltpu.VMEM((2, COLS, ROWS), jnp.bfloat16))
        out_shape.append(jax.ShapeDtypeStruct((1, N), jnp.float32))
    return pl.pallas_call(
        lambda *refs: partial_kernel(z_first, *refs),
        in_specs=[SMEM, SMEM] + [VMEM] * (len(weights) + 1),
        out_specs=[VMEM] * len(out_shape),
        out_shape=out_shape,
        compiler_params=limit(4),
        cost_estimate=pl.CostEstimate(
            flops=2 * ROWS * COLS * FEATURES, bytes_accessed=16 * 1024 * 1024, transcendentals=0
        ),
        name="partial_re" if z_first else "partial_im",
    )(sig, pos, *[in_vmem(v) for v in weights], in_vmem(images))


HIGH, LOW = 32, 128


def insert_kernel(bound_ref, w_ref, ins_ref, *refs):
    scale = bound_ref[4:5, 0:1] * (1.0 / HEADROOM)
    high_ids = lax.broadcasted_iota(jnp.int32, (HIGH, PIX), 0)
    low_ids = lax.broadcasted_iota(jnp.int32, (LOW, PIX), 0)

    def step(i, acc):
        row = pl.ds(i, 1)
        ids = ins_ref[row, :]
        high = lax.shift_right_logical(ids, 7)
        low = lax.bitwise_and(ids, LOW - 1)
        value = w_ref[row, :] * scale
        head = value.astype(jnp.bfloat16).astype(jnp.float32)
        tail = value - head
        here = high == high_ids
        rows = jnp.concatenate(
            [jnp.where(here, head, 0.0), jnp.where(here, tail, 0.0)], axis=0
        ).astype(jnp.bfloat16)
        table = jnp.where(low == low_ids, 1.0, 0.0).astype(jnp.bfloat16)
        return acc + lax.dot_general(rows, table, DIMS, preferred_element_type=jnp.float32)

    empty = jnp.zeros((2 * HIGH, LOW), jnp.float32)
    acc = lax.fori_loop(0, 16, step, empty, unroll=1 if len(refs) == 1 else 4)
    slab = acc[:HIGH] + acc[HIGH:]
    if len(refs) == 1:
        refs[0][...] = slab
    else:
        im_ref, out_ref = refs
        for h in range(HIGH):
            at = slice(h * LOW, (h + 1) * LOW)
            out_ref[0:1, at] = slab[h : h + 1, :]
            out_ref[1:2, at] = im_ref[h : h + 1, :]


def insert(bound, weighted, insertion, *im):
    shape = (2, VOX) if im else (HIGH, LOW)
    return pl.pallas_call(
        insert_kernel,
        in_specs=[VMEM] * (3 + len(im)),
        out_specs=VMEM,
        out_shape=jax.ShapeDtypeStruct(shape, jnp.float32),
        compiler_params=limit(8),
        cost_estimate=pl.CostEstimate(
            flops=4 * HIGH * LOW * 16 * PIX, bytes_accessed=512 * 1024, transcendentals=0
        ),
        name="insert_re" if im else "insert_im",
    )(bound, weighted.reshape(16, PIX), insertion, *im)


def img_index(z, x, c):
    return (z * X + x) * CORES + c


def pairs(dz, dx, dc=0):
    return [
        (img_index(z, x, c), img_index((z + dz) % Z, (x + dx) % X, (c + dc) % CORES))
        for z in range(Z)
        for x in range(X)
        for c in range(CORES)
    ]


Z_GROUPS = [[img_index(z, x, c) for z in range(Z)] for x in range(X) for c in range(CORES)]


def send(value, dz=0, dx=0, dc=0):
    return lax.ppermute(value, "img", pairs(dz, dx, dc))


def all_to_all_z(value):
    return lax.all_to_all(
        value, "img", split_axis=0, concat_axis=0, tiled=True, axis_index_groups=Z_GROUPS
    )


def gather(projections, unit):
    mine = projections[:, :, :SPLIT]
    row = [mine, send(mine, dx=-1), send(mine, dx=-2), send(mine, dx=1)]
    ahead = behind = assemble(row, unit)
    messages = {0: ahead}
    for k in range(1, Z // 2 + 1):
        behind = send(behind, dz=1)
        messages[Z - k] = behind
        if k < Z // 2:
            ahead = send(ahead, dz=-1)
            messages[k] = ahead
    batches = []
    for places in (EARLY, LATE):
        column = pick([messages[k] for k in places])
        for dx in (-1, -2, 1):
            batches.append(send(column, dx=dx))
    return [messages[k] for k in range(Z)], batches


def wide(value):
    return value.astype(jnp.float32)


def narrow(value):
    return value.astype(jnp.float16)


def scatter_z_first(parts):
    half = Z // 2
    behind = narrow(parts[half])
    for k in range(half, 0, -1):
        if k < half:
            behind = narrow(parts[k] + wide(behind))
        behind = send(behind, dz=1)
    ahead = narrow(parts[half + 1])
    for k in range(half - 1, 0, -1):
        if k < half - 1:
            ahead = narrow(parts[Z - k] + wide(ahead))
        ahead = send(ahead, dz=-1)
    row = parts[0] + wide(behind) + wide(ahead)
    arrived = [send(narrow(row[k]), dx=k) for k in range(1, X)]
    return row[0] + wide(arrived[0]) + wide(arrived[1]) + wide(arrived[2])


def scatter_x_first(parts):
    arrived = [send(narrow(parts[k]), dx=k) for k in range(1, X)]
    column = narrow(parts[0] + wide(arrived[0]) + wide(arrived[1]) + wide(arrived[2]))
    return jnp.sum(wide(all_to_all_z(column)), axis=0)


def exchange_refs(value):
    out = [value]
    for k in range(1, REFS):
        out.append(lax.ppermute(value, "ref", [(r, (r + k) % REFS) for r in range(REFS)]))
    return out


def one_device(particles, projections, significance, insertion):
    img = lax.axis_index("img")
    ref = lax.axis_index("ref")
    z, x, core = img >> 3, (img >> 1) & 3, img & 1
    pos = jnp.stack([z, x, core, ref]).astype(jnp.int32)
    sig = lax.dynamic_slice_in_dim(significance, img - core, 2, axis=0)
    table = jnp.asarray(shift_tables())

    mate = send(particles, dc=1)
    unit = prepare(particles, projections)
    unit, pos, sig = lax.optimization_barrier((unit, pos, sig))
    messages, batches = gather(projections, unit)
    shifted = shifted_images(table, particles, mate)

    acc = score_first(sig, pos, messages, shifted)
    scores, stats = score_rest(sig, pos, messages, batches, shifted, acc)
    merged = merge(stats, send(stats, dc=1))
    every = exchange_refs(merged)
    sums_im, weights, evidence = partial_sums(False, sig, pos, (scores, *every), shifted[1])
    (sums_re,) = partial_sums(True, sig, pos, (weights, merged), shifted[0])
    total_im = scatter_x_first(sums_im.reshape(X, Z, 2, 8, PIX))
    total_re = scatter_z_first(sums_re.reshape(Z, X, 2, 8, PIX))
    ids = insertion.reshape(16, PIX)
    slab = insert(merged, total_im, ids)
    volume = insert(merged, total_re, ids, slab)
    return volume, evidence.reshape(N)


def solution(mesh):
    in_specs = (P("img", None), P(("img", "ref"), None, None), P(), P(("img", "ref"), None, None))
    out_specs = (P(None, ("img", "ref")), P("img"))
    return jax.shard_map(
        one_device, mesh=mesh, in_specs=in_specs, out_specs=out_specs, check_vma=False
    )
```

```python
import math

import jax
import jax.numpy as jnp
import numpy as np
from jax import lax
from jax.experimental import pallas as pl
from jax.experimental.pallas import tpu as pltpu
from jax.sharding import PartitionSpec as P

SIDE = 64
PIX = 2048
FEATURES = 2 * PIX
VOX = 4096
Z, X, CORES, REFS = 8, 4, 2, 4
RUNS = Z * X
COLS = RUNS * 8
N = 256
SHIFTS = 5
ROWS = SHIFTS * N
NEGATIVE = -1e30
SCALE = 2.0 / math.sqrt(FEATURES)
HEADROOM = 2.5
EXTRA = 128
SPLIT = 2304
REST = FEATURES - SPLIT
BORDER = SPLIT - PIX
UNIT = REST + EXTRA
MESSAGE = X * SPLIT + UNIT
EARLY = (0, 1, 2, 6, 7)
LATE = (3, 4, 5)


def shift_tables():
    p = np.arange(PIX)
    unit = np.float32(2.0 * math.pi / SIDE)
    ax = (unit * (p % SIDE - SIDE // 2).astype(np.float32)).astype(np.float64)
    ay = (unit * (p // SIDE).astype(np.float32)).astype(np.float64)
    rows = [np.cos(ax), np.sin(ax), np.cos(ay), np.sin(ay)]
    return np.stack(rows + rows).astype(np.float32)


VMEM = pl.BlockSpec(memory_space=pltpu.VMEM)
SMEM = pl.BlockSpec(memory_space=pltpu.SMEM)
LANES = 512
PTILE = 512


def in_vmem(value):
    return pltpu.with_memory_space_constraint(value, pltpu.VMEM)


def limit(mib):
    return pltpu.CompilerParams(vmem_limit_bytes=mib * 1024 * 1024)


def prepare_kernel(image_ref, proj_ref, out_ref):
    top = jnp.zeros((16, FEATURES), jnp.bfloat16)
    for i in range(N // 16):
        top = jnp.maximum(top, jnp.abs(image_ref[i * 16 : i * 16 + 16, :]))
    largest = jnp.max(top.astype(jnp.float32), axis=0, keepdims=True)
    largest = jnp.max(largest, axis=1, keepdims=True)
    out_ref[:, :, 0:REST] = proj_ref[:, :, SPLIT:]
    for b in range(2):
        out_ref[b, :, REST:] = jnp.broadcast_to(largest, (8, EXTRA)).astype(jnp.bfloat16)


def prepare(images, projections):
    return pl.pallas_call(
        prepare_kernel,
        in_specs=[VMEM, VMEM],
        out_specs=VMEM,
        out_shape=pltpu.VMEM((2, 8, UNIT), jnp.bfloat16),
        compiler_params=limit(2),
        name="prepare",
    )(in_vmem(images), in_vmem(projections))


def assemble_kernel(*refs):
    *parts, out_ref = refs
    for k, part in enumerate(parts):
        out_ref[:, :, k * SPLIT : k * SPLIT + part.shape[2]] = part[...]


def assemble(row, unit):
    return pl.pallas_call(
        assemble_kernel,
        in_specs=[VMEM] * (X + 1),
        out_specs=VMEM,
        out_shape=pltpu.VMEM((2, 8, MESSAGE), jnp.bfloat16),
        compiler_params=limit(2),
        name="assemble",
    )(*[in_vmem(v) for v in (*row, unit)])


def pick_kernel(*refs):
    *messages, out_ref = refs
    for k, message in enumerate(messages):
        out_ref[k] = message[:, :, X * SPLIT :]


def pick(messages):
    return pl.pallas_call(
        pick_kernel,
        in_specs=[VMEM] * len(messages),
        out_specs=VMEM,
        out_shape=pltpu.VMEM((len(messages), 2, 8, UNIT), jnp.bfloat16),
        compiler_params=limit(2),
        name="pick",
    )(*[in_vmem(v) for v in messages])


def shift_kernel(table_ref, own_ref, mate_ref, out_re, out_im):
    for q, image_ref in enumerate((own_ref, mate_ref)):
        for j in range(PIX // LANES):
            at = slice(j * LANES, (j + 1) * LANES)
            at_im = slice(PIX + j * LANES, PIX + (j + 1) * LANES)
            tables = [table_ref[k : k + 1, at] for k in range(4)]

            @pl.loop(0, N // 16)
            def _(i):
                rows = pl.ds(pl.multiple_of(i * 16, 16), 16)
                re_in, im_in = image_ref[rows, at], image_ref[rows, at_im]
                out_re[q, 0, rows, at] = re_in
                out_im[q, 0, rows, at] = im_in
                re, im = re_in.astype(jnp.float32), im_in.astype(jnp.float32)
                for k in range(2):
                    c, s = tables[2 * k], tables[2 * k + 1]
                    rc, rs, ic, is_ = re * c, re * s, im * c, im * s
                    out_re[q, 1 + 2 * k, rows, at] = (rc - is_).astype(jnp.bfloat16)
                    out_im[q, 1 + 2 * k, rows, at] = (rs + ic).astype(jnp.bfloat16)
                    out_re[q, 2 + 2 * k, rows, at] = (rc + is_).astype(jnp.bfloat16)
                    out_im[q, 2 + 2 * k, rows, at] = (ic - rs).astype(jnp.bfloat16)


def shifted_images(table, own, mate):
    shape = pltpu.VMEM((2, SHIFTS, N, PIX), jnp.bfloat16)
    return pl.pallas_call(
        shift_kernel,
        in_specs=[VMEM] * 3,
        out_specs=[VMEM, VMEM],
        out_shape=[shape, shape],
        compiler_params=limit(4),
        cost_estimate=pl.CostEstimate(
            flops=48 * N * PIX, bytes_accessed=24 * 1024 * 1024, transcendentals=0
        ),
        name="shift",
    )(in_vmem(table), in_vmem(own), in_vmem(mate))


def run_entry(sig_ref, pos_ref, q, dz, dx):
    zz = lax.rem(pos_ref[0] + dz, Z)
    xx = lax.rem(pos_ref[1] + dx, X)
    at = (((zz * X + xx) * CORES + pos_ref[2]) * REFS + pos_ref[3]) * 2
    row = lax.rem(pos_ref[2] + q, 2)
    return sig_ref[row, at], sig_ref[row, at + 1], zz


DIMS = (((1,), (1,)), ((), ()))


def score_first_kernel(sig_ref, pos_ref, *refs):
    messages, (re_ref, im_ref, acc_ref, sel) = refs[:Z], refs[Z:]

    @pl.loop(0, 2)
    def _(q):
        for o in range(RUNS):
            dz, dx = o // X, o % X
            _, second, _ = run_entry(sig_ref, pos_ref, q, dz, dx)
            sel[o] = messages[dz][second, :, dx * SPLIT : (dx + 1) * SPLIT]
        acc_ref[q] = lax.dot_general(
            re_ref[q].reshape(ROWS, PIX),
            sel[:, :, 0:PIX].reshape(COLS, PIX),
            DIMS,
            preferred_element_type=jnp.float32,
        )
        acc_ref[q] += lax.dot_general(
            im_ref[q, :, :, 0:BORDER].reshape(ROWS, BORDER),
            sel[:, :, PIX:].reshape(COLS, BORDER),
            DIMS,
            preferred_element_type=jnp.float32,
        )


def score_first(sig, pos, messages, shifted):
    return pl.pallas_call(
        score_first_kernel,
        in_specs=[SMEM, SMEM] + [VMEM] * (Z + 2),
        out_specs=VMEM,
        out_shape=pltpu.VMEM((2, ROWS, COLS), jnp.float32),
        scratch_shapes=[pltpu.VMEM((RUNS, 8, SPLIT), jnp.bfloat16)],
        compiler_params=limit(8),
        cost_estimate=pl.CostEstimate(
            flops=4 * ROWS * COLS * SPLIT, bytes_accessed=16 * 1024 * 1024, transcendentals=0
        ),
        name="score_first",
    )(sig, pos, *[in_vmem(v) for v in messages], *[in_vmem(v) for v in shifted])


def score_rest_kernel(sig_ref, pos_ref, *refs):
    messages, batches = refs[:Z], refs[Z : Z + 6]
    im_ref, acc = refs[Z + 6 : Z + 8]
    st_ref, stat_ref, sel, work, mask = refs[Z + 8 :]

    def unit(dz, dx, second, at):
        if dx == 0:
            return messages[dz][second, :, X * SPLIT + at.start : X * SPLIT + at.stop]
        early = dz in EARLY
        place = (EARLY if early else LATE).index(dz)
        return batches[dx - 1 if early else dx + 2][place, second, :, at]

    stat_ref[...] = jnp.zeros_like(stat_ref)
    largest = jnp.zeros((8, EXTRA), jnp.float32)
    for o in range(RUNS):
        top = unit(o // X, o % X, 0, slice(REST, UNIT))
        largest = jnp.maximum(largest, top.astype(jnp.float32))
    stat_ref[4:5, 0:EXTRA] = jnp.max(largest, axis=0, keepdims=True)

    @pl.loop(0, 2)
    def _(q):
        for o in range(RUNS):
            first, second, _ = run_entry(sig_ref, pos_ref, q, o // X, o % X)
            sel[o] = unit(o // X, o % X, second, slice(0, REST))
            live = (first + second).astype(jnp.float32)
            mask[o * 8 : o * 8 + 8, :] = jnp.full((8, 128), live, jnp.float32)
        work[...] = acc[q] + lax.dot_general(
            im_ref[q, :, :, BORDER:].reshape(ROWS, REST),
            sel[...].reshape(COLS, REST),
            DIMS,
            preferred_element_type=jnp.float32,
        )
        live = mask[:, 0:1] > 0.5
        top = jnp.full((1, N), NEGATIVE, jnp.float32)
        for t in range(SHIFTS):
            s = work[t * N : (t + 1) * N, :].T * SCALE
            s = jnp.where(live, s, NEGATIVE)
            st_ref[q, :, t * N : (t + 1) * N] = s
            top = jnp.maximum(top, jnp.max(s, axis=0, keepdims=True))
        total = jnp.zeros((1, N), jnp.float32)
        for t in range(SHIFTS):
            s = st_ref[q, :, t * N : (t + 1) * N]
            e = jnp.where(live, jnp.exp(s - top), 0.0)
            total = total + jnp.sum(e, axis=0, keepdims=True)
        stat_ref[pl.ds(q, 1), :] = top
        stat_ref[pl.ds(2 + q, 1), :] = total


def score_rest(sig, pos, messages, batches, shifted, acc):
    return pl.pallas_call(
        score_rest_kernel,
        in_specs=[SMEM, SMEM] + [VMEM] * (Z + 8),
        out_specs=[VMEM, VMEM],
        out_shape=[
            pltpu.VMEM((2, COLS, ROWS), jnp.float32),
            pltpu.VMEM((8, N), jnp.float32),
        ],
        scratch_shapes=[
            pltpu.VMEM((RUNS, 8, REST), jnp.bfloat16),
            pltpu.VMEM((ROWS, COLS), jnp.float32),
            pltpu.VMEM((COLS, 128), jnp.float32),
        ],
        compiler_params=limit(8),
        cost_estimate=pl.CostEstimate(
            flops=4 * ROWS * COLS * REST, bytes_accessed=16 * 1024 * 1024, transcendentals=2 * ROWS * COLS
        ),
        name="score_rest",
    )(
        sig,
        pos,
        *[in_vmem(v) for v in (*messages, *batches, shifted[1], acc)],
    )


def merge_kernel(stat_ref, other_ref, out_ref):
    out_ref[...] = jnp.zeros_like(out_ref)
    for q in range(2):
        a, b = stat_ref[q : q + 1, :], other_ref[1 - q : 2 - q, :]
        top = jnp.maximum(a, b)
        out_ref[q : q + 1, :] = top
        out_ref[2 + q : 3 + q, :] = stat_ref[2 + q : 3 + q, :] * jnp.exp(a - top) + other_ref[
            3 - q : 4 - q, :
        ] * jnp.exp(b - top)
    bound = jnp.max(jnp.maximum(stat_ref[4:5, :], other_ref[4:5, :]), axis=1, keepdims=True)
    out_ref[4:5, :] = jnp.broadcast_to(jnp.maximum(bound, 1e-30), (1, N))


def merge(stats, other):
    return pl.pallas_call(
        merge_kernel,
        in_specs=[VMEM, VMEM],
        out_specs=VMEM,
        out_shape=pltpu.VMEM((8, N), jnp.float32),
        compiler_params=limit(2),
        name="merge",
    )(in_vmem(stats), in_vmem(other))


def partial_kernel(z_first, sig_ref, pos_ref, *refs):
    if not z_first:
        w_ref, bound_ref, image_ref, *out_refs = refs
        bound = bound_ref[4:5, 0:1]
    else:
        st_ref, *every = refs[:5]
        image_ref, *out_refs, w_ref, ev_ref = refs[5:]
        for q in range(2):
            tops = [r[q : q + 1, :] for r in every]
            top = jnp.maximum(jnp.maximum(tops[0], tops[1]), jnp.maximum(tops[2], tops[3]))
            total = sum(r[2 + q : 3 + q, :] * jnp.exp(t - top) for r, t in zip(every, tops))
            evidence = top + jnp.log(total)
            if q == 0:
                ev_ref[...] = evidence
            for t in range(SHIFTS):
                s = st_ref[q, :, t * N : (t + 1) * N]
                w_ref[q, :, t * N : (t + 1) * N] = jnp.exp(s - evidence).astype(jnp.bfloat16)
        bound = every[0][4:5, 0:1]
    scale = HEADROOM / bound
    entries = [
        [run_entry(sig_ref, pos_ref, q, dz, dx) for dz in range(Z) for dx in range(X)]
        for q in range(2)
    ]

    @pl.loop(0, PIX // PTILE)
    def _(i):
        at = pl.ds(pl.multiple_of(i * PTILE, PTILE), PTILE)
        for q in range(2):
            value = (
                jnp.dot(
                    w_ref[q],
                    image_ref[q, :, :, at].reshape(ROWS, PTILE),
                    preferred_element_type=jnp.float32,
                )
                * scale
            )
            for o in range(RUNS):
                _, second, zz = entries[q][o]
                out_ref = out_refs[o // X if z_first else o % X]
                base = (o % X if z_first else zz) * 16
                rows = pl.ds(pl.multiple_of(base + second * 8, 8), 8)
                block = value[o * 8 : o * 8 + 8, :]
                if q == 0:
                    other = pl.ds(pl.multiple_of(base + (1 - second) * 8, 8), 8)
                    out_ref[rows, at] = block
                    out_ref[other, at] = jnp.zeros_like(block)
                else:
                    out_ref[rows, at] += block


def partial_sums(z_first, sig, pos, weights, images):
    many, rows = (Z, X * 16) if z_first else (X, Z * 16)
    out_shape = [pltpu.VMEM((rows, PIX), jnp.float32)] * many
    if z_first:
        out_shape.append(pltpu.VMEM((2, COLS, ROWS), jnp.bfloat16))
        out_shape.append(jax.ShapeDtypeStruct((1, N), jnp.float32))
    return pl.pallas_call(
        lambda *refs: partial_kernel(z_first, *refs),
        in_specs=[SMEM, SMEM] + [VMEM] * (len(weights) + 1),
        out_specs=[VMEM] * len(out_shape),
        out_shape=out_shape,
        compiler_params=limit(4),
        cost_estimate=pl.CostEstimate(
            flops=2 * ROWS * COLS * FEATURES, bytes_accessed=16 * 1024 * 1024, transcendentals=0
        ),
        name="partial_re" if z_first else "partial_im",
    )(sig, pos, *[in_vmem(v) for v in weights], in_vmem(images))


HIGH, LOW = 32, 128


def insert_kernel(bound_ref, w_ref, ins_ref, *refs):
    scale = bound_ref[4:5, 0:1] * (1.0 / HEADROOM)
    high_ids = lax.broadcasted_iota(jnp.int32, (HIGH, PIX), 0)
    low_ids = lax.broadcasted_iota(jnp.int32, (LOW, PIX), 0)

    def step(i, acc):
        row = pl.ds(i, 1)
        ids = ins_ref[row, :]
        high = lax.shift_right_logical(ids, 7)
        low = lax.bitwise_and(ids, LOW - 1)
        value = w_ref[row, :] * scale
        head = value.astype(jnp.bfloat16).astype(jnp.float32)
        tail = value - head
        here = high == high_ids
        rows = jnp.concatenate(
            [jnp.where(here, head, 0.0), jnp.where(here, tail, 0.0)], axis=0
        ).astype(jnp.bfloat16)
        table = jnp.where(low == low_ids, 1.0, 0.0).astype(jnp.bfloat16)
        return acc + lax.dot_general(rows, table, DIMS, preferred_element_type=jnp.float32)

    empty = jnp.zeros((2 * HIGH, LOW), jnp.float32)
    acc = lax.fori_loop(0, 16, step, empty, unroll=1 if len(refs) == 1 else 4)
    slab = acc[:HIGH] + acc[HIGH:]
    if len(refs) == 1:
        refs[0][...] = slab
    else:
        re_ref, out_ref = refs
        for h in range(HIGH):
            at = slice(h * LOW, (h + 1) * LOW)
            out_ref[0:1, at] = re_ref[h : h + 1, :]
            out_ref[1:2, at] = slab[h : h + 1, :]


def insert(bound, weighted, insertion, *re):
    shape = (2, VOX) if re else (HIGH, LOW)
    return pl.pallas_call(
        insert_kernel,
        in_specs=[VMEM] * (3 + len(re)),
        out_specs=VMEM,
        out_shape=jax.ShapeDtypeStruct(shape, jnp.float32),
        compiler_params=limit(8),
        cost_estimate=pl.CostEstimate(
            flops=4 * HIGH * LOW * 16 * PIX, bytes_accessed=512 * 1024, transcendentals=0
        ),
        name="insert_im" if re else "insert_re",
    )(bound, weighted.reshape(16, PIX), insertion, *re)


def img_index(z, x, c):
    return (z * X + x) * CORES + c


def pairs(dz, dx, dc=0):
    return [
        (img_index(z, x, c), img_index((z + dz) % Z, (x + dx) % X, (c + dc) % CORES))
        for z in range(Z)
        for x in range(X)
        for c in range(CORES)
    ]


Z_GROUPS = [[img_index(z, x, c) for z in range(Z)] for x in range(X) for c in range(CORES)]


def send(value, dz=0, dx=0, dc=0):
    return lax.ppermute(value, "img", pairs(dz, dx, dc))


def all_to_all_z(value):
    return lax.all_to_all(
        value, "img", split_axis=0, concat_axis=0, tiled=True, axis_index_groups=Z_GROUPS
    )


def gather(projections, unit):
    mine = projections[:, :, :SPLIT]
    row = [mine, send(mine, dx=-1), send(mine, dx=-2), send(mine, dx=1)]
    ahead = behind = assemble(row, unit)
    messages = {0: ahead}
    for k in range(1, Z // 2 + 1):
        behind = send(behind, dz=1)
        messages[Z - k] = behind
        if k < Z // 2:
            ahead = send(ahead, dz=-1)
            messages[k] = ahead
    batches = []
    for places in (EARLY, LATE):
        column = pick([messages[k] for k in places])
        for dx in (-1, -2, 1):
            batches.append(send(column, dx=dx))
    return [messages[k] for k in range(Z)], batches


def wide(value):
    return value.astype(jnp.float32)


def narrow(value):
    return value.astype(jnp.float16)


def scatter_z_first(parts):
    half = Z // 2
    behind = narrow(parts[half])
    for k in range(half, 0, -1):
        if k < half:
            behind = narrow(parts[k] + wide(behind))
        behind = send(behind, dz=1)
    ahead = narrow(parts[half + 1])
    for k in range(half - 1, 0, -1):
        if k < half - 1:
            ahead = narrow(parts[Z - k] + wide(ahead))
        ahead = send(ahead, dz=-1)
    row = parts[0] + wide(behind) + wide(ahead)
    arrived = [send(narrow(row[k]), dx=k) for k in range(1, X)]
    return row[0] + wide(arrived[0]) + wide(arrived[1]) + wide(arrived[2])


def scatter_x_first(parts):
    arrived = [send(narrow(parts[k]), dx=k) for k in range(1, X)]
    column = narrow(parts[0] + wide(arrived[0]) + wide(arrived[1]) + wide(arrived[2]))
    return jnp.sum(wide(all_to_all_z(column)), axis=0)


def exchange_refs(value):
    out = [value]
    for k in range(1, REFS):
        out.append(lax.ppermute(value, "ref", [(r, (r + k) % REFS) for r in range(REFS)]))
    return out


def one_device(particles, projections, significance, insertion):
    img = lax.axis_index("img")
    ref = lax.axis_index("ref")
    z, x, core = img >> 3, (img >> 1) & 3, img & 1
    pos = jnp.stack([z, x, core, ref]).astype(jnp.int32)
    sig = lax.dynamic_slice_in_dim(significance, img - core, 2, axis=0)
    table = jnp.asarray(shift_tables())

    mate = send(particles, dc=1)
    unit = prepare(particles, projections)
    unit, pos, sig = lax.optimization_barrier((unit, pos, sig))
    messages, batches = gather(projections, unit)
    shifted = shifted_images(table, particles, mate)

    acc = score_first(sig, pos, messages, shifted)
    scores, stats = score_rest(sig, pos, messages, batches, shifted, acc)
    merged = merge(stats, send(stats, dc=1))
    every = exchange_refs(merged)
    *sums_re, weights, evidence = partial_sums(True, sig, pos, (scores, *every), shifted[0])
    sums_im = partial_sums(False, sig, pos, (weights, merged), shifted[1])
    total_re = scatter_z_first([v.reshape(X, 2, 8, PIX) for v in sums_re])
    total_im = scatter_x_first([v.reshape(Z, 2, 8, PIX) for v in sums_im])
    ids = insertion.reshape(16, PIX)
    slab = insert(merged, total_re, ids)
    volume = insert(merged, total_im, ids, slab)
    return volume, evidence.reshape(N)


def solution(mesh):
    in_specs = (P("img", None), P(("img", "ref"), None, None), P(), P(("img", "ref"), None, None))
    out_specs = (P(None, ("img", "ref")), P("img"))
    return jax.shard_map(
        one_device, mesh=mesh, in_specs=in_specs, out_specs=out_specs, check_vma=False
    )
```

```python
import math

import jax
import jax.numpy as jnp
import numpy as np
from jax import lax
from jax.experimental import pallas as pl
from jax.experimental.pallas import tpu as pltpu
from jax.sharding import PartitionSpec as P

SIDE = 64
PIX = 2048
FEATURES = 2 * PIX
VOX = 4096
Z, X, CORES, REFS = 8, 4, 2, 4
RUNS = Z * X
COLS = RUNS * 8
N = 256
SHIFTS = 5
ROWS = SHIFTS * N
NEGATIVE = -1e30
SCALE = 2.0 / math.sqrt(FEATURES)
HEADROOM = 2.5
EXTRA = 128
SPLIT = 2304
REST = FEATURES - SPLIT
BORDER = SPLIT - PIX
UNIT = REST + EXTRA
MESSAGE = X * SPLIT + UNIT
EARLY = (0, 1, 2, 6, 7)
LATE = (3, 4, 5)


def shift_tables():
    p = np.arange(PIX)
    unit = np.float32(2.0 * math.pi / SIDE)
    ax = (unit * (p % SIDE - SIDE // 2).astype(np.float32)).astype(np.float64)
    ay = (unit * (p // SIDE).astype(np.float32)).astype(np.float64)
    rows = [np.cos(ax), np.sin(ax), np.cos(ay), np.sin(ay)]
    return np.stack(rows + rows).astype(np.float32)


VMEM = pl.BlockSpec(memory_space=pltpu.VMEM)
SMEM = pl.BlockSpec(memory_space=pltpu.SMEM)
LANES = 512
PTILE = 512


def in_vmem(value):
    return pltpu.with_memory_space_constraint(value, pltpu.VMEM)


def limit(mib):
    return pltpu.CompilerParams(vmem_limit_bytes=mib * 1024 * 1024)


def prepare_kernel(image_ref, proj_ref, out_ref):
    top = jnp.zeros((16, FEATURES), jnp.bfloat16)
    for i in range(N // 16):
        top = jnp.maximum(top, jnp.abs(image_ref[i * 16 : i * 16 + 16, :]))
    largest = jnp.max(top.astype(jnp.float32), axis=0, keepdims=True)
    largest = jnp.max(largest, axis=1, keepdims=True)
    out_ref[:, :, 0:REST] = proj_ref[:, :, SPLIT:]
    for b in range(2):
        out_ref[b, :, REST:] = jnp.broadcast_to(largest, (8, EXTRA)).astype(jnp.bfloat16)


def prepare(images, projections):
    return pl.pallas_call(
        prepare_kernel,
        in_specs=[VMEM, VMEM],
        out_specs=VMEM,
        out_shape=pltpu.VMEM((2, 8, UNIT), jnp.bfloat16),
        compiler_params=limit(2),
        name="prepare",
    )(in_vmem(images), in_vmem(projections))


def assemble_kernel(*refs):
    *parts, out_ref = refs
    for k, part in enumerate(parts):
        out_ref[:, :, k * SPLIT : k * SPLIT + part.shape[2]] = part[...]


def assemble(row, unit):
    return pl.pallas_call(
        assemble_kernel,
        in_specs=[VMEM] * (X + 1),
        out_specs=VMEM,
        out_shape=pltpu.VMEM((2, 8, MESSAGE), jnp.bfloat16),
        compiler_params=limit(2),
        name="assemble",
    )(*[in_vmem(v) for v in (*row, unit)])


def pick_kernel(*refs):
    *messages, out_ref = refs
    for k, message in enumerate(messages):
        out_ref[k] = message[:, :, X * SPLIT :]


def pick(messages):
    return pl.pallas_call(
        pick_kernel,
        in_specs=[VMEM] * len(messages),
        out_specs=VMEM,
        out_shape=pltpu.VMEM((len(messages), 2, 8, UNIT), jnp.bfloat16),
        compiler_params=limit(2),
        name="pick",
    )(*[in_vmem(v) for v in messages])


def shift_kernel(table_ref, own_ref, mate_ref, out_re, out_im):
    for q, image_ref in enumerate((own_ref, mate_ref)):
        for j in range(PIX // LANES):
            at = slice(j * LANES, (j + 1) * LANES)
            at_im = slice(PIX + j * LANES, PIX + (j + 1) * LANES)
            tables = [table_ref[k : k + 1, at] for k in range(4)]

            @pl.loop(0, N // 16)
            def _(i):
                rows = pl.ds(pl.multiple_of(i * 16, 16), 16)
                re_in, im_in = image_ref[rows, at], image_ref[rows, at_im]
                out_re[q, 0, rows, at] = re_in
                out_im[q, 0, rows, at] = im_in
                re, im = re_in.astype(jnp.float32), im_in.astype(jnp.float32)
                for k in range(2):
                    c, s = tables[2 * k], tables[2 * k + 1]
                    rc, rs, ic, is_ = re * c, re * s, im * c, im * s
                    out_re[q, 1 + 2 * k, rows, at] = (rc - is_).astype(jnp.bfloat16)
                    out_im[q, 1 + 2 * k, rows, at] = (rs + ic).astype(jnp.bfloat16)
                    out_re[q, 2 + 2 * k, rows, at] = (rc + is_).astype(jnp.bfloat16)
                    out_im[q, 2 + 2 * k, rows, at] = (ic - rs).astype(jnp.bfloat16)


def shifted_images(table, own, mate):
    shape = pltpu.VMEM((2, SHIFTS, N, PIX), jnp.bfloat16)
    return pl.pallas_call(
        shift_kernel,
        in_specs=[VMEM] * 3,
        out_specs=[VMEM, VMEM],
        out_shape=[shape, shape],
        compiler_params=limit(4),
        cost_estimate=pl.CostEstimate(
            flops=48 * N * PIX, bytes_accessed=24 * 1024 * 1024, transcendentals=0
        ),
        name="shift",
    )(in_vmem(table), in_vmem(own), in_vmem(mate))


def run_entry(sig_ref, pos_ref, q, dz, dx):
    zz = lax.rem(pos_ref[0] + dz, Z)
    xx = lax.rem(pos_ref[1] + dx, X)
    at = (((zz * X + xx) * CORES + pos_ref[2]) * REFS + pos_ref[3]) * 2
    row = lax.rem(pos_ref[2] + q, 2)
    return sig_ref[row, at], sig_ref[row, at + 1], zz


DIMS = (((1,), (1,)), ((), ()))


def score_first_kernel(sig_ref, pos_ref, *refs):
    messages, (re_ref, im_ref, acc_ref, sel) = refs[:Z], refs[Z:]

    @pl.loop(0, 2)
    def _(q):
        for o in range(RUNS):
            dz, dx = o // X, o % X
            _, second, _ = run_entry(sig_ref, pos_ref, q, dz, dx)
            sel[o] = messages[dz][second, :, dx * SPLIT : (dx + 1) * SPLIT]
        acc_ref[q] = lax.dot_general(
            re_ref[q].reshape(ROWS, PIX),
            sel[:, :, 0:PIX].reshape(COLS, PIX),
            DIMS,
            preferred_element_type=jnp.float32,
        )
        acc_ref[q] += lax.dot_general(
            im_ref[q, :, :, 0:BORDER].reshape(ROWS, BORDER),
            sel[:, :, PIX:].reshape(COLS, BORDER),
            DIMS,
            preferred_element_type=jnp.float32,
        )


def score_first(sig, pos, messages, shifted):
    return pl.pallas_call(
        score_first_kernel,
        in_specs=[SMEM, SMEM] + [VMEM] * (Z + 2),
        out_specs=VMEM,
        out_shape=pltpu.VMEM((2, ROWS, COLS), jnp.float32),
        scratch_shapes=[pltpu.VMEM((RUNS, 8, SPLIT), jnp.bfloat16)],
        compiler_params=limit(8),
        cost_estimate=pl.CostEstimate(
            flops=4 * ROWS * COLS * SPLIT, bytes_accessed=16 * 1024 * 1024, transcendentals=0
        ),
        name="score_first",
    )(sig, pos, *[in_vmem(v) for v in messages], *[in_vmem(v) for v in shifted])


def score_rest_kernel(sig_ref, pos_ref, *refs):
    messages, batches = refs[:Z], refs[Z : Z + 6]
    im_ref, acc = refs[Z + 6 : Z + 8]
    st_ref, stat_ref, sel, work, mask = refs[Z + 8 :]

    def unit(dz, dx, second, at):
        if dx == 0:
            return messages[dz][second, :, X * SPLIT + at.start : X * SPLIT + at.stop]
        early = dz in EARLY
        place = (EARLY if early else LATE).index(dz)
        return batches[dx - 1 if early else dx + 2][place, second, :, at]

    stat_ref[...] = jnp.zeros_like(stat_ref)
    largest = jnp.zeros((8, EXTRA), jnp.float32)
    for o in range(RUNS):
        top = unit(o // X, o % X, 0, slice(REST, UNIT))
        largest = jnp.maximum(largest, top.astype(jnp.float32))
    stat_ref[4:5, 0:EXTRA] = jnp.max(largest, axis=0, keepdims=True)

    @pl.loop(0, 2)
    def _(q):
        for o in range(RUNS):
            first, second, _ = run_entry(sig_ref, pos_ref, q, o // X, o % X)
            sel[o] = unit(o // X, o % X, second, slice(0, REST))
            live = (first + second).astype(jnp.float32)
            mask[o * 8 : o * 8 + 8, :] = jnp.full((8, 128), live, jnp.float32)
        work[...] = acc[q] + lax.dot_general(
            im_ref[q, :, :, BORDER:].reshape(ROWS, REST),
            sel[...].reshape(COLS, REST),
            DIMS,
            preferred_element_type=jnp.float32,
        )
        live = mask[:, 0:1] > 0.5
        top = jnp.full((1, N), NEGATIVE, jnp.float32)
        for t in range(SHIFTS):
            s = work[t * N : (t + 1) * N, :].T * SCALE
            s = jnp.where(live, s, NEGATIVE)
            st_ref[q, :, t * N : (t + 1) * N] = s
            top = jnp.maximum(top, jnp.max(s, axis=0, keepdims=True))
        total = jnp.zeros((1, N), jnp.float32)
        for t in range(SHIFTS):
            s = st_ref[q, :, t * N : (t + 1) * N]
            e = jnp.where(live, jnp.exp(s - top), 0.0)
            total = total + jnp.sum(e, axis=0, keepdims=True)
        stat_ref[pl.ds(q, 1), :] = top
        stat_ref[pl.ds(2 + q, 1), :] = total


def score_rest(sig, pos, messages, batches, shifted, acc):
    return pl.pallas_call(
        score_rest_kernel,
        in_specs=[SMEM, SMEM] + [VMEM] * (Z + 8),
        out_specs=[VMEM, VMEM],
        out_shape=[
            pltpu.VMEM((2, COLS, ROWS), jnp.float32),
            pltpu.VMEM((8, N), jnp.float32),
        ],
        scratch_shapes=[
            pltpu.VMEM((RUNS, 8, REST), jnp.bfloat16),
            pltpu.VMEM((ROWS, COLS), jnp.float32),
            pltpu.VMEM((COLS, 128), jnp.float32),
        ],
        compiler_params=limit(8),
        cost_estimate=pl.CostEstimate(
            flops=4 * ROWS * COLS * REST, bytes_accessed=16 * 1024 * 1024, transcendentals=2 * ROWS * COLS
        ),
        name="score_rest",
    )(
        sig,
        pos,
        *[in_vmem(v) for v in (*messages, *batches, shifted[1], acc)],
    )


def merge_kernel(stat_ref, other_ref, out_ref):
    out_ref[...] = jnp.zeros_like(out_ref)
    for q in range(2):
        a, b = stat_ref[q : q + 1, :], other_ref[1 - q : 2 - q, :]
        top = jnp.maximum(a, b)
        out_ref[q : q + 1, :] = top
        out_ref[2 + q : 3 + q, :] = stat_ref[2 + q : 3 + q, :] * jnp.exp(a - top) + other_ref[
            3 - q : 4 - q, :
        ] * jnp.exp(b - top)
    bound = jnp.max(jnp.maximum(stat_ref[4:5, :], other_ref[4:5, :]), axis=1, keepdims=True)
    out_ref[4:5, :] = jnp.broadcast_to(jnp.maximum(bound, 1e-30), (1, N))


def merge(stats, other):
    return pl.pallas_call(
        merge_kernel,
        in_specs=[VMEM, VMEM],
        out_specs=VMEM,
        out_shape=pltpu.VMEM((8, N), jnp.float32),
        compiler_params=limit(2),
        name="merge",
    )(in_vmem(stats), in_vmem(other))


def partial_kernel(z_first, sig_ref, pos_ref, *refs):
    if not z_first:
        w_ref, bound_ref, im_ref, *out_refs = refs
        bound = bound_ref[4:5, 0:1]
    else:
        st_ref, *every = refs[:5]
        re_ref, im_ref, *out_refs, w_ref, ev_ref = refs[5:]
        for q in range(2):
            tops = [r[q : q + 1, :] for r in every]
            top = jnp.maximum(jnp.maximum(tops[0], tops[1]), jnp.maximum(tops[2], tops[3]))
            total = sum(r[2 + q : 3 + q, :] * jnp.exp(t - top) for r, t in zip(every, tops))
            evidence = top + jnp.log(total)
            if q == 0:
                ev_ref[...] = evidence
            for t in range(SHIFTS):
                s = st_ref[q, :, t * N : (t + 1) * N]
                w_ref[q, :, t * N : (t + 1) * N] = jnp.exp(s - evidence).astype(jnp.bfloat16)
        bound = every[0][4:5, 0:1]
    scale = HEADROOM / bound
    entries = [
        [run_entry(sig_ref, pos_ref, q, dz, dx) for dz in range(Z) for dx in range(X)]
        for q in range(2)
    ]

    def one_tile(image_ref, start, out_start, width):
        at_in = pl.ds(pl.multiple_of(start, 128), width)
        at = pl.ds(pl.multiple_of(out_start, 128), width)
        for q in range(2):
            value = (
                jnp.dot(
                    w_ref[q],
                    image_ref[q, :, :, at_in].reshape(ROWS, width),
                    preferred_element_type=jnp.float32,
                )
                * scale
            )
            for o in range(RUNS):
                _, second, zz = entries[q][o]
                out_ref = out_refs[o // X if z_first else o % X]
                base = (o % X if z_first else zz) * 16
                rows = pl.ds(pl.multiple_of(base + second * 8, 8), 8)
                block = value[o * 8 : o * 8 + 8, :]
                if q == 0:
                    other = pl.ds(pl.multiple_of(base + (1 - second) * 8, 8), 8)
                    out_ref[rows, at] = block
                    out_ref[other, at] = jnp.zeros_like(block)
                else:
                    out_ref[rows, at] += block

    if z_first:
        pl.loop(0, PIX // PTILE)(lambda i: one_tile(re_ref, i * PTILE, i * PTILE, PTILE))
        one_tile(im_ref, 0, PIX, BORDER)
    else:
        half = REST // 2
        pl.loop(0, 2)(lambda i: one_tile(im_ref, BORDER + i * half, i * half, half))


def partial_sums(z_first, sig, pos, weights, *images):
    many, rows = (Z, X * 16) if z_first else (X, Z * 16)
    out_shape = [pltpu.VMEM((rows, SPLIT if z_first else REST), jnp.float32)] * many
    if z_first:
        out_shape.append(pltpu.VMEM((2, COLS, ROWS), jnp.bfloat16))
        out_shape.append(jax.ShapeDtypeStruct((1, N), jnp.float32))
    return pl.pallas_call(
        lambda *refs: partial_kernel(z_first, *refs),
        in_specs=[SMEM, SMEM] + [VMEM] * (len(weights) + len(images)),
        out_specs=[VMEM] * len(out_shape),
        out_shape=out_shape,
        compiler_params=limit(4),
        cost_estimate=pl.CostEstimate(
            flops=2 * ROWS * COLS * FEATURES, bytes_accessed=16 * 1024 * 1024, transcendentals=0
        ),
        name="partial_first" if z_first else "partial_rest",
    )(sig, pos, *[in_vmem(v) for v in (*weights, *images)])


HIGH, LOW = 32, 128


def insert_kernel(bound_ref, w_ref, ins_ref, *refs):
    scale = bound_ref[4:5, 0:1] * (1.0 / HEADROOM)

    def add(acc, i, at, at_ids, width):
        row = pl.ds(i, 1)
        ids = ins_ref[row, at_ids]
        high = lax.shift_right_logical(ids, 7)
        low = lax.bitwise_and(ids, LOW - 1)
        value = w_ref[row, at] * scale
        head = value.astype(jnp.bfloat16).astype(jnp.float32)
        tail = value - head
        here = high == lax.broadcasted_iota(jnp.int32, (HIGH, width), 0)
        rows = jnp.concatenate(
            [jnp.where(here, head, 0.0), jnp.where(here, tail, 0.0)], axis=0
        ).astype(jnp.bfloat16)
        there = low == lax.broadcasted_iota(jnp.int32, (LOW, width), 0)
        table = jnp.where(there, 1.0, 0.0).astype(jnp.bfloat16)
        return acc + lax.dot_general(rows, table, DIMS, preferred_element_type=jnp.float32)

    empty = jnp.zeros((2 * HIGH, LOW), jnp.float32)
    if len(refs) == 3:
        re_ref, im_ref, out_ref = refs
        step = lambda i, acc: add(acc, i, slice(0, REST), slice(BORDER, PIX), REST)
        acc = lax.fori_loop(0, 16, step, empty, unroll=4)
        slab = im_ref[...] + acc[:HIGH] + acc[HIGH:]
        for h in range(HIGH):
            at = slice(h * LOW, (h + 1) * LOW)
            out_ref[0:1, at] = re_ref[h : h + 1, :]
            out_ref[1:2, at] = slab[h : h + 1, :]
    else:
        re_ref, im_ref = refs

        def step(i, both):
            re, im = both
            re = add(re, i, slice(0, PIX), slice(0, PIX), PIX)
            im = add(im, i, slice(PIX, SPLIT), slice(0, BORDER), BORDER)
            return re, im

        re, im = lax.fori_loop(0, 16, step, (empty, empty), unroll=2)
        re_ref[...] = re[:HIGH] + re[HIGH:]
        im_ref[...] = im[:HIGH] + im[HIGH:]


def insert(bound, weighted, insertion, *slabs):
    slab = jax.ShapeDtypeStruct((HIGH, LOW), jnp.float32)
    return pl.pallas_call(
        insert_kernel,
        in_specs=[VMEM] * (3 + len(slabs)),
        out_specs=VMEM if slabs else [VMEM, VMEM],
        out_shape=jax.ShapeDtypeStruct((2, VOX), jnp.float32) if slabs else [slab, slab],
        compiler_params=limit(8),
        cost_estimate=pl.CostEstimate(
            flops=4 * HIGH * LOW * 16 * PIX, bytes_accessed=512 * 1024, transcendentals=0
        ),
        name="insert_rest" if slabs else "insert_first",
    )(bound, weighted.reshape(16, weighted.shape[-1]), insertion, *slabs)


def img_index(z, x, c):
    return (z * X + x) * CORES + c


def pairs(dz, dx, dc=0):
    return [
        (img_index(z, x, c), img_index((z + dz) % Z, (x + dx) % X, (c + dc) % CORES))
        for z in range(Z)
        for x in range(X)
        for c in range(CORES)
    ]


Z_GROUPS = [[img_index(z, x, c) for z in range(Z)] for x in range(X) for c in range(CORES)]


def send(value, dz=0, dx=0, dc=0):
    return lax.ppermute(value, "img", pairs(dz, dx, dc))


def all_to_all_z(value):
    return lax.all_to_all(
        value, "img", split_axis=0, concat_axis=0, tiled=True, axis_index_groups=Z_GROUPS
    )


def gather(projections, unit):
    mine = projections[:, :, :SPLIT]
    row = [mine, send(mine, dx=-1), send(mine, dx=-2), send(mine, dx=1)]
    ahead = behind = assemble(row, unit)
    messages = {0: ahead}
    for k in range(1, Z // 2 + 1):
        behind = send(behind, dz=1)
        messages[Z - k] = behind
        if k < Z // 2:
            ahead = send(ahead, dz=-1)
            messages[k] = ahead
    batches = []
    for places in (EARLY, LATE):
        column = pick([messages[k] for k in places])
        for dx in (-1, -2, 1):
            batches.append(send(column, dx=dx))
    return [messages[k] for k in range(Z)], batches


def wide(value):
    return value.astype(jnp.float32)


def narrow(value):
    return value.astype(jnp.float16)


def scatter_z_first(parts):
    half = Z // 2
    behind = narrow(parts[half])
    for k in range(half, 0, -1):
        if k < half:
            behind = narrow(parts[k] + wide(behind))
        behind = send(behind, dz=1)
    ahead = narrow(parts[half + 1])
    for k in range(half - 1, 0, -1):
        if k < half - 1:
            ahead = narrow(parts[Z - k] + wide(ahead))
        ahead = send(ahead, dz=-1)
    row = parts[0] + wide(behind) + wide(ahead)
    arrived = [send(narrow(row[k]), dx=k) for k in range(1, X)]
    return row[0] + wide(arrived[0]) + wide(arrived[1]) + wide(arrived[2])


def scatter_x_first(parts):
    arrived = [send(narrow(parts[k]), dx=k) for k in range(1, X)]
    column = narrow(parts[0] + wide(arrived[0]) + wide(arrived[1]) + wide(arrived[2]))
    return jnp.sum(wide(all_to_all_z(column)), axis=0)


def exchange_refs(value):
    out = [value]
    for k in range(1, REFS):
        out.append(lax.ppermute(value, "ref", [(r, (r + k) % REFS) for r in range(REFS)]))
    return out


def one_device(particles, projections, significance, insertion):
    img = lax.axis_index("img")
    ref = lax.axis_index("ref")
    z, x, core = img >> 3, (img >> 1) & 3, img & 1
    pos = jnp.stack([z, x, core, ref]).astype(jnp.int32)
    sig = lax.dynamic_slice_in_dim(significance, img - core, 2, axis=0)
    table = jnp.asarray(shift_tables())

    mate = send(particles, dc=1)
    unit = prepare(particles, projections)
    unit, pos, sig = lax.optimization_barrier((unit, pos, sig))
    messages, batches = gather(projections, unit)
    shifted = shifted_images(table, particles, mate)

    acc = score_first(sig, pos, messages, shifted)
    scores, stats = score_rest(sig, pos, messages, batches, shifted, acc)
    merged = merge(stats, send(stats, dc=1))
    every = exchange_refs(merged)
    *sums, weights, evidence = partial_sums(True, sig, pos, (scores, *every), *shifted)
    sums_rest = partial_sums(False, sig, pos, (weights, merged), shifted[1])
    total = scatter_z_first([v.reshape(X, 2, 8, SPLIT) for v in sums])
    total_rest = scatter_x_first([v.reshape(Z, 2, 8, REST) for v in sums_rest])
    ids = insertion.reshape(16, PIX)
    slabs = insert(merged, total, ids)
    volume = insert(merged, total_rest, ids, *slabs)
    return volume, evidence.reshape(N)


def solution(mesh):
    in_specs = (P("img", None), P(("img", "ref"), None, None), P(), P(("img", "ref"), None, None))
    out_specs = (P(None, ("img", "ref")), P("img"))
    return jax.shard_map(
        one_device, mesh=mesh, in_specs=in_specs, out_specs=out_specs, check_vma=False
    )
```

```python
import math

import jax
import jax.numpy as jnp
import numpy as np
from jax import lax
from jax.experimental import pallas as pl
from jax.experimental.pallas import tpu as pltpu
from jax.sharding import PartitionSpec as P

SIDE = 64
PIX = 2048
FEATURES = 2 * PIX
VOX = 4096
Z, X, CORES, REFS = 8, 4, 2, 4
RUNS = Z * X
COLS = RUNS * 8
N = 256
SHIFTS = 5
ROWS = SHIFTS * N
NEGATIVE = -1e30
SCALE = 2.0 / math.sqrt(FEATURES)
HEADROOM = 2.5
EXTRA = 128
SPLIT = 2560
REST = FEATURES - SPLIT
BORDER = SPLIT - PIX
UNIT = REST + EXTRA
FAR = 2 * SPLIT
MESSAGE = X * SPLIT + UNIT
EARLY = (0, 1, 2, 6, 7)
LATE = (3, 4, 5)


def shift_tables():
    p = np.arange(PIX)
    unit = np.float32(2.0 * math.pi / SIDE)
    ax = (unit * (p % SIDE - SIDE // 2).astype(np.float32)).astype(np.float64)
    ay = (unit * (p // SIDE).astype(np.float32)).astype(np.float64)
    rows = [np.cos(ax), np.sin(ax), np.cos(ay), np.sin(ay)]
    return np.stack(rows + rows).astype(np.float32)


VMEM = pl.BlockSpec(memory_space=pltpu.VMEM)
SMEM = pl.BlockSpec(memory_space=pltpu.SMEM)
LANES = 512
PTILE = 512


def in_vmem(value):
    return pltpu.with_memory_space_constraint(value, pltpu.VMEM)


def limit(mib):
    return pltpu.CompilerParams(vmem_limit_bytes=mib * 1024 * 1024)


def prepare_kernel(image_ref, proj_ref, out_ref):
    top = jnp.zeros((16, FEATURES), jnp.bfloat16)
    for i in range(N // 16):
        top = jnp.maximum(top, jnp.abs(image_ref[i * 16 : i * 16 + 16, :]))
    largest = jnp.max(top.astype(jnp.float32), axis=0, keepdims=True)
    largest = jnp.max(largest, axis=1, keepdims=True)
    out_ref[:, :, 0:REST] = proj_ref[:, :, SPLIT:]
    for b in range(2):
        out_ref[b, :, REST:] = jnp.broadcast_to(largest, (8, EXTRA)).astype(jnp.bfloat16)


def prepare(images, projections):
    return pl.pallas_call(
        prepare_kernel,
        in_specs=[VMEM, VMEM],
        out_specs=VMEM,
        out_shape=pltpu.VMEM((2, 8, UNIT), jnp.bfloat16),
        compiler_params=limit(2),
        name="prepare",
    )(in_vmem(images), in_vmem(projections))


def assemble_kernel(*refs):
    *parts, out_ref = refs
    for k, part in enumerate(parts):
        out_ref[:, :, k * SPLIT : k * SPLIT + part.shape[2]] = part[...]


def assemble(row, unit):
    return pl.pallas_call(
        assemble_kernel,
        in_specs=[VMEM] * (X + 1),
        out_specs=VMEM,
        out_shape=pltpu.VMEM((2, 8, MESSAGE), jnp.bfloat16),
        compiler_params=limit(2),
        name="assemble",
    )(*[in_vmem(v) for v in (*row, unit)])


def pick_kernel(*refs):
    *messages, out_ref = refs
    for k, message in enumerate(messages):
        out_ref[k] = message[:, :, message.shape[2] - UNIT :]


def pick(messages):
    return pl.pallas_call(
        pick_kernel,
        in_specs=[VMEM] * len(messages),
        out_specs=VMEM,
        out_shape=pltpu.VMEM((len(messages), 2, 8, UNIT), jnp.bfloat16),
        compiler_params=limit(2),
        name="pick",
    )(*[in_vmem(v) for v in messages])


def shift_kernel(table_ref, own_ref, mate_ref, out_re, out_im):
    for q, image_ref in enumerate((own_ref, mate_ref)):
        for j in range(PIX // LANES):
            at = slice(j * LANES, (j + 1) * LANES)
            at_im = slice(PIX + j * LANES, PIX + (j + 1) * LANES)
            tables = [table_ref[k : k + 1, at] for k in range(4)]

            @pl.loop(0, N // 16)
            def _(i):
                rows = pl.ds(pl.multiple_of(i * 16, 16), 16)
                re_in, im_in = image_ref[rows, at], image_ref[rows, at_im]
                out_re[q, 0, rows, at] = re_in
                out_im[q, 0, rows, at] = im_in
                re, im = re_in.astype(jnp.float32), im_in.astype(jnp.float32)
                for k in range(2):
                    c, s = tables[2 * k], tables[2 * k + 1]
                    rc, rs, ic, is_ = re * c, re * s, im * c, im * s
                    out_re[q, 1 + 2 * k, rows, at] = (rc - is_).astype(jnp.bfloat16)
                    out_im[q, 1 + 2 * k, rows, at] = (rs + ic).astype(jnp.bfloat16)
                    out_re[q, 2 + 2 * k, rows, at] = (rc + is_).astype(jnp.bfloat16)
                    out_im[q, 2 + 2 * k, rows, at] = (ic - rs).astype(jnp.bfloat16)


def shifted_images(table, own, mate):
    shape = pltpu.VMEM((2, SHIFTS, N, PIX), jnp.bfloat16)
    return pl.pallas_call(
        shift_kernel,
        in_specs=[VMEM] * 3,
        out_specs=[VMEM, VMEM],
        out_shape=[shape, shape],
        compiler_params=limit(4),
        cost_estimate=pl.CostEstimate(
            flops=48 * N * PIX, bytes_accessed=24 * 1024 * 1024, transcendentals=0
        ),
        name="shift",
    )(in_vmem(table), in_vmem(own), in_vmem(mate))


def run_entry(sig_ref, pos_ref, q, dz, dx):
    zz = lax.rem(pos_ref[0] + dz, Z)
    xx = lax.rem(pos_ref[1] + dx, X)
    at = (((zz * X + xx) * CORES + pos_ref[2]) * REFS + pos_ref[3]) * 2
    row = lax.rem(pos_ref[2] + q, 2)
    return sig_ref[row, at], sig_ref[row, at + 1], zz


DIMS = (((1,), (1,)), ((), ()))


def message_part(messages, dz, block, start, stop):
    if dz == Z // 2 and start >= FAR:
        return messages[Z][block, :, start - FAR : stop - FAR]
    return messages[dz][block, :, start:stop]


def score_first_kernel(sig_ref, pos_ref, *refs):
    messages, (re_ref, im_ref, acc_ref, sel) = refs[: Z + 1], refs[Z + 1 :]

    @pl.loop(0, 2)
    def _(q):
        for o in range(RUNS):
            dz, dx = o // X, o % X
            _, second, _ = run_entry(sig_ref, pos_ref, q, dz, dx)
            sel[o] = message_part(messages, dz, second, dx * SPLIT, (dx + 1) * SPLIT)
        acc_ref[q] = lax.dot_general(
            re_ref[q].reshape(ROWS, PIX),
            sel[:, :, 0:PIX].reshape(COLS, PIX),
            DIMS,
            preferred_element_type=jnp.float32,
        )
        acc_ref[q] += lax.dot_general(
            im_ref[q, :, :, 0:BORDER].reshape(ROWS, BORDER),
            sel[:, :, PIX:].reshape(COLS, BORDER),
            DIMS,
            preferred_element_type=jnp.float32,
        )


def score_first(sig, pos, messages, shifted):
    return pl.pallas_call(
        score_first_kernel,
        in_specs=[SMEM, SMEM] + [VMEM] * (Z + 3),
        out_specs=VMEM,
        out_shape=pltpu.VMEM((2, ROWS, COLS), jnp.float32),
        scratch_shapes=[pltpu.VMEM((RUNS, 8, SPLIT), jnp.bfloat16)],
        compiler_params=limit(8),
        cost_estimate=pl.CostEstimate(
            flops=4 * ROWS * COLS * SPLIT, bytes_accessed=16 * 1024 * 1024, transcendentals=0
        ),
        name="score_first",
    )(sig, pos, *[in_vmem(v) for v in messages], *[in_vmem(v) for v in shifted])


def score_rest_kernel(sig_ref, pos_ref, *refs):
    messages, batches = refs[: Z + 1], refs[Z + 1 : Z + 7]
    im_ref, acc = refs[Z + 7 : Z + 9]
    st_ref, stat_ref, sel, work, mask = refs[Z + 9 :]

    def unit(dz, dx, second, at):
        if dx == 0:
            return message_part(messages, dz, second, X * SPLIT + at.start, X * SPLIT + at.stop)
        early = dz in EARLY
        place = (EARLY if early else LATE).index(dz)
        return batches[dx - 1 if early else dx + 2][place, second, :, at]

    stat_ref[...] = jnp.zeros_like(stat_ref)
    largest = jnp.zeros((8, EXTRA), jnp.float32)
    for o in range(RUNS):
        top = unit(o // X, o % X, 0, slice(REST, UNIT))
        largest = jnp.maximum(largest, top.astype(jnp.float32))
    stat_ref[4:5, 0:EXTRA] = jnp.max(largest, axis=0, keepdims=True)

    @pl.loop(0, 2)
    def _(q):
        for o in range(RUNS):
            first, second, _ = run_entry(sig_ref, pos_ref, q, o // X, o % X)
            sel[o] = unit(o // X, o % X, second, slice(0, REST))
            live = (first + second).astype(jnp.float32)
            mask[o * 8 : o * 8 + 8, :] = jnp.full((8, 128), live, jnp.float32)
        work[...] = acc[q] + lax.dot_general(
            im_ref[q, :, :, BORDER:].reshape(ROWS, REST),
            sel[...].reshape(COLS, REST),
            DIMS,
            preferred_element_type=jnp.float32,
        )
        live = mask[:, 0:1] > 0.5
        top = jnp.full((1, N), NEGATIVE, jnp.float32)
        for t in range(SHIFTS):
            s = work[t * N : (t + 1) * N, :].T * SCALE
            s = jnp.where(live, s, NEGATIVE)
            st_ref[q, :, t * N : (t + 1) * N] = s
            top = jnp.maximum(top, jnp.max(s, axis=0, keepdims=True))
        total = jnp.zeros((1, N), jnp.float32)
        for t in range(SHIFTS):
            s = st_ref[q, :, t * N : (t + 1) * N]
            e = jnp.where(live, jnp.exp(s - top), 0.0)
            total = total + jnp.sum(e, axis=0, keepdims=True)
        stat_ref[pl.ds(q, 1), :] = top
        stat_ref[pl.ds(2 + q, 1), :] = total


def score_rest(sig, pos, messages, batches, shifted, acc):
    return pl.pallas_call(
        score_rest_kernel,
        in_specs=[SMEM, SMEM] + [VMEM] * (Z + 9),
        out_specs=[VMEM, VMEM],
        out_shape=[
            pltpu.VMEM((2, COLS, ROWS), jnp.float32),
            pltpu.VMEM((8, N), jnp.float32),
        ],
        scratch_shapes=[
            pltpu.VMEM((RUNS, 8, REST), jnp.bfloat16),
            pltpu.VMEM((ROWS, COLS), jnp.float32),
            pltpu.VMEM((COLS, 128), jnp.float32),
        ],
        compiler_params=limit(8),
        cost_estimate=pl.CostEstimate(
            flops=4 * ROWS * COLS * REST, bytes_accessed=16 * 1024 * 1024, transcendentals=2 * ROWS * COLS
        ),
        name="score_rest",
    )(
        sig,
        pos,
        *[in_vmem(v) for v in (*messages, *batches, shifted[1], acc)],
    )


def merge_kernel(stat_ref, other_ref, out_ref):
    out_ref[...] = jnp.zeros_like(out_ref)
    for q in range(2):
        a, b = stat_ref[q : q + 1, :], other_ref[1 - q : 2 - q, :]
        top = jnp.maximum(a, b)
        out_ref[q : q + 1, :] = top
        out_ref[2 + q : 3 + q, :] = stat_ref[2 + q : 3 + q, :] * jnp.exp(a - top) + other_ref[
            3 - q : 4 - q, :
        ] * jnp.exp(b - top)
    bound = jnp.max(jnp.maximum(stat_ref[4:5, :], other_ref[4:5, :]), axis=1, keepdims=True)
    out_ref[4:5, :] = jnp.broadcast_to(jnp.maximum(bound, 1e-30), (1, N))


def merge(stats, other):
    return pl.pallas_call(
        merge_kernel,
        in_specs=[VMEM, VMEM],
        out_specs=VMEM,
        out_shape=pltpu.VMEM((8, N), jnp.float32),
        compiler_params=limit(2),
        name="merge",
    )(in_vmem(stats), in_vmem(other))


def partial_kernel(z_first, sig_ref, pos_ref, *refs):
    if not z_first:
        w_ref, bound_ref, im_ref, *out_refs = refs
        bound = bound_ref[4:5, 0:1]
    else:
        st_ref, *every = refs[:5]
        re_ref, im_ref, *out_refs, w_ref, ev_ref = refs[5:]
        for q in range(2):
            tops = [r[q : q + 1, :] for r in every]
            top = jnp.maximum(jnp.maximum(tops[0], tops[1]), jnp.maximum(tops[2], tops[3]))
            total = sum(r[2 + q : 3 + q, :] * jnp.exp(t - top) for r, t in zip(every, tops))
            evidence = top + jnp.log(total)
            if q == 0:
                ev_ref[...] = evidence
            for t in range(SHIFTS):
                s = st_ref[q, :, t * N : (t + 1) * N]
                w_ref[q, :, t * N : (t + 1) * N] = jnp.exp(s - evidence).astype(jnp.bfloat16)
        bound = every[0][4:5, 0:1]
    scale = HEADROOM / bound
    entries = [
        [run_entry(sig_ref, pos_ref, q, dz, dx) for dz in range(Z) for dx in range(X)]
        for q in range(2)
    ]

    def one_tile(image_ref, start, out_start, width):
        at_in = pl.ds(pl.multiple_of(start, 128), width)
        at = pl.ds(pl.multiple_of(out_start, 128), width)
        for q in range(2):
            value = (
                jnp.dot(
                    w_ref[q],
                    image_ref[q, :, :, at_in].reshape(ROWS, width),
                    preferred_element_type=jnp.float32,
                )
                * scale
            )
            for o in range(RUNS):
                _, second, zz = entries[q][o]
                out_ref = out_refs[o // X if z_first else o % X]
                base = (o % X if z_first else zz) * 16
                rows = pl.ds(pl.multiple_of(base + second * 8, 8), 8)
                block = value[o * 8 : o * 8 + 8, :]
                if q == 0:
                    other = pl.ds(pl.multiple_of(base + (1 - second) * 8, 8), 8)
                    out_ref[rows, at] = block
                    out_ref[other, at] = jnp.zeros_like(block)
                else:
                    out_ref[rows, at] += block

    if z_first:
        pl.loop(0, PIX // PTILE)(lambda i: one_tile(re_ref, i * PTILE, i * PTILE, PTILE))
        one_tile(im_ref, 0, PIX, BORDER)
    else:
        half = REST // 2
        pl.loop(0, 2)(lambda i: one_tile(im_ref, BORDER + i * half, i * half, half))


def partial_sums(z_first, sig, pos, weights, *images):
    many, rows = (Z, X * 16) if z_first else (X, Z * 16)
    out_shape = [pltpu.VMEM((rows, SPLIT if z_first else REST), jnp.float32)] * many
    if z_first:
        out_shape.append(pltpu.VMEM((2, COLS, ROWS), jnp.bfloat16))
        out_shape.append(jax.ShapeDtypeStruct((1, N), jnp.float32))
    return pl.pallas_call(
        lambda *refs: partial_kernel(z_first, *refs),
        in_specs=[SMEM, SMEM] + [VMEM] * (len(weights) + len(images)),
        out_specs=[VMEM] * len(out_shape),
        out_shape=out_shape,
        compiler_params=limit(4),
        cost_estimate=pl.CostEstimate(
            flops=2 * ROWS * COLS * FEATURES, bytes_accessed=16 * 1024 * 1024, transcendentals=0
        ),
        name="partial_first" if z_first else "partial_rest",
    )(sig, pos, *[in_vmem(v) for v in (*weights, *images)])


HIGH, LOW = 32, 128


def insert_kernel(bound_ref, w_ref, ins_ref, *refs):
    scale = bound_ref[4:5, 0:1] * (1.0 / HEADROOM)

    def add(acc, i, at, at_ids, width):
        row = pl.ds(i, 1)
        ids = ins_ref[row, at_ids]
        high = lax.shift_right_logical(ids, 7)
        low = lax.bitwise_and(ids, LOW - 1)
        value = w_ref[row, at] * scale
        head = value.astype(jnp.bfloat16).astype(jnp.float32)
        tail = value - head
        here = high == lax.broadcasted_iota(jnp.int32, (HIGH, width), 0)
        rows = jnp.concatenate(
            [jnp.where(here, head, 0.0), jnp.where(here, tail, 0.0)], axis=0
        ).astype(jnp.bfloat16)
        there = low == lax.broadcasted_iota(jnp.int32, (LOW, width), 0)
        table = jnp.where(there, 1.0, 0.0).astype(jnp.bfloat16)
        return acc + lax.dot_general(rows, table, DIMS, preferred_element_type=jnp.float32)

    empty = jnp.zeros((2 * HIGH, LOW), jnp.float32)
    if len(refs) == 3:
        re_ref, im_ref, out_ref = refs
        step = lambda i, acc: add(acc, i, slice(0, REST), slice(BORDER, PIX), REST)
        acc = lax.fori_loop(0, 16, step, empty, unroll=2)
        slab = im_ref[...] + acc[:HIGH] + acc[HIGH:]
        for h in range(HIGH):
            at = slice(h * LOW, (h + 1) * LOW)
            out_ref[0:1, at] = re_ref[h : h + 1, :]
            out_ref[1:2, at] = slab[h : h + 1, :]
    else:
        re_ref, im_ref = refs

        def step(i, both):
            re, im = both
            re = add(re, i, slice(0, PIX), slice(0, PIX), PIX)
            im = add(im, i, slice(PIX, SPLIT), slice(0, BORDER), BORDER)
            return re, im

        re, im = lax.fori_loop(0, 16, step, (empty, empty))
        re_ref[...] = re[:HIGH] + re[HIGH:]
        im_ref[...] = im[:HIGH] + im[HIGH:]


def insert(bound, weighted, insertion, *slabs):
    slab = jax.ShapeDtypeStruct((HIGH, LOW), jnp.float32)
    return pl.pallas_call(
        insert_kernel,
        in_specs=[VMEM] * (3 + len(slabs)),
        out_specs=VMEM if slabs else [VMEM, VMEM],
        out_shape=jax.ShapeDtypeStruct((2, VOX), jnp.float32) if slabs else [slab, slab],
        compiler_params=limit(8),
        cost_estimate=pl.CostEstimate(
            flops=4 * HIGH * LOW * 16 * PIX, bytes_accessed=512 * 1024, transcendentals=0
        ),
        name="insert_rest" if slabs else "insert_first",
    )(bound, weighted.reshape(16, weighted.shape[-1]), insertion, *slabs)


def img_index(z, x, c):
    return (z * X + x) * CORES + c


def pairs(dz, dx, dc=0):
    return [
        (img_index(z, x, c), img_index((z + dz) % Z, (x + dx) % X, (c + dc) % CORES))
        for z in range(Z)
        for x in range(X)
        for c in range(CORES)
    ]


Z_GROUPS = [[img_index(z, x, c) for z in range(Z)] for x in range(X) for c in range(CORES)]


def send(value, dz=0, dx=0, dc=0):
    return lax.ppermute(value, "img", pairs(dz, dx, dc))


def all_to_all_z(value):
    return lax.all_to_all(
        value, "img", split_axis=0, concat_axis=0, tiled=True, axis_index_groups=Z_GROUPS
    )


def gather(projections, unit):
    mine = projections[:, :, :SPLIT]
    row = [mine, send(mine, dx=-1), send(mine, dx=-2), send(mine, dx=1)]
    ahead = behind = assemble(row, unit)
    messages = {0: ahead}
    for k in range(1, Z // 2):
        behind = send(behind, dz=1)
        messages[Z - k] = behind
        ahead = send(ahead, dz=-1)
        messages[k] = ahead
    left = send(behind[:, :, :FAR], dz=1)
    right = send(ahead[:, :, FAR:], dz=-1)
    late = [messages[3], right, messages[5]]
    batches = []
    for column in (pick([messages[k] for k in EARLY]), pick(late)):
        for dx in (-1, -2, 1):
            batches.append(send(column, dx=dx))
    messages[Z // 2] = left
    return [messages[k] for k in range(Z)] + [right], batches


def wide(value):
    return value.astype(jnp.float32)


def narrow(value):
    return value.astype(jnp.float16)


def scatter_z_first(parts):
    far, cut = parts[Z // 2], X // 2
    behind = send(narrow(far[:cut]), dz=1)
    ahead = send(narrow(far[cut:]), dz=-1)
    behind = jnp.concatenate([parts[3][:cut] + wide(behind), parts[3][cut:]])
    ahead = jnp.concatenate([parts[5][:cut], parts[5][cut:] + wide(ahead)])
    for k in range(3, 0, -1):
        behind = send(narrow(behind), dz=1)
        ahead = send(narrow(ahead), dz=-1)
        if k > 1:
            behind = parts[k - 1] + wide(behind)
            ahead = parts[Z - k + 1] + wide(ahead)
    row = parts[0] + wide(behind) + wide(ahead)
    arrived = [send(narrow(row[k]), dx=k) for k in range(1, X)]
    return row[0] + wide(arrived[0]) + wide(arrived[1]) + wide(arrived[2])


def scatter_x_first(parts):
    arrived = [send(narrow(parts[k]), dx=k) for k in range(1, X)]
    column = narrow(parts[0] + wide(arrived[0]) + wide(arrived[1]) + wide(arrived[2]))
    return jnp.sum(wide(all_to_all_z(column)), axis=0)


def exchange_refs(value):
    out = [value]
    for k in range(1, REFS):
        out.append(lax.ppermute(value, "ref", [(r, (r + k) % REFS) for r in range(REFS)]))
    return out


def one_device(particles, projections, significance, insertion):
    img = lax.axis_index("img")
    ref = lax.axis_index("ref")
    z, x, core = img >> 3, (img >> 1) & 3, img & 1
    pos = jnp.stack([z, x, core, ref]).astype(jnp.int32)
    sig = lax.dynamic_slice_in_dim(significance, img - core, 2, axis=0)
    table = jnp.asarray(shift_tables())

    mate = send(particles, dc=1)
    unit = prepare(particles, projections)
    unit, pos, sig = lax.optimization_barrier((unit, pos, sig))
    messages, batches = gather(projections, unit)
    shifted = shifted_images(table, particles, mate)

    acc = score_first(sig, pos, messages, shifted)
    scores, stats = score_rest(sig, pos, messages, batches, shifted, acc)
    merged = merge(stats, send(stats, dc=1))
    every = exchange_refs(merged)
    *sums, weights, evidence = partial_sums(True, sig, pos, (scores, *every), *shifted)
    sums_rest = partial_sums(False, sig, pos, (weights, merged), shifted[1])
    total = scatter_z_first([v.reshape(X, 2, 8, SPLIT) for v in sums])
    total_rest = scatter_x_first([v.reshape(Z, 2, 8, REST) for v in sums_rest])
    ids = insertion.reshape(16, PIX)
    slabs = insert(merged, total, ids)
    volume = insert(merged, total_rest, ids, *slabs)
    return volume, evidence.reshape(N)


def solution(mesh):
    in_specs = (P("img", None), P(("img", "ref"), None, None), P(), P(("img", "ref"), None, None))
    out_specs = (P(None, ("img", "ref")), P("img"))
    return jax.shard_map(
        one_device, mesh=mesh, in_specs=in_specs, out_specs=out_specs, check_vma=False
    )
```

```python
import math

import jax
import jax.numpy as jnp
import numpy as np
from jax import lax
from jax.experimental import pallas as pl
from jax.experimental.pallas import tpu as pltpu
from jax.sharding import PartitionSpec as P

SIDE = 64
PIX = 2048
FEATURES = 2 * PIX
VOX = 4096
Z, X, CORES, REFS = 8, 4, 2, 4
RUNS = Z * X
COLS = RUNS * 8
N = 256
SHIFTS = 5
ROWS = SHIFTS * N
NEGATIVE = -1e30
SCALE = 2.0 / math.sqrt(FEATURES)
HEADROOM = 2.5
EXTRA = 128
SPLIT = 2560
REST = FEATURES - SPLIT
BORDER = SPLIT - PIX
UNIT = REST + EXTRA
FAR = 2 * SPLIT
MESSAGE = X * SPLIT + UNIT
FIRST = 2304
OTHERS = FEATURES - FIRST
EDGE = FIRST - PIX
EARLY = (0, 1, 2, 6, 7)
LATE = (3, 4, 5)


def shift_tables():
    p = np.arange(PIX)
    unit = np.float32(2.0 * math.pi / SIDE)
    ax = (unit * (p % SIDE - SIDE // 2).astype(np.float32)).astype(np.float64)
    ay = (unit * (p // SIDE).astype(np.float32)).astype(np.float64)
    rows = [np.cos(ax), np.sin(ax), np.cos(ay), np.sin(ay)]
    return np.stack(rows + rows).astype(np.float32)


VMEM = pl.BlockSpec(memory_space=pltpu.VMEM)
SMEM = pl.BlockSpec(memory_space=pltpu.SMEM)
LANES = 512
PTILE = 512


def in_vmem(value):
    return pltpu.with_memory_space_constraint(value, pltpu.VMEM)


def limit(mib):
    return pltpu.CompilerParams(vmem_limit_bytes=mib * 1024 * 1024)


def prepare_kernel(image_ref, proj_ref, out_ref):
    top = jnp.zeros((16, FEATURES), jnp.bfloat16)
    for i in range(N // 16):
        top = jnp.maximum(top, jnp.abs(image_ref[i * 16 : i * 16 + 16, :]))
    largest = jnp.max(top.astype(jnp.float32), axis=0, keepdims=True)
    largest = jnp.max(largest, axis=1, keepdims=True)
    out_ref[:, :, 0:REST] = proj_ref[:, :, SPLIT:]
    for b in range(2):
        out_ref[b, :, REST:] = jnp.broadcast_to(largest, (8, EXTRA)).astype(jnp.bfloat16)


def prepare(images, projections):
    return pl.pallas_call(
        prepare_kernel,
        in_specs=[VMEM, VMEM],
        out_specs=VMEM,
        out_shape=pltpu.VMEM((2, 8, UNIT), jnp.bfloat16),
        compiler_params=limit(2),
        name="prepare",
    )(in_vmem(images), in_vmem(projections))


def assemble_kernel(*refs):
    *parts, out_ref = refs
    for k, part in enumerate(parts):
        out_ref[:, :, k * SPLIT : k * SPLIT + part.shape[2]] = part[...]


def assemble(row, unit):
    return pl.pallas_call(
        assemble_kernel,
        in_specs=[VMEM] * (X + 1),
        out_specs=VMEM,
        out_shape=pltpu.VMEM((2, 8, MESSAGE), jnp.bfloat16),
        compiler_params=limit(2),
        name="assemble",
    )(*[in_vmem(v) for v in (*row, unit)])


def pick_kernel(*refs):
    *messages, out_ref = refs
    for k, message in enumerate(messages):
        out_ref[k] = message[:, :, message.shape[2] - UNIT :]


def pick(messages):
    return pl.pallas_call(
        pick_kernel,
        in_specs=[VMEM] * len(messages),
        out_specs=VMEM,
        out_shape=pltpu.VMEM((len(messages), 2, 8, UNIT), jnp.bfloat16),
        compiler_params=limit(2),
        name="pick",
    )(*[in_vmem(v) for v in messages])


def shift_kernel(table_ref, own_ref, mate_ref, out_re, out_im):
    for q, image_ref in enumerate((own_ref, mate_ref)):
        for j in range(PIX // LANES):
            at = slice(j * LANES, (j + 1) * LANES)
            at_im = slice(PIX + j * LANES, PIX + (j + 1) * LANES)
            tables = [table_ref[k : k + 1, at] for k in range(4)]

            @pl.loop(0, N // 16)
            def _(i):
                rows = pl.ds(pl.multiple_of(i * 16, 16), 16)
                re_in, im_in = image_ref[rows, at], image_ref[rows, at_im]
                out_re[q, 0, rows, at] = re_in
                out_im[q, 0, rows, at] = im_in
                re, im = re_in.astype(jnp.float32), im_in.astype(jnp.float32)
                for k in range(2):
                    c, s = tables[2 * k], tables[2 * k + 1]
                    rc, rs, ic, is_ = re * c, re * s, im * c, im * s
                    out_re[q, 1 + 2 * k, rows, at] = (rc - is_).astype(jnp.bfloat16)
                    out_im[q, 1 + 2 * k, rows, at] = (rs + ic).astype(jnp.bfloat16)
                    out_re[q, 2 + 2 * k, rows, at] = (rc + is_).astype(jnp.bfloat16)
                    out_im[q, 2 + 2 * k, rows, at] = (ic - rs).astype(jnp.bfloat16)


def shifted_images(table, own, mate):
    shape = pltpu.VMEM((2, SHIFTS, N, PIX), jnp.bfloat16)
    return pl.pallas_call(
        shift_kernel,
        in_specs=[VMEM] * 3,
        out_specs=[VMEM, VMEM],
        out_shape=[shape, shape],
        compiler_params=limit(4),
        cost_estimate=pl.CostEstimate(
            flops=48 * N * PIX, bytes_accessed=24 * 1024 * 1024, transcendentals=0
        ),
        name="shift",
    )(in_vmem(table), in_vmem(own), in_vmem(mate))


def run_entry(sig_ref, pos_ref, q, dz, dx):
    zz = lax.rem(pos_ref[0] + dz, Z)
    xx = lax.rem(pos_ref[1] + dx, X)
    at = (((zz * X + xx) * CORES + pos_ref[2]) * REFS + pos_ref[3]) * 2
    row = lax.rem(pos_ref[2] + q, 2)
    return sig_ref[row, at], sig_ref[row, at + 1], zz


DIMS = (((1,), (1,)), ((), ()))


def message_part(messages, dz, block, start, stop):
    if dz == Z // 2 and start >= FAR:
        return messages[Z][block, :, start - FAR : stop - FAR]
    return messages[dz][block, :, start:stop]


def score_first_kernel(sig_ref, pos_ref, *refs):
    messages, (re_ref, im_ref, acc_ref, sel) = refs[: Z + 1], refs[Z + 1 :]

    @pl.loop(0, 2)
    def _(q):
        for o in range(RUNS):
            dz, dx = o // X, o % X
            _, second, _ = run_entry(sig_ref, pos_ref, q, dz, dx)
            sel[o] = message_part(messages, dz, second, dx * SPLIT, (dx + 1) * SPLIT)
        acc_ref[q] = lax.dot_general(
            re_ref[q].reshape(ROWS, PIX),
            sel[:, :, 0:PIX].reshape(COLS, PIX),
            DIMS,
            preferred_element_type=jnp.float32,
        )
        acc_ref[q] += lax.dot_general(
            im_ref[q, :, :, 0:BORDER].reshape(ROWS, BORDER),
            sel[:, :, PIX:].reshape(COLS, BORDER),
            DIMS,
            preferred_element_type=jnp.float32,
        )


def score_first(sig, pos, messages, shifted):
    return pl.pallas_call(
        score_first_kernel,
        in_specs=[SMEM, SMEM] + [VMEM] * (Z + 3),
        out_specs=VMEM,
        out_shape=pltpu.VMEM((2, ROWS, COLS), jnp.float32),
        scratch_shapes=[pltpu.VMEM((RUNS, 8, SPLIT), jnp.bfloat16)],
        compiler_params=limit(8),
        cost_estimate=pl.CostEstimate(
            flops=4 * ROWS * COLS * SPLIT, bytes_accessed=16 * 1024 * 1024, transcendentals=0
        ),
        name="score_first",
    )(sig, pos, *[in_vmem(v) for v in messages], *[in_vmem(v) for v in shifted])


def score_rest_kernel(sig_ref, pos_ref, *refs):
    messages, batches = refs[: Z + 1], refs[Z + 1 : Z + 7]
    im_ref, acc = refs[Z + 7 : Z + 9]
    st_ref, stat_ref, sel, work, mask = refs[Z + 9 :]

    def unit(dz, dx, second, at):
        if dx == 0:
            return message_part(messages, dz, second, X * SPLIT + at.start, X * SPLIT + at.stop)
        early = dz in EARLY
        place = (EARLY if early else LATE).index(dz)
        return batches[dx - 1 if early else dx + 2][place, second, :, at]

    stat_ref[...] = jnp.zeros_like(stat_ref)
    largest = jnp.zeros((8, EXTRA), jnp.float32)
    for o in range(RUNS):
        top = unit(o // X, o % X, 0, slice(REST, UNIT))
        largest = jnp.maximum(largest, top.astype(jnp.float32))
    stat_ref[4:5, 0:EXTRA] = jnp.max(largest, axis=0, keepdims=True)

    @pl.loop(0, 2)
    def _(q):
        for o in range(RUNS):
            first, second, _ = run_entry(sig_ref, pos_ref, q, o // X, o % X)
            sel[o] = unit(o // X, o % X, second, slice(0, REST))
            live = (first + second).astype(jnp.float32)
            mask[o * 8 : o * 8 + 8, :] = jnp.full((8, 128), live, jnp.float32)
        work[...] = acc[q] + lax.dot_general(
            im_ref[q, :, :, BORDER:].reshape(ROWS, REST),
            sel[...].reshape(COLS, REST),
            DIMS,
            preferred_element_type=jnp.float32,
        )
        live = mask[:, 0:1] > 0.5
        top = jnp.full((1, N), NEGATIVE, jnp.float32)
        for t in range(SHIFTS):
            s = work[t * N : (t + 1) * N, :].T * SCALE
            s = jnp.where(live, s, NEGATIVE)
            st_ref[q, :, t * N : (t + 1) * N] = s
            top = jnp.maximum(top, jnp.max(s, axis=0, keepdims=True))
        total = jnp.zeros((1, N), jnp.float32)
        for t in range(SHIFTS):
            s = st_ref[q, :, t * N : (t + 1) * N]
            e = jnp.where(live, jnp.exp(s - top), 0.0)
            total = total + jnp.sum(e, axis=0, keepdims=True)
        stat_ref[pl.ds(q, 1), :] = top
        stat_ref[pl.ds(2 + q, 1), :] = total


def score_rest(sig, pos, messages, batches, shifted, acc):
    return pl.pallas_call(
        score_rest_kernel,
        in_specs=[SMEM, SMEM] + [VMEM] * (Z + 9),
        out_specs=[VMEM, VMEM],
        out_shape=[
            pltpu.VMEM((2, COLS, ROWS), jnp.float32),
            pltpu.VMEM((8, N), jnp.float32),
        ],
        scratch_shapes=[
            pltpu.VMEM((RUNS, 8, REST), jnp.bfloat16),
            pltpu.VMEM((ROWS, COLS), jnp.float32),
            pltpu.VMEM((COLS, 128), jnp.float32),
        ],
        compiler_params=limit(8),
        cost_estimate=pl.CostEstimate(
            flops=4 * ROWS * COLS * REST, bytes_accessed=16 * 1024 * 1024, transcendentals=2 * ROWS * COLS
        ),
        name="score_rest",
    )(
        sig,
        pos,
        *[in_vmem(v) for v in (*messages, *batches, shifted[1], acc)],
    )


def merge_kernel(stat_ref, other_ref, out_ref):
    out_ref[...] = jnp.zeros_like(out_ref)
    for q in range(2):
        a, b = stat_ref[q : q + 1, :], other_ref[1 - q : 2 - q, :]
        top = jnp.maximum(a, b)
        out_ref[q : q + 1, :] = top
        out_ref[2 + q : 3 + q, :] = stat_ref[2 + q : 3 + q, :] * jnp.exp(a - top) + other_ref[
            3 - q : 4 - q, :
        ] * jnp.exp(b - top)
    bound = jnp.max(jnp.maximum(stat_ref[4:5, :], other_ref[4:5, :]), axis=1, keepdims=True)
    out_ref[4:5, :] = jnp.broadcast_to(jnp.maximum(bound, 1e-30), (1, N))


def merge(stats, other):
    return pl.pallas_call(
        merge_kernel,
        in_specs=[VMEM, VMEM],
        out_specs=VMEM,
        out_shape=pltpu.VMEM((8, N), jnp.float32),
        compiler_params=limit(2),
        name="merge",
    )(in_vmem(stats), in_vmem(other))


def partial_kernel(z_first, sig_ref, pos_ref, *refs):
    if not z_first:
        w_ref, bound_ref, im_ref, *out_refs = refs
        bound = bound_ref[4:5, 0:1]
    else:
        st_ref, *every = refs[:5]
        re_ref, im_ref, *out_refs, w_ref, ev_ref = refs[5:]
        for q in range(2):
            tops = [r[q : q + 1, :] for r in every]
            top = jnp.maximum(jnp.maximum(tops[0], tops[1]), jnp.maximum(tops[2], tops[3]))
            total = sum(r[2 + q : 3 + q, :] * jnp.exp(t - top) for r, t in zip(every, tops))
            evidence = top + jnp.log(total)
            if q == 0:
                ev_ref[...] = evidence
            for t in range(SHIFTS):
                s = st_ref[q, :, t * N : (t + 1) * N]
                w_ref[q, :, t * N : (t + 1) * N] = jnp.exp(s - evidence).astype(jnp.bfloat16)
        bound = every[0][4:5, 0:1]
    scale = HEADROOM / bound
    entries = [
        [run_entry(sig_ref, pos_ref, q, dz, dx) for dz in range(Z) for dx in range(X)]
        for q in range(2)
    ]

    def one_tile(image_ref, start, out_start, width):
        at_in = pl.ds(pl.multiple_of(start, 128), width)
        at = pl.ds(pl.multiple_of(out_start, 128), width)
        for q in range(2):
            value = (
                jnp.dot(
                    w_ref[q],
                    image_ref[q, :, :, at_in].reshape(ROWS, width),
                    preferred_element_type=jnp.float32,
                )
                * scale
            )
            for o in range(RUNS):
                _, second, zz = entries[q][o]
                out_ref = out_refs[o // X if z_first else o % X]
                base = (o % X if z_first else zz) * 16
                rows = pl.ds(pl.multiple_of(base + second * 8, 8), 8)
                block = value[o * 8 : o * 8 + 8, :]
                if q == 0:
                    other = pl.ds(pl.multiple_of(base + (1 - second) * 8, 8), 8)
                    out_ref[rows, at] = block
                    out_ref[other, at] = jnp.zeros_like(block)
                else:
                    out_ref[rows, at] += block

    if z_first:
        pl.loop(0, PIX // PTILE)(lambda i: one_tile(re_ref, i * PTILE, i * PTILE, PTILE))
        one_tile(im_ref, 0, PIX, EDGE)
    else:
        half = OTHERS // 2
        pl.loop(0, 2)(lambda i: one_tile(im_ref, EDGE + i * half, i * half, half))


def partial_sums(z_first, sig, pos, weights, *images):
    many, rows = (Z, X * 16) if z_first else (X, Z * 16)
    out_shape = [pltpu.VMEM((rows, FIRST if z_first else OTHERS), jnp.float32)] * many
    if z_first:
        out_shape.append(pltpu.VMEM((2, COLS, ROWS), jnp.bfloat16))
        out_shape.append(jax.ShapeDtypeStruct((1, N), jnp.float32))
    return pl.pallas_call(
        lambda *refs: partial_kernel(z_first, *refs),
        in_specs=[SMEM, SMEM] + [VMEM] * (len(weights) + len(images)),
        out_specs=[VMEM] * len(out_shape),
        out_shape=out_shape,
        compiler_params=limit(4),
        cost_estimate=pl.CostEstimate(
            flops=2 * ROWS * COLS * FEATURES, bytes_accessed=16 * 1024 * 1024, transcendentals=0
        ),
        name="partial_first" if z_first else "partial_rest",
    )(sig, pos, *[in_vmem(v) for v in (*weights, *images)])


HIGH, LOW = 32, 128


def insert_kernel(bound_ref, w_ref, ins_ref, *refs):
    scale = bound_ref[4:5, 0:1] * (1.0 / HEADROOM)

    def add(acc, i, at, at_ids, width):
        row = pl.ds(i, 1)
        ids = ins_ref[row, at_ids]
        high = lax.shift_right_logical(ids, 7)
        low = lax.bitwise_and(ids, LOW - 1)
        value = w_ref[row, at] * scale
        head = value.astype(jnp.bfloat16).astype(jnp.float32)
        tail = value - head
        here = high == lax.broadcasted_iota(jnp.int32, (HIGH, width), 0)
        rows = jnp.concatenate(
            [jnp.where(here, head, 0.0), jnp.where(here, tail, 0.0)], axis=0
        ).astype(jnp.bfloat16)
        there = low == lax.broadcasted_iota(jnp.int32, (LOW, width), 0)
        table = jnp.where(there, 1.0, 0.0).astype(jnp.bfloat16)
        return acc + lax.dot_general(rows, table, DIMS, preferred_element_type=jnp.float32)

    empty = jnp.zeros((2 * HIGH, LOW), jnp.float32)
    if len(refs) == 3:
        re_ref, im_ref, out_ref = refs
        step = lambda i, acc: add(acc, i, slice(0, OTHERS), slice(EDGE, PIX), OTHERS)
        acc = lax.fori_loop(0, 16, step, empty, unroll=4)
        slab = im_ref[...] + acc[:HIGH] + acc[HIGH:]
        for h in range(HIGH):
            at = slice(h * LOW, (h + 1) * LOW)
            out_ref[0:1, at] = re_ref[h : h + 1, :]
            out_ref[1:2, at] = slab[h : h + 1, :]
    else:
        re_ref, im_ref = refs

        def step(i, both):
            re, im = both
            re = add(re, i, slice(0, PIX), slice(0, PIX), PIX)
            im = add(im, i, slice(PIX, FIRST), slice(0, EDGE), EDGE)
            return re, im

        re, im = lax.fori_loop(0, 16, step, (empty, empty), unroll=2)
        re_ref[...] = re[:HIGH] + re[HIGH:]
        im_ref[...] = im[:HIGH] + im[HIGH:]


def insert(bound, weighted, insertion, *slabs):
    slab = jax.ShapeDtypeStruct((HIGH, LOW), jnp.float32)
    return pl.pallas_call(
        insert_kernel,
        in_specs=[VMEM] * (3 + len(slabs)),
        out_specs=VMEM if slabs else [VMEM, VMEM],
        out_shape=jax.ShapeDtypeStruct((2, VOX), jnp.float32) if slabs else [slab, slab],
        compiler_params=limit(8),
        cost_estimate=pl.CostEstimate(
            flops=4 * HIGH * LOW * 16 * PIX, bytes_accessed=512 * 1024, transcendentals=0
        ),
        name="insert_rest" if slabs else "insert_first",
    )(bound, weighted.reshape(16, weighted.shape[-1]), insertion, *slabs)


def img_index(z, x, c):
    return (z * X + x) * CORES + c


def pairs(dz, dx, dc=0):
    return [
        (img_index(z, x, c), img_index((z + dz) % Z, (x + dx) % X, (c + dc) % CORES))
        for z in range(Z)
        for x in range(X)
        for c in range(CORES)
    ]


Z_GROUPS = [[img_index(z, x, c) for z in range(Z)] for x in range(X) for c in range(CORES)]


def send(value, dz=0, dx=0, dc=0):
    return lax.ppermute(value, "img", pairs(dz, dx, dc))


def all_to_all_z(value):
    return lax.all_to_all(
        value, "img", split_axis=0, concat_axis=0, tiled=True, axis_index_groups=Z_GROUPS
    )


def gather(projections, unit):
    mine = projections[:, :, :SPLIT]
    row = [mine, send(mine, dx=-1), send(mine, dx=-2), send(mine, dx=1)]
    ahead = behind = assemble(row, unit)
    messages = {0: ahead}
    for k in range(1, Z // 2):
        behind = send(behind, dz=1)
        messages[Z - k] = behind
        ahead = send(ahead, dz=-1)
        messages[k] = ahead
    left = send(behind[:, :, :FAR], dz=1)
    right = send(ahead[:, :, FAR:], dz=-1)
    late = [messages[3], right, messages[5]]
    batches = []
    for column in (pick([messages[k] for k in EARLY]), pick(late)):
        for dx in (-1, -2, 1):
            batches.append(send(column, dx=dx))
    messages[Z // 2] = left
    return [messages[k] for k in range(Z)] + [right], batches


def wide(value):
    return value.astype(jnp.float32)


def narrow(value):
    return value.astype(jnp.float16)


def scatter_z_first(parts):
    half = Z // 2
    behind = narrow(parts[half])
    for k in range(half, 0, -1):
        if k < half:
            behind = narrow(parts[k] + wide(behind))
        behind = send(behind, dz=1)
    ahead = narrow(parts[half + 1])
    for k in range(half - 1, 0, -1):
        if k < half - 1:
            ahead = narrow(parts[Z - k] + wide(ahead))
        ahead = send(ahead, dz=-1)
    row = parts[0] + wide(behind) + wide(ahead)
    arrived = [send(narrow(row[k]), dx=k) for k in range(1, X)]
    return row[0] + wide(arrived[0]) + wide(arrived[1]) + wide(arrived[2])


def scatter_x_first(parts):
    arrived = [send(narrow(parts[k]), dx=k) for k in range(1, X)]
    column = narrow(parts[0] + wide(arrived[0]) + wide(arrived[1]) + wide(arrived[2]))
    return jnp.sum(wide(all_to_all_z(column)), axis=0)


def exchange_refs(value):
    out = [value]
    for k in range(1, REFS):
        out.append(lax.ppermute(value, "ref", [(r, (r + k) % REFS) for r in range(REFS)]))
    return out


def one_device(particles, projections, significance, insertion):
    img = lax.axis_index("img")
    ref = lax.axis_index("ref")
    z, x, core = img >> 3, (img >> 1) & 3, img & 1
    pos = jnp.stack([z, x, core, ref]).astype(jnp.int32)
    sig = lax.dynamic_slice_in_dim(significance, img - core, 2, axis=0)
    table = jnp.asarray(shift_tables())

    mate = send(particles, dc=1)
    unit = prepare(particles, projections)
    unit, pos, sig = lax.optimization_barrier((unit, pos, sig))
    messages, batches = gather(projections, unit)
    shifted = shifted_images(table, particles, mate)

    acc = score_first(sig, pos, messages, shifted)
    scores, stats = score_rest(sig, pos, messages, batches, shifted, acc)
    merged = merge(stats, send(stats, dc=1))
    every = exchange_refs(merged)
    *sums, weights, evidence = partial_sums(True, sig, pos, (scores, *every), *shifted)
    sums_rest = partial_sums(False, sig, pos, (weights, merged), shifted[1])
    total = scatter_z_first([v.reshape(X, 2, 8, FIRST) for v in sums])
    total_rest = scatter_x_first([v.reshape(Z, 2, 8, OTHERS) for v in sums_rest])
    ids = insertion.reshape(16, PIX)
    slabs = insert(merged, total, ids)
    volume = insert(merged, total_rest, ids, *slabs)
    return volume, evidence.reshape(N)


def solution(mesh):
    in_specs = (P("img", None), P(("img", "ref"), None, None), P(), P(("img", "ref"), None, None))
    out_specs = (P(None, ("img", "ref")), P("img"))
    return jax.shard_map(
        one_device, mesh=mesh, in_specs=in_specs, out_specs=out_specs, check_vma=False
    )
```
